32 devices in a mesh: rep: 2 (over y), grp: 16 (over z, x, core).
Axes of the slice: x: 2, y: 2, z: 4, core: 2. Of those that a mesh axis runs over, the one named last changes fastest.
Arguments:
- layer_inputs: bfloat16 [4096, 3584], P('grp'), may hold values from -32 to 32
- loss_adjoint_matrix: bfloat16 [4096, 3584], P('grp'), may hold values from -0.375 to 0.375
- attention_projection_matrix: bfloat16 [3584, 768], P(('rep', 'grp')), may hold values from -0.09375 to 0.09375
- merge_projection_transposed: bfloat16 [3584, 512], P(('rep', 'grp')), may hold values from -0.25 to 0.25
- packed_sequence_labels: int32 [16, 256], P('grp'), may hold values from 0 to 3, never falling along the last dimension, each value on 1 to 128 neighbouring positions
- dropout_factors: bfloat16 [2, 4096, 4, 256], P('rep', 'grp'), may hold values from -0.75 to 0.75
- straggler_filter: int32 [2, 16], P(None, 'grp'), may hold values from 0 to 1, as said below
Outputs:
- gradient: float32 [3584, 1280], P(('rep', 'grp'))
The draws below stay inside these ranges and needn't reach their ends.
Inputs may be any that keep to these rules, and one draw needn't show every extreme that they name: `straggler_filter`: each column (partition) holds exactly one 1, the surviving replica; all other entries are 0.
All inputs are finite; a program needn't handle non-finite values.
Results may differ from the reference program's by a relative error of at most 0.008.
The reference program's roundings to bfloat16 on the way (of `dropped`, `attended`, `attn_grad`, `val_grad` and `score_grad`) count: a program that leaves them out, or rounds other values in their place, can miss the bound.
Values may be sent and summed in bfloat16 or wider, within the bound.
No kernel may reach another device: no remote copies, remote signals or barrier semaphores. Data moves between devices by JAX's collectives and lax.ppermute only.
A program may use at most 64 MiB of HBM per device.

```python
import math
import jax
import jax.numpy as jnp
import numpy as np
from jax import lax

D = 3584
HD = 128
HQ = 4
SEQ = 256
TOKENS = 4096
N_REP = 2
N_GRP = 16


def draw_layer_inputs(key, part):
    normal_part = jax.random.truncated_normal(key, -6.0, 6.0, (TOKENS, D), jnp.float32)
    return normal_part.astype(jnp.bfloat16)


def draw_straggler_filter(key, part):
    chosen = jax.random.randint(jax.random.fold_in(key, 5), (N_GRP,), 0, N_REP)
    return (jnp.arange(N_REP)[:, None] == chosen[None, :]).astype(jnp.int32)


def block_scale(stream_key, dims, split, smallest, largest):
    def one(dim, blocks):
        draws = jax.random.uniform(jax.random.fold_in(jax.random.fold_in(stream_key, 6), dim), (blocks,), jnp.float32, smallest / len(split), largest / len(split))
        return jnp.repeat(jnp.exp(draws), dims[dim] // blocks).reshape((-1,) + (1,) * (len(dims) - dim - 1))

    factor_of = one(*split[0])
    for cut in split[1:]:
        factor_of = factor_of * one(*cut)
    return factor_of


def length_profile(number_of, total, reach, skew):
    portions = [(1 << 20) // math.isqrt(rank ** skew) + 1 for rank in range(2, number_of + 1)]
    rest, given = total - reach - (number_of - 1), [1] * (number_of - 1)
    while rest > 0:
        free = [i for i in range(number_of - 1) if given[i] < reach]
        whole, left = sum([portions[i] for i in free]), rest
        for i in free:
            more = min(reach - given[i], max(1, left * portions[i] // whole), rest)
            given[i] = given[i] + more
            rest = rest - more
    return np.array([reach] + given)


def uneven(own_key, number_of, total, limit, skew):
    if number_of == 2:
        one = jax.random.randint(own_key, (), max(1, total - limit), min(limit, total - 1) + 1)
        return jnp.stack([one, total - one])
    tallies = jnp.asarray(length_profile(number_of, total, limit, skew), jnp.int32)
    twos = (number_of - 1) // 2
    donor, sink = tallies[1:1 + 2 * twos:2], tallies[2:2 + 2 * twos:2]
    slack = jnp.minimum(donor - 1, limit - sink)
    moved = jax.random.randint(jax.random.fold_in(own_key, 1), (twos,), 0, 1 << 20) % (slack + 1)
    tallies = tallies.at[1:1 + 2 * twos:2].set(donor - moved).at[2:2 + 2 * twos:2].set(sink + moved)
    return tallies[jax.random.permutation(jax.random.fold_in(own_key, 2), number_of)]


def centred(rng, extent, width, reach, shards=(), kind=jnp.bfloat16):
    drawn = width * jax.random.normal(rng, extent, jnp.float32)
    if shards:
        drawn = drawn * block_scale(rng, extent, shards, -0.22, 0.18)
    return jnp.clip(drawn, -reach, reach).astype(kind)


def setup_inputs(seed: int = 0) -> dict:
    streams_of = jax.random.split(jax.random.key(seed), 8)
    layer_inputs = draw_layer_inputs(jax.random.fold_in(streams_of[7], 71), 0)
    loss_adjoint_matrix = centred(streams_of[1], (TOKENS, D), (4.0 / TOKENS ** 0.5), 0.375, ((0, 16),))
    attention_projection_matrix = centred(streams_of[2], (D, (HQ + 2) * HD), D ** -0.5, 0.09375, ((0, 32),))
    merge_projection_transposed = centred(streams_of[3], (D, HQ * HD), (HQ * HD) ** -0.5, 0.25, ((0, 32),))
    packed_sequence_labels = jax.vmap(lambda own: jnp.searchsorted(jnp.cumsum(uneven(own, 4, SEQ, SEQ // 2, 1)), jnp.arange(SEQ), side="right"))(jax.random.split(streams_of[4], N_GRP)).reshape((N_GRP, SEQ)).astype(jnp.int32)
    dropout_factors = centred(streams_of[5], (N_REP, TOKENS, HQ, SEQ), 0.3, 0.75, ((0, 2), (1, 16)))
    straggler_filter = draw_straggler_filter(jax.random.fold_in(streams_of[7], 71), 0)
    return dict(layer_inputs=layer_inputs, loss_adjoint_matrix=loss_adjoint_matrix, attention_projection_matrix=attention_projection_matrix, merge_projection_transposed=merge_projection_transposed, packed_sequence_labels=packed_sequence_labels, dropout_factors=dropout_factors, straggler_filter=straggler_filter)


def head_grads(hidden_rows, cot_rows, attention_projection_matrix, merge_projection_transposed, doc_row, noise_rows):
    score_scale = 1.0 / jnp.sqrt(jnp.float32(HD))
    projected = jnp.dot(hidden_rows, attention_projection_matrix, preferred_element_type=jnp.float32).astype(jnp.bfloat16)
    queries = projected[:, :HQ * HD]
    key_rows = projected[:, HQ * HD:(HQ + 1) * HD]
    val_rows = projected[:, (HQ + 1) * HD:]
    query_heads = queries.reshape(SEQ, HQ, HD).astype(jnp.float32)
    keys_wide = key_rows.astype(jnp.float32)
    vals_wide = val_rows.astype(jnp.float32)
    position = jnp.arange(SEQ, dtype=jnp.int32)
    allowed = (doc_row[:, None] == doc_row[None, :]) & (position[None, :] <= position[:, None])
    scores = jnp.einsum('ihd,jd->hij', query_heads, keys_wide) * score_scale
    scores = jnp.where(allowed[None], scores, -jnp.inf)
    highest = lax.optimization_barrier(jnp.max(scores, axis=2, keepdims=True))
    expon = jnp.exp(scores - highest)
    attn_probs = expon / lax.optimization_barrier(jnp.sum(expon, axis=2, keepdims=True))
    factor = 1.0 + jnp.transpose(noise_rows.astype(jnp.float32), (1, 0, 2))
    dropped = (attn_probs * factor).astype(jnp.bfloat16)
    dropped_wide = dropped.astype(jnp.float32)
    attended = jnp.einsum('hij,jd->ihd', dropped_wide, vals_wide).astype(jnp.bfloat16).reshape(SEQ, HQ * HD)
    attn_grad = jnp.dot(cot_rows, merge_projection_transposed, preferred_element_type=jnp.float32).astype(jnp.bfloat16)
    grad_heads = attn_grad.reshape(SEQ, HQ, HD).astype(jnp.float32)
    val_grad = jnp.einsum('hij,ihd->jd', dropped_wide, grad_heads).astype(jnp.bfloat16)
    prob_grad = jnp.einsum('ihd,jd->hij', grad_heads, vals_wide) * factor
    inner = lax.optimization_barrier(jnp.sum(attn_probs * prob_grad, axis=2, keepdims=True))
    score_grad = (attn_probs * (prob_grad - inner) * score_scale).astype(jnp.bfloat16)
    score_wide = score_grad.astype(jnp.float32)
    query_grad = jnp.einsum('hij,jd->ihd', score_wide, keys_wide).astype(jnp.bfloat16).reshape(SEQ, HQ * HD)
    key_grad = jnp.einsum('hij,ihd->jd', score_wide, query_heads).astype(jnp.bfloat16)
    stacked = jnp.concatenate([query_grad, key_grad, val_grad], axis=1)
    proj_grad = jnp.dot(hidden_rows.T, stacked, preferred_element_type=jnp.float32)
    out_grad = jnp.dot(cot_rows.T, attended, preferred_element_type=jnp.float32)
    return jnp.concatenate([proj_grad, out_grad], axis=1)

def reference(layer_inputs, loss_adjoint_matrix, attention_projection_matrix, merge_projection_transposed, packed_sequence_labels, dropout_factors, straggler_filter):
    hidden_pieces = layer_inputs.reshape(N_GRP, SEQ, D)
    cotangent_pieces = loss_adjoint_matrix.reshape(N_GRP, SEQ, D)
    noise_pieces = jnp.transpose(dropout_factors.reshape(N_REP, N_GRP, SEQ, HQ, SEQ), (1, 0, 2, 3, 4))
    kept_worker_position = lax.optimization_barrier(jnp.sum(jnp.arange(N_REP, dtype=jnp.int32)[:, None] * straggler_filter, axis=0)).astype(jnp.int32)

    def loop_body(running_total, items):
        hidden_rows, cot_rows, doc_row, noise_group, chosen = items
        noise_rows = lax.dynamic_index_in_dim(noise_group, chosen, 0, keepdims=False)
        return (running_total + head_grads(hidden_rows, cot_rows, attention_projection_matrix, merge_projection_transposed, doc_row, noise_rows), None)
    initial_sum = jnp.zeros((D, (2 * HQ + 2) * HD), jnp.float32)
    running_total, unused_value = lax.scan(loop_body, initial_sum, (hidden_pieces, cotangent_pieces, packed_sequence_labels, noise_pieces, kept_worker_position))
    return running_total
```

```python
import functools
import math

import jax
import jax.numpy as jnp
from jax import lax
from jax.experimental import pallas as pl
from jax.experimental.pallas import tpu as pltpu
from jax.sharding import PartitionSpec as P


def from_root(block, axis, holder):
    block = jnp.where(lax.axis_index(axis) == holder, block, jnp.zeros_like(block))
    return lax.psum(block, axis)


def token_grads(projected_wide, attn_wide, doc_row, noise_rows):
    seq_len = projected_wide.shape[0]
    head_size = (projected_wide.shape[1] - attn_wide.shape[1]) // 2
    heads = attn_wide.shape[1] // head_size
    score_scale = 1.0 / jnp.sqrt(jnp.float32(head_size))
    projected = projected_wide.astype(jnp.bfloat16)
    queries = projected[:, : heads * head_size]
    key_rows = projected[:, heads * head_size : (heads + 1) * head_size]
    val_rows = projected[:, (heads + 1) * head_size :]
    query_heads = queries.reshape(seq_len, heads, head_size).astype(jnp.float32)
    keys_wide = key_rows.astype(jnp.float32)
    vals_wide = val_rows.astype(jnp.float32)
    position = jnp.arange(seq_len, dtype=jnp.int32)
    allowed = (doc_row[:, None] == doc_row[None, :]) & (position[None, :] <= position[:, None])
    scores = jnp.einsum("ihd,jd->hij", query_heads, keys_wide) * score_scale
    scores = jnp.where(allowed[None], scores, -jnp.inf)
    highest = jnp.max(scores, axis=2, keepdims=True)
    expon = jnp.exp(scores - highest)
    attn_probs = expon / jnp.sum(expon, axis=2, keepdims=True)
    factor = 1.0 + jnp.transpose(noise_rows.astype(jnp.float32), (1, 0, 2))
    dropped = (attn_probs * factor).astype(jnp.bfloat16)
    dropped_wide = dropped.astype(jnp.float32)
    attended = (
        jnp.einsum("hij,jd->ihd", dropped_wide, vals_wide)
        .astype(jnp.bfloat16)
        .reshape(seq_len, heads * head_size)
    )
    attn_grad = attn_wide.astype(jnp.bfloat16)
    grad_heads = attn_grad.reshape(seq_len, heads, head_size).astype(jnp.float32)
    val_grad = jnp.einsum("hij,ihd->jd", dropped_wide, grad_heads).astype(jnp.bfloat16)
    prob_grad = jnp.einsum("ihd,jd->hij", grad_heads, vals_wide) * factor
    inner = jnp.sum(attn_probs * prob_grad, axis=2, keepdims=True)
    score_grad = (attn_probs * (prob_grad - inner) * score_scale).astype(jnp.bfloat16)
    score_wide = score_grad.astype(jnp.float32)
    query_grad = (
        jnp.einsum("hij,jd->ihd", score_wide, keys_wide)
        .astype(jnp.bfloat16)
        .reshape(seq_len, heads * head_size)
    )
    key_grad = jnp.einsum("hij,ihd->jd", score_wide, query_heads).astype(jnp.bfloat16)
    stacked = jnp.concatenate([query_grad, key_grad, val_grad], axis=1)
    return (stacked, attended)


def weight_rows(hidden_rows, cot_rows, stacked, attended, first_row, row_count):
    hidden_cols = lax.dynamic_slice_in_dim(hidden_rows, first_row, row_count, 1)
    cot_cols = lax.dynamic_slice_in_dim(cot_rows, first_row, row_count, 1)
    proj_grad = jnp.dot(hidden_cols.T, stacked, preferred_element_type=jnp.float32)
    out_grad = jnp.dot(cot_cols.T, attended, preferred_element_type=jnp.float32)
    return jnp.concatenate([proj_grad, out_grad], axis=1)


def generic_device(
    layer_inputs,
    loss_adjoint_matrix,
    attention_projection_matrix,
    merge_projection_transposed,
    packed_sequence_labels,
    dropout_factors,
    straggler_filter,
):
    duplicate_workers = lax.axis_size("rep")
    member = lax.axis_index("rep")
    kept_worker = jnp.sum(jnp.arange(duplicate_workers, dtype=jnp.int32) * straggler_filter[:, 0])
    row_count = layer_inputs.shape[1] // duplicate_workers
    first_row = member * row_count
    qkv_full, out_full = (
        lax.all_gather(attention_projection_matrix, ("rep", "grp"), axis=0, tiled=True),
        lax.all_gather(merge_projection_transposed, ("rep", "grp"), axis=0, tiled=True),
    )
    projected_wide = jnp.dot(layer_inputs, qkv_full, preferred_element_type=jnp.float32)
    attn_wide = jnp.dot(loss_adjoint_matrix, out_full, preferred_element_type=jnp.float32)
    chosen_noise = from_root(dropout_factors[0], "rep", kept_worker)
    stacked, attended = token_grads(
        projected_wide, attn_wide, packed_sequence_labels[0], chosen_noise
    )
    gradient = weight_rows(
        layer_inputs, loss_adjoint_matrix, stacked, attended, first_row, row_count
    )
    return lax.psum_scatter(gradient, "grp", scatter_dimension=0, tiled=True)


def dot(a, b, dims):
    return lax.dot_general(a, b, (dims, ((), ())), preferred_element_type=jnp.float32)


def transpose_kernel(order_ref, x_ref, y_ref, keep_ref, send_ref, flipped):
    half = keep_ref.shape[1]
    blocks = order_ref.shape[0]
    rows = 2 * half // blocks
    for which, source in enumerate((x_ref, y_ref)):
        width = source.shape[1]
        step = 256 if width % 256 == 0 else width
        for first in range(0, width, step):
            flipped[pl.ds(first, step), :] = source[:, pl.ds(first, step)].T
        for block in range(blocks):
            first = pl.multiple_of(order_ref[block] * rows, 16)
            target = keep_ref if block < blocks // 2 else send_ref
            place = (block % (blocks // 2)) * rows
            target[which, pl.ds(place, rows), :] = flipped[pl.ds(first, rows), :]


def transpose_inputs(order, x, y):
    tokens, width = x.shape
    out = jax.ShapeDtypeStruct((2, width // 2, tokens), x.dtype)
    vmem = pl.BlockSpec(memory_space=pltpu.VMEM)
    return pl.pallas_call(
        transpose_kernel,
        out_shape=(out, out),
        in_specs=[pl.BlockSpec(memory_space=pltpu.SMEM), vmem, vmem],
        out_specs=(vmem, vmem),
        scratch_shapes=[pltpu.VMEM((width, tokens), x.dtype)],
        cost_estimate=pl.CostEstimate(flops=0, bytes_accessed=8 * x.size, transcendentals=0),
        name="flip",
    )(order, x, y)


def back_kernel(keep_ref, other_ref, out_ref):
    tokens = keep_ref.shape[2]
    half = keep_ref.shape[1]
    step = 256 if half % 256 == 0 else half
    for which in range(2):
        for place, source in enumerate((keep_ref, other_ref)):
            for first in range(0, half, step):
                out_ref[which, pl.ds(place * tokens, tokens), pl.ds(first, step)] = source[
                    which, pl.ds(first, step), :
                ].T


def back(keep, other):
    _, half, tokens = keep.shape
    vmem = pl.BlockSpec(memory_space=pltpu.VMEM)
    return pl.pallas_call(
        back_kernel,
        out_shape=jax.ShapeDtypeStruct((2, 2 * tokens, half), keep.dtype),
        in_specs=[vmem, vmem],
        out_specs=vmem,
        cost_estimate=pl.CostEstimate(flops=0, bytes_accessed=8 * keep.size, transcendentals=0),
        name="flip_back",
    )(keep, other)


def project_kernel(split, pieces, *refs):
    rows_ref, piece_refs = refs[0], refs[1 : 1 + pieces]
    own_ref, other_ref, weights, sems = refs[1 + pieces :]
    depth = piece_refs[0].shape[0]
    copies = [
        pltpu.make_async_copy(piece, weights.at[pl.ds(n * depth, depth), :], sems.at[n])
        for n, piece in enumerate(piece_refs)
    ]
    for copy in copies:
        copy.start()
    for copy in copies:
        copy.wait()
    tokens = own_ref.shape[0]
    for place, target in enumerate((own_ref, other_ref)):
        rows = pl.ds(place * tokens, tokens)
        target[:, :split] = dot(rows_ref[0, rows, :], weights[:, :split], ((1,), (0,)))
        target[:, split:] = dot(rows_ref[1, rows, :], weights[:, split:], ((1,), (0,)))


def project(rows, pieces, split):
    _, both, half = rows.shape
    columns = pieces[0].shape[1]
    out = jax.ShapeDtypeStruct((both // 2, columns), jnp.float32)
    vmem = pl.BlockSpec(memory_space=pltpu.VMEM)
    return pl.pallas_call(
        functools.partial(project_kernel, split, len(pieces)),
        out_shape=(out, out),
        in_specs=[vmem] + [pl.BlockSpec(memory_space=pl.ANY)] * len(pieces),
        out_specs=(vmem, vmem),
        scratch_shapes=[
            pltpu.VMEM((half, columns), pieces[0].dtype),
            pltpu.SemaphoreType.DMA((len(pieces),)),
        ],
        cost_estimate=pl.CostEstimate(
            flops=2 * both * half * columns,
            bytes_accessed=2 * rows.size + 2 * half * columns,
            transcendentals=0,
        ),
        name="project",
    )(rows, *pieces)


def attend_kernel(
    heads, member_ref, own_ref, other_ref, pair_ref, row_ref, column_ref, noise_ref,
    att_ref, query_ref, keep_ref, send_ref,
):
    tokens = own_ref.shape[0]
    size = pair_ref.shape[1]
    scale = 1.0 / math.sqrt(size)
    low = jnp.bfloat16

    def part(first):
        return (own_ref[:, pl.ds(first, size)] + other_ref[:, pl.ds(first, size)]).astype(low)

    first_member = member_ref[0] == 0
    mine = part(heads * size).astype(jnp.float32)
    pair = pair_ref[...].astype(jnp.float32)
    keys = jnp.where(first_member, mine, pair).astype(low)
    vals = jnp.where(first_member, pair, mine).astype(low)
    query_at = lax.broadcasted_iota(jnp.int32, (tokens, tokens), 0)
    key_at = lax.broadcasted_iota(jnp.int32, (tokens, tokens), 1)
    allowed = (column_ref[...] == row_ref[...]) & (key_at <= query_at)
    key_grad = jnp.zeros((tokens, size), jnp.float32)
    val_grad = jnp.zeros((tokens, size), jnp.float32)
    for head in range(heads):
        here = pl.ds(head * size, size)
        query = part(head * size)
        grad = part((heads + 1 + head) * size)
        scores = dot(query, keys, ((1,), (1,))) * scale
        scores = jnp.where(allowed, scores, -jnp.inf)
        expon = jnp.exp(scores - jnp.max(scores, axis=1, keepdims=True))
        probs = expon / jnp.sum(expon, axis=1, keepdims=True)
        factor = 1.0 + noise_ref[head].astype(jnp.float32)
        dropped = (probs * factor).astype(low)
        att_ref[:, here] = dot(dropped, vals, ((1,), (0,))).astype(low)
        val_grad += dot(dropped, grad, ((0,), (0,)))
        prob_grad = dot(grad, vals, ((1,), (1,))) * factor
        inner = jnp.sum(probs * prob_grad, axis=1, keepdims=True)
        score_grad = (probs * (prob_grad - inner) * scale).astype(low)
        query_ref[:, here] = dot(score_grad, keys, ((1,), (0,))).astype(low)
        key_grad += dot(score_grad, query, ((0,), (0,)))
    keep_ref[...] = jnp.where(first_member, key_grad, val_grad)
    send_ref[...] = jnp.where(first_member, val_grad, key_grad)


def attend(member, own, other, pair, labels, noise):
    tokens, size = pair.shape
    heads = noise.shape[0]
    vmem = pl.BlockSpec(memory_space=pltpu.VMEM)
    wide = jax.ShapeDtypeStruct((tokens, heads * size), jnp.bfloat16)
    narrow = jax.ShapeDtypeStruct((tokens, size), jnp.float32)
    return pl.pallas_call(
        functools.partial(attend_kernel, heads),
        out_shape=(wide, wide, narrow, narrow),
        in_specs=[pl.BlockSpec(memory_space=pltpu.SMEM)] + [vmem] * 6,
        out_specs=(vmem,) * 4,
        cost_estimate=pl.CostEstimate(
            flops=12 * heads * tokens * tokens * size,
            bytes_accessed=8 * own.size + 2 * noise.size,
            transcendentals=noise.size,
        ),
        name="attend",
    )(member, own, other, pair, labels, labels.reshape(tokens, 1), noise)


def grads_kernel(keep_ref, other_ref, own_ref, theirs_ref, mine_ref, away_ref):
    half = mine_ref.shape[0]
    for place, target in ((1, away_ref), (0, mine_ref)):
        rows = pl.ds(place * half, half)
        total = dot(keep_ref[0, rows, :], own_ref[...], ((1,), (0,)))
        total += dot(other_ref[0, rows, :], theirs_ref[...], ((1,), (0,)))
        target[...] = total.astype(target.dtype)


def grads(keep, other, which, own, theirs):
    _, half, tokens = keep.shape
    columns = own.shape[1]
    vmem = pl.BlockSpec(memory_space=pltpu.VMEM)
    side = pl.BlockSpec((1, half, tokens), lambda n: (which, 0, 0))
    flat = pl.BlockSpec((tokens, columns), lambda n: (0, 0))
    out = pl.BlockSpec((half // 2, columns), lambda n: (0, 0))
    return pl.pallas_call(
        grads_kernel,
        grid=(1,),
        out_shape=(
            jax.ShapeDtypeStruct((half // 2, columns), jnp.float32),
            jax.ShapeDtypeStruct((half // 2, columns), jnp.bfloat16),
        ),
        in_specs=[side, side, flat, flat],
        out_specs=(out, out),
        cost_estimate=pl.CostEstimate(
            flops=4 * half * tokens * columns,
            bytes_accessed=4 * half * tokens + 3 * half * columns,
            transcendentals=0,
        ),
        name="grads",
    )(keep, other, own, theirs)


def paired_device(
    layer_inputs,
    loss_adjoint_matrix,
    attention_projection_matrix,
    merge_projection_transposed,
    packed_sequence_labels,
    dropout_factors,
    straggler_filter,
):
    grp = lax.axis_size("grp")
    lines = grp // 4
    member, place = lax.axis_index("rep"), lax.axis_index("grp")
    line, side, core = place // 4, (place // 2) % 2, place % 2
    first = member == 0

    def coords(g):
        return g // 4, (g // 2) % 2, g % 2

    def index(line, side, core):
        return (line % lines) * 4 + side * 2 + core

    def moved(change):
        return [(g, index(*change(*coords(g)))) for g in range(grp)]

    def across_core(a):
        return lax.ppermute(a, "grp", moved(lambda z, x, c: (z, x, 1 - c)))

    def across_side(a):
        return lax.ppermute(a, "grp", moved(lambda z, x, c: (z, 1 - x, c)))

    def along_line(a, steps):
        return lax.ppermute(a, "grp", moved(lambda z, x, c: (z + steps, x, c)))

    def across_rep(a):
        return lax.ppermute(a, "rep", [(0, 1), (1, 0)])

    heads, tokens = dropout_factors.shape[2], dropout_factors.shape[3]
    share = heads // 2
    width = merge_projection_transposed.shape[1]
    size = width // heads
    split = (share + 1) * size

    def half_columns(member):
        queries = attention_projection_matrix[:, member * share * size : (member + 1) * share * size]
        pair = attention_projection_matrix[:, width + member * size : width + (member + 1) * size]
        merge = merge_projection_transposed[:, member * share * size : (member + 1) * share * size]
        return jnp.concatenate([queries, pair, merge], axis=1)

    halves = (half_columns(0), half_columns(1))
    mine = jnp.where(first, halves[0], halves[1])
    theirs = jnp.where(first, halves[1], halves[0])
    block = jnp.concatenate([mine, across_rep(theirs)], axis=0)

    gathered = {(0, 0): block, (1, 0): across_side(block)}
    for steps in range(1, lines):
        gathered[0, lines - steps] = along_line(block, steps)
    for steps in range(1, lines):
        gathered[1, lines - steps] = across_side(gathered[0, lines - steps])
    pieces = [gathered[s, n] for s in range(2) for n in range(lines)]

    order = jnp.stack(
        [
            (member ^ m) * grp + ((line + n) % lines) * 4 + (side ^ s) * 2 + (core ^ c)
            for c in range(2)
            for s in range(2)
            for n in range(lines)
            for m in range(2)
        ]
    ).astype(jnp.int32)
    keep, send = transpose_inputs(order, layer_inputs, loss_adjoint_matrix)
    other = across_core(send)
    rows = back(keep, other)

    noise = jnp.transpose(dropout_factors[0], (1, 0, 2))
    noise_mine = jnp.where(first, noise[:share], noise[share:])
    noise_theirs = jnp.where(first, noise[share:], noise[:share])
    kept_worker = jnp.sum(jnp.arange(2, dtype=jnp.int32) * straggler_filter[:, 0])
    noise_used = jnp.where(kept_worker == member, noise_mine, across_rep(noise_theirs))

    own_part, away_part = project(rows, pieces, split)
    in_part = across_core(away_part)
    pair = (own_part[:, share * size : split] + in_part[:, share * size : split]).astype(jnp.bfloat16)
    pair = across_rep(pair)
    att, query_grad, pair_keep, pair_send = attend(
        member.reshape(1), own_part, in_part, pair, packed_sequence_labels, noise_used
    )
    pair_grad = (pair_keep + across_rep(pair_send)).astype(jnp.bfloat16)

    def reduced(which, grad):
        stays, leaves = grads(keep, other, which, grad, across_core(grad))
        total = stays + across_side(leaves).astype(jnp.float32)
        total = total.reshape(lines, total.shape[0] // lines, total.shape[1])
        low = total.astype(jnp.bfloat16)
        final = total[0]
        for steps in range(1, lines):
            final = final + along_line(low[steps], steps).astype(jnp.float32)
        cut = final.shape[0] // 2
        ours, partner = final[:cut], across_rep(final[cut:])
        return jnp.where(first, ours, partner), jnp.where(first, partner, ours)

    merge_low, merge_high = reduced(1, att)
    query_low, query_high = reduced(0, query_grad)
    pair_low, pair_high = reduced(0, pair_grad)
    return jnp.concatenate(
        [query_low, query_high, pair_low, pair_high, merge_low, merge_high], axis=1
    )


def per_device(*args):
    rep, grp = lax.axis_size("rep"), lax.axis_size("grp")
    depth, heads = args[0].shape[1], args[5].shape[2]
    size = args[3].shape[1] // heads
    even = depth % (rep * grp * 16) == 0 and depth % 256 == 0 and heads % 2 == 0 and size % 128 == 0
    if rep == 2 and grp % 4 == 0 and grp > 4 and even and args[0].shape[0] % 128 == 0:
        return paired_device(*args)
    return generic_device(*args)


def solution(mesh):
    placed = (
        P("grp", None),
        P("grp", None),
        P(("rep", "grp"), None),
        P(("rep", "grp"), None),
        P("grp", None),
        P("rep", "grp", None, None),
        P(None, "grp"),
    )
    return jax.shard_map(
        per_device, mesh=mesh, in_specs=placed, out_specs=P(("rep", "grp"), None), check_vma=False
    )
```

```python
import functools
import math

import jax
import jax.numpy as jnp
from jax import lax
from jax.experimental import pallas as pl
from jax.experimental.pallas import tpu as pltpu
from jax.sharding import PartitionSpec as P


def from_root(block, axis, holder):
    block = jnp.where(lax.axis_index(axis) == holder, block, jnp.zeros_like(block))
    return lax.psum(block, axis)


def token_grads(projected_wide, attn_wide, doc_row, noise_rows):
    seq_len = projected_wide.shape[0]
    head_size = (projected_wide.shape[1] - attn_wide.shape[1]) // 2
    heads = attn_wide.shape[1] // head_size
    score_scale = 1.0 / jnp.sqrt(jnp.float32(head_size))
    projected = projected_wide.astype(jnp.bfloat16)
    queries = projected[:, : heads * head_size]
    key_rows = projected[:, heads * head_size : (heads + 1) * head_size]
    val_rows = projected[:, (heads + 1) * head_size :]
    query_heads = queries.reshape(seq_len, heads, head_size).astype(jnp.float32)
    keys_wide = key_rows.astype(jnp.float32)
    vals_wide = val_rows.astype(jnp.float32)
    position = jnp.arange(seq_len, dtype=jnp.int32)
    allowed = (doc_row[:, None] == doc_row[None, :]) & (position[None, :] <= position[:, None])
    scores = jnp.einsum("ihd,jd->hij", query_heads, keys_wide) * score_scale
    scores = jnp.where(allowed[None], scores, -jnp.inf)
    highest = jnp.max(scores, axis=2, keepdims=True)
    expon = jnp.exp(scores - highest)
    attn_probs = expon / jnp.sum(expon, axis=2, keepdims=True)
    factor = 1.0 + jnp.transpose(noise_rows.astype(jnp.float32), (1, 0, 2))
    dropped = (attn_probs * factor).astype(jnp.bfloat16)
    dropped_wide = dropped.astype(jnp.float32)
    attended = (
        jnp.einsum("hij,jd->ihd", dropped_wide, vals_wide)
        .astype(jnp.bfloat16)
        .reshape(seq_len, heads * head_size)
    )
    attn_grad = attn_wide.astype(jnp.bfloat16)
    grad_heads = attn_grad.reshape(seq_len, heads, head_size).astype(jnp.float32)
    val_grad = jnp.einsum("hij,ihd->jd", dropped_wide, grad_heads).astype(jnp.bfloat16)
    prob_grad = jnp.einsum("ihd,jd->hij", grad_heads, vals_wide) * factor
    inner = jnp.sum(attn_probs * prob_grad, axis=2, keepdims=True)
    score_grad = (attn_probs * (prob_grad - inner) * score_scale).astype(jnp.bfloat16)
    score_wide = score_grad.astype(jnp.float32)
    query_grad = (
        jnp.einsum("hij,jd->ihd", score_wide, keys_wide)
        .astype(jnp.bfloat16)
        .reshape(seq_len, heads * head_size)
    )
    key_grad = jnp.einsum("hij,ihd->jd", score_wide, query_heads).astype(jnp.bfloat16)
    stacked = jnp.concatenate([query_grad, key_grad, val_grad], axis=1)
    return (stacked, attended)


def weight_rows(hidden_rows, cot_rows, stacked, attended, first_row, row_count):
    hidden_cols = lax.dynamic_slice_in_dim(hidden_rows, first_row, row_count, 1)
    cot_cols = lax.dynamic_slice_in_dim(cot_rows, first_row, row_count, 1)
    proj_grad = jnp.dot(hidden_cols.T, stacked, preferred_element_type=jnp.float32)
    out_grad = jnp.dot(cot_cols.T, attended, preferred_element_type=jnp.float32)
    return jnp.concatenate([proj_grad, out_grad], axis=1)


def generic_device(
    layer_inputs,
    loss_adjoint_matrix,
    attention_projection_matrix,
    merge_projection_transposed,
    packed_sequence_labels,
    dropout_factors,
    straggler_filter,
):
    duplicate_workers = lax.axis_size("rep")
    member = lax.axis_index("rep")
    kept_worker = jnp.sum(jnp.arange(duplicate_workers, dtype=jnp.int32) * straggler_filter[:, 0])
    row_count = layer_inputs.shape[1] // duplicate_workers
    first_row = member * row_count
    qkv_full, out_full = (
        lax.all_gather(attention_projection_matrix, ("rep", "grp"), axis=0, tiled=True),
        lax.all_gather(merge_projection_transposed, ("rep", "grp"), axis=0, tiled=True),
    )
    projected_wide = jnp.dot(layer_inputs, qkv_full, preferred_element_type=jnp.float32)
    attn_wide = jnp.dot(loss_adjoint_matrix, out_full, preferred_element_type=jnp.float32)
    chosen_noise = from_root(dropout_factors[0], "rep", kept_worker)
    stacked, attended = token_grads(
        projected_wide, attn_wide, packed_sequence_labels[0], chosen_noise
    )
    gradient = weight_rows(
        layer_inputs, loss_adjoint_matrix, stacked, attended, first_row, row_count
    )
    return lax.psum_scatter(gradient, "grp", scatter_dimension=0, tiled=True)


def dot(a, b, dims):
    return lax.dot_general(a, b, (dims, ((), ())), preferred_element_type=jnp.float32)


VMEM = pl.BlockSpec(memory_space=pltpu.VMEM)
SMEM = pl.BlockSpec(memory_space=pltpu.SMEM)


def cost(flops, count):
    return pl.CostEstimate(flops=flops, bytes_accessed=count, transcendentals=0)


def flip_kernel(order_ref, x_ref, y_ref, keep_ref, send_ref, flipped):
    half = keep_ref.shape[1]
    blocks = order_ref.shape[1]
    rows = 2 * half // blocks
    for which, source in enumerate((x_ref, y_ref)):
        width = source.shape[1]
        step = 256 if width % 256 == 0 else width
        for first in range(0, width, step):
            flipped[pl.ds(first, step), :] = source[:, pl.ds(first, step)].T
        for block in range(blocks):
            first = pl.multiple_of(order_ref[which, block] * rows, 16)
            target = keep_ref if block < blocks // 2 else send_ref
            place = (block % (blocks // 2)) * rows
            target[which, pl.ds(place, rows), :] = flipped[pl.ds(first, rows), :]


def flip(order, x, y):
    tokens, width = x.shape
    out = jax.ShapeDtypeStruct((2, width // 2, tokens), x.dtype)
    return pl.pallas_call(
        flip_kernel,
        out_shape=(out, out),
        in_specs=[SMEM, VMEM, VMEM],
        out_specs=(VMEM, VMEM),
        scratch_shapes=[pltpu.VMEM((width, tokens), x.dtype)],
        cost_estimate=cost(0, 8 * x.size),
        name="flip",
    )(order, x, y)


def back_kernel(keep_ref, other_ref, out_ref):
    _, parts, _, depth = out_ref.shape
    tokens = keep_ref.shape[2]
    for which in range(2):
        for place, source in enumerate((keep_ref, other_ref)):
            for part in range(parts):
                block = source[which, pl.ds(part * depth, depth), :]
                out_ref[which, part, pl.ds(place * tokens, tokens), :] = block.T


def back(keep, other, parts):
    _, half, tokens = keep.shape
    return pl.pallas_call(
        back_kernel,
        out_shape=jax.ShapeDtypeStruct((2, parts, 2 * tokens, half // parts), keep.dtype),
        in_specs=[VMEM, VMEM],
        out_specs=VMEM,
        cost_estimate=cost(0, 8 * keep.size),
        name="back",
    )(keep, other)


def project_kernel(split, places, more, *refs):
    pieces = len(places)
    rows_ref, piece_refs = refs[0], refs[1 : 1 + pieces]
    added = refs[1 + pieces : 3 + pieces] if more else (None, None)
    targets = refs[-2:]
    tokens = targets[0].shape[0]
    for place, (target, start) in enumerate(zip(targets, added)):
        rows = pl.ds(place * tokens, tokens)
        for which, columns in ((0, slice(None, split)), (1, slice(split, None))):
            total = None if start is None else start[:, columns]
            for piece, at in zip(piece_refs, places):
                term = dot(rows_ref[which, at[which], rows, :], piece[:, columns], ((1,), (0,)))
                total = term if total is None else total + term
            target[:, columns] = total


def project(rows, pieces, places, split, added=()):
    both = rows.shape[2]
    depth, columns = pieces[0].shape
    out = jax.ShapeDtypeStruct((both // 2, columns), jnp.float32)
    return pl.pallas_call(
        functools.partial(project_kernel, split, places, bool(added)),
        out_shape=(out, out),
        in_specs=[VMEM] * (1 + len(pieces) + len(added)),
        out_specs=(VMEM, VMEM),
        cost_estimate=cost(
            2 * both * depth * columns * len(pieces), 2 * rows.size + 2 * depth * columns * len(pieces)
        ),
        name="project",
    )(rows, *pieces, *added)


def forward_kernel(
    heads, member_ref, own_ref, other_ref, pair_ref, row_ref, column_ref, noise_ref,
    att_ref, probs_ref, parts_ref,
):
    tokens = own_ref.shape[0]
    size = pair_ref.shape[1]
    scale = 1.0 / math.sqrt(size)
    low = jnp.bfloat16

    def part(first):
        return (own_ref[:, pl.ds(first, size)] + other_ref[:, pl.ds(first, size)]).astype(low)

    first_member = member_ref[0] == 0
    mine = part(heads * size).astype(jnp.float32)
    pair = pair_ref[...].astype(jnp.float32)
    keys = jnp.where(first_member, mine, pair).astype(low)
    vals = jnp.where(first_member, pair, mine).astype(low)
    parts_ref[2 * heads] = keys
    parts_ref[2 * heads + 1] = vals
    query_at = lax.broadcasted_iota(jnp.int32, (tokens, tokens), 0)
    key_at = lax.broadcasted_iota(jnp.int32, (tokens, tokens), 1)
    allowed = (column_ref[...] == row_ref[...]) & (key_at <= query_at)
    for head in range(heads):
        query = part(head * size)
        parts_ref[head] = query
        parts_ref[heads + head] = part((heads + 1 + head) * size)
        scores = dot(query, keys, ((1,), (1,))) * scale
        scores = jnp.where(allowed, scores, -jnp.inf)
        expon = jnp.exp(scores - jnp.max(scores, axis=1, keepdims=True))
        probs = expon / jnp.sum(expon, axis=1, keepdims=True)
        probs_ref[head] = probs
        dropped = (probs * (1.0 + noise_ref[head].astype(jnp.float32))).astype(low)
        att_ref[:, pl.ds(head * size, size)] = dot(dropped, vals, ((1,), (0,))).astype(low)


def forward(member, own, other, pair, labels, noise):
    tokens, size = pair.shape
    heads = noise.shape[0]
    return pl.pallas_call(
        functools.partial(forward_kernel, heads),
        out_shape=(
            jax.ShapeDtypeStruct((tokens, heads * size), jnp.bfloat16),
            jax.ShapeDtypeStruct(noise.shape, jnp.float32),
            jax.ShapeDtypeStruct((2 * heads + 2, tokens, size), jnp.bfloat16),
        ),
        in_specs=[SMEM] + [VMEM] * 6,
        out_specs=(VMEM,) * 3,
        cost_estimate=cost(4 * noise.size * size, 8 * own.size + 6 * noise.size),
        name="forward",
    )(member, own, other, pair, labels, labels.reshape(tokens, 1), noise)


def backward_kernel(heads, member_ref, probs_ref, parts_ref, noise_ref, query_ref, keep_ref, send_ref):
    tokens, size = keep_ref.shape
    scale = 1.0 / math.sqrt(size)
    low = jnp.bfloat16
    first_member = member_ref[0] == 0
    keys, vals = parts_ref[2 * heads], parts_ref[2 * heads + 1]
    key_grad = jnp.zeros((tokens, size), jnp.float32)
    val_grad = jnp.zeros((tokens, size), jnp.float32)
    for head in range(heads):
        query, grad = parts_ref[head], parts_ref[heads + head]
        probs = probs_ref[head]
        factor = 1.0 + noise_ref[head].astype(jnp.float32)
        dropped = (probs * factor).astype(low)
        val_grad += dot(dropped, grad, ((0,), (0,)))
        prob_grad = dot(grad, vals, ((1,), (1,))) * factor
        inner = jnp.sum(probs * prob_grad, axis=1, keepdims=True)
        score_grad = (probs * (prob_grad - inner) * scale).astype(low)
        query_ref[:, pl.ds(head * size, size)] = dot(score_grad, keys, ((1,), (0,))).astype(low)
        key_grad += dot(score_grad, query, ((0,), (0,)))
    keep_ref[...] = jnp.where(first_member, key_grad, val_grad)
    send_ref[...] = jnp.where(first_member, val_grad, key_grad)


def backward(member, probs, parts, noise):
    heads, tokens, _ = noise.shape
    size = parts.shape[2]
    narrow = jax.ShapeDtypeStruct((tokens, size), jnp.float32)
    return pl.pallas_call(
        functools.partial(backward_kernel, heads),
        out_shape=(jax.ShapeDtypeStruct((tokens, heads * size), jnp.bfloat16), narrow, narrow),
        in_specs=[SMEM] + [VMEM] * 3,
        out_specs=(VMEM,) * 3,
        cost_estimate=cost(8 * noise.size * size, 6 * noise.size),
        name="backward",
    )(member, probs, parts, noise)


def grads_kernel(keep_ref, other_ref, own_ref, theirs_ref, out_ref):
    total = dot(keep_ref[0], own_ref[...], ((1,), (0,)))
    total += dot(other_ref[0], theirs_ref[...], ((1,), (0,)))
    out_ref[...] = total.astype(out_ref.dtype)


def grads(keep, other, which, side, own, theirs, dtype):
    _, half, tokens = keep.shape
    columns = own.shape[1]
    steps = 4
    rows = half // 2 // steps
    block = pl.BlockSpec((1, rows, tokens), lambda n: (which, side * steps + n, 0))
    flat = pl.BlockSpec((tokens, columns), lambda n: (0, 0))
    return pl.pallas_call(
        grads_kernel,
        grid=(steps,),
        out_shape=jax.ShapeDtypeStruct((half // 2, columns), dtype),
        in_specs=[block, block, flat, flat],
        out_specs=pl.BlockSpec((rows, columns), lambda n: (n, 0)),
        cost_estimate=cost(2 * half * tokens * columns, 2 * half * tokens + 2 * half * columns),
        name="grads",
    )(keep, other, own, theirs)


def place_kernel(member_ref, *refs):
    sources, out_ref = refs[:-1], refs[-1]

    def put(order):
        first = 0
        for pair in range(0, len(sources), 2):
            for n in order:
                source = sources[pair + n]
                out_ref[:, pl.ds(first, source.shape[1])] = source[...]
                first += source.shape[1]

    @pl.when(member_ref[0] == 0)
    def _():
        put((0, 1))

    @pl.when(member_ref[0] != 0)
    def _():
        put((1, 0))


def place_columns(member, *pieces):
    shape = (pieces[0].shape[0], sum(p.shape[1] for p in pieces))
    return pl.pallas_call(
        place_kernel,
        out_shape=jax.ShapeDtypeStruct(shape, pieces[0].dtype),
        in_specs=[SMEM] + [VMEM] * len(pieces),
        out_specs=VMEM,
        cost_estimate=cost(0, 8 * shape[0] * shape[1]),
        name="place",
    )(member, *pieces)


def paired_device(
    layer_inputs,
    loss_adjoint_matrix,
    attention_projection_matrix,
    merge_projection_transposed,
    packed_sequence_labels,
    dropout_factors,
    straggler_filter,
):
    grp = lax.axis_size("grp")
    lines = grp // 4
    bits = lines.bit_length() - 1
    member = lax.axis_index("rep")
    me = member * grp + lax.axis_index("grp")
    first = member == 0
    core_bit, side_bit, line_bits = 1, 2, [4 << n for n in range(bits)]

    def across(a, bit):
        return lax.ppermute(a, "grp", [(g, g ^ bit) for g in range(grp)])

    def across_rep(a):
        return lax.ppermute(a, "rep", [(0, 1), (1, 0)])

    heads, tokens = dropout_factors.shape[2], dropout_factors.shape[3]
    share = heads // 2
    width = merge_projection_transposed.shape[1]
    size = width // heads
    split = (share + 1) * size

    def half_columns(member):
        queries = attention_projection_matrix[:, member * share * size : (member + 1) * share * size]
        pair = attention_projection_matrix[:, width + member * size : width + (member + 1) * size]
        merge = merge_projection_transposed[:, member * share * size : (member + 1) * share * size]
        return jnp.concatenate([queries, pair, merge], axis=1)

    halves = (half_columns(0), half_columns(1))
    mine = jnp.where(first, halves[0], halves[1])
    theirs = jnp.where(first, halves[1], halves[0])
    block = jnp.concatenate([mine, across_rep(theirs)], axis=0)

    gathered = {0: block, side_bit: across(block, side_bit)}
    line = [0]
    for bit in reversed(line_bits):
        for at in line:
            gathered[at | bit] = across(gathered[at], bit)
        line += [at | bit for at in line]
    for at in line[1:]:
        gathered[at | side_bit] = across(gathered[at], side_bit)

    stages = ([side_bit] + line_bits, [line_bits[0], side_bit] + line_bits[1:])

    def keys(which):
        found = [0]
        for bit in stages[which]:
            found = [at | b for at in found for b in (0, bit)]
        return found

    order = jnp.array(
        [
            [c | at | m for c in (0, core_bit) for at in keys(which) for m in (0, grp)]
            for which in range(2)
        ],
        jnp.int32,
    )
    order, block = lax.optimization_barrier((order ^ me, block))
    keep, send = flip(order, layer_inputs, loss_adjoint_matrix)
    other = across(send, core_bit)

    noise = jnp.transpose(dropout_factors[0], (1, 0, 2))
    noise_mine = jnp.where(first, noise[:share], noise[share:])
    noise_theirs = jnp.where(first, noise[share:], noise[:share])
    kept_worker = jnp.sum(jnp.arange(2, dtype=jnp.int32) * straggler_filter[:, 0])
    noise_used = jnp.where(kept_worker == member, noise_mine, across_rep(noise_theirs))

    rows = back(keep, other, 2 * lines)
    rows, noise_used = lax.optimization_barrier((rows, noise_used))
    arrival = [0, side_bit, line_bits[0], line_bits[0] | side_bit]
    arrival += [at for at in gathered if at not in arrival]
    places = [(keys(0).index(at), keys(1).index(at)) for at in arrival]
    early = 5
    parts = project(rows, [gathered[at] for at in arrival[:early]], places[:early], split)
    own_part, away_part = project(
        rows, [gathered[at] for at in arrival[early:]], places[early:], split, parts
    )
    in_part = across(away_part, core_bit)
    pair = (own_part[:, share * size : split] + in_part[:, share * size : split]).astype(jnp.bfloat16)
    pair = across_rep(pair)
    member = member.reshape(1)
    att, probs, pieces = forward(
        member, own_part, in_part, pair, packed_sequence_labels, noise_used
    )
    query_grad, pair_keep, pair_send = backward(member, probs, pieces, noise_used)
    pair_grad = (pair_keep + across_rep(pair_send)).astype(jnp.bfloat16)

    def first_half(which, grad, theirs):
        leaves = grads(keep, other, which, 1, grad, theirs, jnp.bfloat16)
        return leaves, across(leaves, stages[which][0])

    def rest(which, total, arrived):
        for n, bit in enumerate(stages[which]):
            if n:
                cut = total.shape[0] // 2
                leaves, total = total[cut:].astype(jnp.bfloat16), total[:cut]
                arrived = across(leaves, bit)
            total = total + arrived.astype(jnp.float32)
        cut = total.shape[0] // 2
        return total[:cut], across_rep(total[cut:])

    def stays(which, grad, theirs):
        return grads(keep, other, which, 0, grad, theirs, jnp.float32)

    att_theirs, query_theirs = across(att, core_bit), across(query_grad, core_bit)
    att_theirs, query_theirs = lax.optimization_barrier((att_theirs, query_theirs))
    merge_leaves, merge_in = first_half(1, att, att_theirs)
    query_theirs, merge_leaves = lax.optimization_barrier((query_theirs, merge_leaves))
    query_leaves, query_in = first_half(0, query_grad, query_theirs)
    pair_theirs, query_leaves = lax.optimization_barrier((across(pair_grad, core_bit), query_leaves))
    pair_leaves, pair_in = first_half(0, pair_grad, pair_theirs)
    att, query_grad, pair_leaves = lax.optimization_barrier((att, query_grad, pair_leaves))
    merge = rest(1, stays(1, att, att_theirs), merge_in)
    query = rest(0, stays(0, query_grad, query_theirs), query_in)
    pair = rest(0, stays(0, pair_grad, pair_theirs), pair_in)
    return place_columns(member, *query, *pair, *merge)


def per_device(*args):
    rep, grp = lax.axis_size("rep"), lax.axis_size("grp")
    depth, heads = args[0].shape[1], args[5].shape[2]
    size = args[3].shape[1] // heads
    even = depth % (rep * grp * 16) == 0 and depth % 256 == 0 and heads % 2 == 0 and size % 128 == 0
    if rep == 2 and grp in (8, 16, 32) and even and args[0].shape[0] % 128 == 0:
        return paired_device(*args)
    return generic_device(*args)


def solution(mesh):
    placed = (
        P("grp", None),
        P("grp", None),
        P(("rep", "grp"), None),
        P(("rep", "grp"), None),
        P("grp", None),
        P("rep", "grp", None, None),
        P(None, "grp"),
    )
    return jax.shard_map(
        per_device, mesh=mesh, in_specs=placed, out_specs=P(("rep", "grp"), None), check_vma=False
    )
```

```python
import functools
import math

import jax
import jax.numpy as jnp
from jax import lax
from jax.experimental import pallas as pl
from jax.experimental.pallas import tpu as pltpu
from jax.sharding import PartitionSpec as P


def from_root(block, axis, holder):
    block = jnp.where(lax.axis_index(axis) == holder, block, jnp.zeros_like(block))
    return lax.psum(block, axis)


def token_grads(projected_wide, attn_wide, doc_row, noise_rows):
    seq_len = projected_wide.shape[0]
    head_size = (projected_wide.shape[1] - attn_wide.shape[1]) // 2
    heads = attn_wide.shape[1] // head_size
    score_scale = 1.0 / jnp.sqrt(jnp.float32(head_size))
    projected = projected_wide.astype(jnp.bfloat16)
    queries = projected[:, : heads * head_size]
    key_rows = projected[:, heads * head_size : (heads + 1) * head_size]
    val_rows = projected[:, (heads + 1) * head_size :]
    query_heads = queries.reshape(seq_len, heads, head_size).astype(jnp.float32)
    keys_wide = key_rows.astype(jnp.float32)
    vals_wide = val_rows.astype(jnp.float32)
    position = jnp.arange(seq_len, dtype=jnp.int32)
    allowed = (doc_row[:, None] == doc_row[None, :]) & (position[None, :] <= position[:, None])
    scores = jnp.einsum("ihd,jd->hij", query_heads, keys_wide) * score_scale
    scores = jnp.where(allowed[None], scores, -jnp.inf)
    highest = jnp.max(scores, axis=2, keepdims=True)
    expon = jnp.exp(scores - highest)
    attn_probs = expon / jnp.sum(expon, axis=2, keepdims=True)
    factor = 1.0 + jnp.transpose(noise_rows.astype(jnp.float32), (1, 0, 2))
    dropped = (attn_probs * factor).astype(jnp.bfloat16)
    dropped_wide = dropped.astype(jnp.float32)
    attended = (
        jnp.einsum("hij,jd->ihd", dropped_wide, vals_wide)
        .astype(jnp.bfloat16)
        .reshape(seq_len, heads * head_size)
    )
    attn_grad = attn_wide.astype(jnp.bfloat16)
    grad_heads = attn_grad.reshape(seq_len, heads, head_size).astype(jnp.float32)
    val_grad = jnp.einsum("hij,ihd->jd", dropped_wide, grad_heads).astype(jnp.bfloat16)
    prob_grad = jnp.einsum("ihd,jd->hij", grad_heads, vals_wide) * factor
    inner = jnp.sum(attn_probs * prob_grad, axis=2, keepdims=True)
    score_grad = (attn_probs * (prob_grad - inner) * score_scale).astype(jnp.bfloat16)
    score_wide = score_grad.astype(jnp.float32)
    query_grad = (
        jnp.einsum("hij,jd->ihd", score_wide, keys_wide)
        .astype(jnp.bfloat16)
        .reshape(seq_len, heads * head_size)
    )
    key_grad = jnp.einsum("hij,ihd->jd", score_wide, query_heads).astype(jnp.bfloat16)
    stacked = jnp.concatenate([query_grad, key_grad, val_grad], axis=1)
    return (stacked, attended)


def weight_rows(hidden_rows, cot_rows, stacked, attended, first_row, row_count):
    hidden_cols = lax.dynamic_slice_in_dim(hidden_rows, first_row, row_count, 1)
    cot_cols = lax.dynamic_slice_in_dim(cot_rows, first_row, row_count, 1)
    proj_grad = jnp.dot(hidden_cols.T, stacked, preferred_element_type=jnp.float32)
    out_grad = jnp.dot(cot_cols.T, attended, preferred_element_type=jnp.float32)
    return jnp.concatenate([proj_grad, out_grad], axis=1)


def generic_device(
    layer_inputs,
    loss_adjoint_matrix,
    attention_projection_matrix,
    merge_projection_transposed,
    packed_sequence_labels,
    dropout_factors,
    straggler_filter,
):
    duplicate_workers = lax.axis_size("rep")
    member = lax.axis_index("rep")
    kept_worker = jnp.sum(jnp.arange(duplicate_workers, dtype=jnp.int32) * straggler_filter[:, 0])
    row_count = layer_inputs.shape[1] // duplicate_workers
    first_row = member * row_count
    qkv_full, out_full = (
        lax.all_gather(attention_projection_matrix, ("rep", "grp"), axis=0, tiled=True),
        lax.all_gather(merge_projection_transposed, ("rep", "grp"), axis=0, tiled=True),
    )
    projected_wide = jnp.dot(layer_inputs, qkv_full, preferred_element_type=jnp.float32)
    attn_wide = jnp.dot(loss_adjoint_matrix, out_full, preferred_element_type=jnp.float32)
    chosen_noise = from_root(dropout_factors[0], "rep", kept_worker)
    stacked, attended = token_grads(
        projected_wide, attn_wide, packed_sequence_labels[0], chosen_noise
    )
    gradient = weight_rows(
        layer_inputs, loss_adjoint_matrix, stacked, attended, first_row, row_count
    )
    return lax.psum_scatter(gradient, "grp", scatter_dimension=0, tiled=True)


def dot(a, b, dims):
    return lax.dot_general(a, b, (dims, ((), ())), preferred_element_type=jnp.float32)


VMEM = pl.BlockSpec(memory_space=pltpu.VMEM)
SMEM = pl.BlockSpec(memory_space=pltpu.SMEM)


def cost(flops, count):
    return pl.CostEstimate(flops=flops, bytes_accessed=count, transcendentals=0)


def flip_kernel(order_ref, x_ref, keep_ref, send_ref, flipped):
    half = keep_ref.shape[0]
    blocks = order_ref.shape[0]
    rows = 2 * half // blocks
    width = x_ref.shape[1]
    for first in range(0, width, 256):
        flipped[pl.ds(first, 256), :] = x_ref[:, pl.ds(first, 256)].T
    for block in range(blocks):
        first = pl.multiple_of(order_ref[block] * rows, 16)
        target = keep_ref if block < blocks // 2 else send_ref
        place = (block % (blocks // 2)) * rows
        target[pl.ds(place, rows), :] = flipped[pl.ds(first, rows), :]


def flip(order, x):
    tokens, width = x.shape
    out = jax.ShapeDtypeStruct((width // 2, tokens), x.dtype)
    return pl.pallas_call(
        flip_kernel,
        out_shape=(out, out),
        in_specs=[SMEM, VMEM],
        out_specs=(VMEM, VMEM),
        scratch_shapes=[pltpu.VMEM((width, tokens), x.dtype)],
        cost_estimate=cost(0, 4 * x.size),
        name="flip",
    )(order, x)


def stack_kernel(*refs):
    sources, out_ref, sems = refs[:-2], refs[-2], refs[-1]
    copies = []
    first = 0
    for n, source in enumerate(sources):
        rows = source.shape[0]
        copies.append(pltpu.make_async_copy(source, out_ref.at[pl.ds(first, rows), :], sems.at[n]))
        first += rows
    for copy in copies:
        copy.start()
    for copy in copies:
        copy.wait()


def stack(*pieces):
    shape = (sum(p.shape[0] for p in pieces), pieces[0].shape[1])
    return pl.pallas_call(
        stack_kernel,
        out_shape=jax.ShapeDtypeStruct(shape, pieces[0].dtype),
        in_specs=[pl.BlockSpec(memory_space=pl.ANY)] * len(pieces),
        out_specs=VMEM,
        scratch_shapes=[pltpu.SemaphoreType.DMA((len(pieces),))],
        cost_estimate=cost(0, 4 * shape[0] * shape[1]),
        name="stack",
    )(*pieces)


def forward_kernel(
    heads, member_ref, own_ref, other_ref, pair_ref, row_ref, column_ref, noise_ref,
    att_ref, probs_ref, parts_ref,
):
    tokens = own_ref.shape[0]
    size = pair_ref.shape[1]
    scale = 1.0 / math.sqrt(size)
    low = jnp.bfloat16

    def part(first):
        return (own_ref[:, pl.ds(first, size)] + other_ref[:, pl.ds(first, size)]).astype(low)

    first_member = member_ref[0] == 0
    mine = part(heads * size).astype(jnp.float32)
    pair = pair_ref[...].astype(jnp.float32)
    keys = jnp.where(first_member, mine, pair).astype(low)
    vals = jnp.where(first_member, pair, mine).astype(low)
    parts_ref[heads] = keys
    parts_ref[heads + 1] = vals
    query_at = lax.broadcasted_iota(jnp.int32, (tokens, tokens), 0)
    key_at = lax.broadcasted_iota(jnp.int32, (tokens, tokens), 1)
    allowed = (column_ref[...] == row_ref[...]) & (key_at <= query_at)
    for head in range(heads):
        query = part(head * size)
        parts_ref[head] = query
        scores = dot(query, keys, ((1,), (1,))) * scale
        scores = jnp.where(allowed, scores, -jnp.inf)
        expon = jnp.exp(scores - jnp.max(scores, axis=1, keepdims=True))
        probs = expon / jnp.sum(expon, axis=1, keepdims=True)
        probs_ref[head] = probs
        dropped = (probs * (1.0 + noise_ref[head].astype(jnp.float32))).astype(low)
        att_ref[:, pl.ds(head * size, size)] = dot(dropped, vals, ((1,), (0,))).astype(low)


def forward(member, own, other, pair, labels, noise):
    tokens, size = pair.shape
    heads = noise.shape[0]
    return pl.pallas_call(
        functools.partial(forward_kernel, heads),
        out_shape=(
            jax.ShapeDtypeStruct((tokens, heads * size), jnp.bfloat16),
            jax.ShapeDtypeStruct(noise.shape, jnp.float32),
            jax.ShapeDtypeStruct((heads + 2, tokens, size), jnp.bfloat16),
        ),
        in_specs=[SMEM] + [VMEM] * 6,
        out_specs=(VMEM,) * 3,
        cost_estimate=cost(4 * noise.size * size, 8 * own.size + 6 * noise.size),
        name="forward",
    )(member, own, other, pair, labels, labels.reshape(tokens, 1), noise)


def backward_kernel(
    heads, member_ref, own_ref, other_ref, probs_ref, parts_ref, noise_ref, query_ref, keep_ref, send_ref
):
    tokens, size = keep_ref.shape
    scale = 1.0 / math.sqrt(size)
    low = jnp.bfloat16
    first_member = member_ref[0] == 0
    keys, vals = parts_ref[heads], parts_ref[heads + 1]
    key_grad = jnp.zeros((tokens, size), jnp.float32)
    val_grad = jnp.zeros((tokens, size), jnp.float32)
    for head in range(heads):
        here = pl.ds(head * size, size)
        query, grad = parts_ref[head], (own_ref[:, here] + other_ref[:, here]).astype(low)
        probs = probs_ref[head]
        factor = 1.0 + noise_ref[head].astype(jnp.float32)
        dropped = (probs * factor).astype(low)
        val_grad += dot(dropped, grad, ((0,), (0,)))
        prob_grad = dot(grad, vals, ((1,), (1,))) * factor
        inner = jnp.sum(probs * prob_grad, axis=1, keepdims=True)
        score_grad = (probs * (prob_grad - inner) * scale).astype(low)
        query_ref[:, here] = dot(score_grad, keys, ((1,), (0,))).astype(low)
        key_grad += dot(score_grad, query, ((0,), (0,)))
    keep_ref[...] = jnp.where(first_member, key_grad, val_grad)
    send_ref[...] = jnp.where(first_member, val_grad, key_grad)


def backward(member, own, other, probs, parts, noise):
    heads, tokens, _ = noise.shape
    size = parts.shape[2]
    narrow = jax.ShapeDtypeStruct((tokens, size), jnp.float32)
    return pl.pallas_call(
        functools.partial(backward_kernel, heads),
        out_shape=(jax.ShapeDtypeStruct((tokens, heads * size), jnp.bfloat16), narrow, narrow),
        in_specs=[SMEM] + [VMEM] * 5,
        out_specs=(VMEM,) * 3,
        cost_estimate=cost(8 * noise.size * size, 6 * noise.size),
        name="backward",
    )(member, own, other, probs, parts, noise)


def place_kernel(member_ref, *refs):
    sources, out_ref = refs[:-1], refs[-1]

    def put(order):
        first = 0
        for pair in range(0, len(sources), 2):
            for n in order:
                source = sources[pair + n]
                out_ref[:, pl.ds(first, source.shape[1])] = source[...].astype(out_ref.dtype)
                first += source.shape[1]

    @pl.when(member_ref[0] == 0)
    def _():
        put((0, 1))

    @pl.when(member_ref[0] != 0)
    def _():
        put((1, 0))


def place_columns(member, *pieces):
    shape = (pieces[0].shape[0], sum(p.shape[1] for p in pieces))
    return pl.pallas_call(
        place_kernel,
        out_shape=jax.ShapeDtypeStruct(shape, pieces[0].dtype),
        in_specs=[SMEM] + [VMEM] * len(pieces),
        out_specs=VMEM,
        cost_estimate=cost(0, 8 * shape[0] * shape[1]),
        name="place",
    )(member, *pieces)


def paired_device(
    layer_inputs,
    loss_adjoint_matrix,
    attention_projection_matrix,
    merge_projection_transposed,
    packed_sequence_labels,
    dropout_factors,
    straggler_filter,
):
    grp = lax.axis_size("grp")
    member = lax.axis_index("rep")
    me = member * grp + lax.axis_index("grp")
    first = member == 0
    core, side, near, far = 1, 2, 4, 8

    def across(a, bit):
        return lax.ppermute(a, "grp", [(g, g ^ bit) for g in range(grp)])

    def across_rep(a):
        return lax.ppermute(a, "rep", [(0, 1), (1, 0)])

    heads = dropout_factors.shape[2]
    share = heads // 2
    width = merge_projection_transposed.shape[1]
    size = width // heads
    part = share * size

    def exchanged(low, high):
        mine, theirs = jnp.where(first, low, high), jnp.where(first, high, low)
        return jnp.concatenate([mine, across_rep(theirs)], axis=0)

    def qkv_columns(m):
        return jnp.concatenate(
            [
                attention_projection_matrix[:, m * part : (m + 1) * part],
                attention_projection_matrix[:, width + m * size : width + (m + 1) * size],
            ],
            axis=1,
        )

    qkv = exchanged(qkv_columns(0), qkv_columns(1))
    merge = exchanged(merge_projection_transposed[:, :part], merge_projection_transposed[:, part:])

    qkv_near, qkv_far = across(qkv, near), across(qkv, far)
    qkv_both = across(qkv_far, near)
    qkv_side = [
        across(qkv, side), across(qkv_far, side), across(qkv_near, side), across(qkv_both, side)
    ]
    merge_far = across(merge, far)
    merge_line = stack(merge, merge_far)
    merge_pieces = [merge_line, across(merge_line, side), across(merge_line, near)]
    merge_pieces.append(across(merge_pieces[2], side))

    def order(bits):
        found = [0]
        for bit in (core, *bits, grp):
            found = [at | b for at in found for b in (0, bit)]
        return jnp.array(found, jnp.int32) ^ me

    stages = ((side, near, far), (near, side, far))
    x_keep, x_send = flip(order(stages[0]), layer_inputs)
    y_keep, y_send = flip(order(stages[1]), loss_adjoint_matrix)
    x_other, y_other = across(x_send, core), across(y_send, core)

    noise = jnp.transpose(dropout_factors[0], (1, 0, 2))
    noise_mine = jnp.where(first, noise[:share], noise[share:])
    noise_theirs = jnp.where(first, noise[share:], noise[:share])
    kept_worker = jnp.sum(jnp.arange(2, dtype=jnp.int32) * straggler_filter[:, 0])
    noise_used = jnp.where(kept_worker == member, noise_mine, across_rep(noise_theirs))

    def project(rows, parts):
        total, first = None, 0
        for weights in parts:
            depth = weights.shape[0]
            term = dot(rows[first : first + depth], weights, ((0,), (0,)))
            total = term if total is None else total + term
            first += depth
        return total

    qkv_line = stack(qkv, qkv_far, qkv_near, qkv_both)
    qkv_parts = (qkv_line, stack(*qkv_side[:3]), qkv_side[3])
    qkv_in = across(project(x_other, qkv_parts), core)
    qkv_own = project(x_keep, qkv_parts)
    merge_in = across(project(y_other, merge_pieces), core)
    merge_own = project(y_keep, merge_pieces)

    pair = (qkv_own[:, part:] + qkv_in[:, part:]).astype(jnp.bfloat16)
    pair = across_rep(pair)
    member = member.reshape(1)
    att, probs, pieces = forward(member, qkv_own, qkv_in, pair, packed_sequence_labels, noise_used)
    query_grad, pair_keep, pair_send = backward(
        member, merge_own, merge_in, probs, pieces, noise_used
    )
    pair_grad = (pair_keep + across_rep(pair_send)).astype(jnp.bfloat16)

    def reduced(keep, other, bits, grad, theirs):
        cut = keep.shape[0] // 2

        def half(rows):
            return dot(keep[rows], grad, ((1,), (0,))), other[rows]

        leaves, rows = half(slice(cut, None))
        leaves = (leaves + dot(rows, theirs, ((1,), (0,)))).astype(jnp.bfloat16)
        total, rows = half(slice(None, cut))
        for n, bit in enumerate(bits):
            arrived = across(leaves, bit)
            if n == 0:
                total = total + dot(rows, theirs, ((1,), (0,)))
            total = total + arrived.astype(jnp.float32)
            cut = total.shape[0] // 2
            leaves, total = total[cut:].astype(jnp.bfloat16), total[:cut]
            if n == len(bits) - 1:
                last = leaves
        return total, across_rep(last)

    merge = reduced(y_keep, y_other, stages[1], att, across(att, core))
    query = reduced(x_keep, x_other, stages[0], query_grad, across(query_grad, core))
    pair = reduced(x_keep, x_other, stages[0], pair_grad, across(pair_grad, core))
    return place_columns(member, *query, *pair, *merge)


def paired(mesh, shapes):
    rep, grp = mesh.shape["rep"], mesh.shape["grp"]
    depth, heads, tokens = shapes[0][1], shapes[5][2], shapes[5][3]
    size = shapes[3][1] // heads
    even = depth % (rep * grp * 16) == 0 and depth % 256 == 0
    return rep == 2 and grp == 16 and even and heads % 2 == 0 and size % 128 == 0 and tokens % 128 == 0


def solution(mesh):
    placed = (
        P("grp", None),
        P("grp", None),
        P(("rep", "grp"), None),
        P(("rep", "grp"), None),
        P("grp", None),
        P("rep", "grp", None, None),
        P(None, "grp"),
    )

    def on_devices(body):
        return jax.shard_map(
            body, mesh=mesh, in_specs=placed, out_specs=P(("rep", "grp"), None), check_vma=False
        )

    def step(*args):
        if not paired(mesh, [a.shape for a in args]):
            return on_devices(generic_device)(*args)
        return on_devices(paired_device)(*args)

    return step
```

```python
import functools
import math

import jax
import jax.numpy as jnp
from jax import lax
from jax.experimental import pallas as pl
from jax.experimental.pallas import tpu as pltpu
from jax.sharding import PartitionSpec as P


def from_root(block, axis, holder):
    block = jnp.where(lax.axis_index(axis) == holder, block, jnp.zeros_like(block))
    return lax.psum(block, axis)


def token_grads(projected_wide, attn_wide, doc_row, noise_rows):
    seq_len = projected_wide.shape[0]
    head_size = (projected_wide.shape[1] - attn_wide.shape[1]) // 2
    heads = attn_wide.shape[1] // head_size
    score_scale = 1.0 / jnp.sqrt(jnp.float32(head_size))
    projected = projected_wide.astype(jnp.bfloat16)
    queries = projected[:, : heads * head_size]
    key_rows = projected[:, heads * head_size : (heads + 1) * head_size]
    val_rows = projected[:, (heads + 1) * head_size :]
    query_heads = queries.reshape(seq_len, heads, head_size).astype(jnp.float32)
    keys_wide = key_rows.astype(jnp.float32)
    vals_wide = val_rows.astype(jnp.float32)
    position = jnp.arange(seq_len, dtype=jnp.int32)
    allowed = (doc_row[:, None] == doc_row[None, :]) & (position[None, :] <= position[:, None])
    scores = jnp.einsum("ihd,jd->hij", query_heads, keys_wide) * score_scale
    scores = jnp.where(allowed[None], scores, -jnp.inf)
    highest = jnp.max(scores, axis=2, keepdims=True)
    expon = jnp.exp(scores - highest)
    attn_probs = expon / jnp.sum(expon, axis=2, keepdims=True)
    factor = 1.0 + jnp.transpose(noise_rows.astype(jnp.float32), (1, 0, 2))
    dropped = (attn_probs * factor).astype(jnp.bfloat16)
    dropped_wide = dropped.astype(jnp.float32)
    attended = (
        jnp.einsum("hij,jd->ihd", dropped_wide, vals_wide)
        .astype(jnp.bfloat16)
        .reshape(seq_len, heads * head_size)
    )
    attn_grad = attn_wide.astype(jnp.bfloat16)
    grad_heads = attn_grad.reshape(seq_len, heads, head_size).astype(jnp.float32)
    val_grad = jnp.einsum("hij,ihd->jd", dropped_wide, grad_heads).astype(jnp.bfloat16)
    prob_grad = jnp.einsum("ihd,jd->hij", grad_heads, vals_wide) * factor
    inner = jnp.sum(attn_probs * prob_grad, axis=2, keepdims=True)
    score_grad = (attn_probs * (prob_grad - inner) * score_scale).astype(jnp.bfloat16)
    score_wide = score_grad.astype(jnp.float32)
    query_grad = (
        jnp.einsum("hij,jd->ihd", score_wide, keys_wide)
        .astype(jnp.bfloat16)
        .reshape(seq_len, heads * head_size)
    )
    key_grad = jnp.einsum("hij,ihd->jd", score_wide, query_heads).astype(jnp.bfloat16)
    stacked = jnp.concatenate([query_grad, key_grad, val_grad], axis=1)
    return (stacked, attended)


def weight_rows(hidden_rows, cot_rows, stacked, attended, first_row, row_count):
    hidden_cols = lax.dynamic_slice_in_dim(hidden_rows, first_row, row_count, 1)
    cot_cols = lax.dynamic_slice_in_dim(cot_rows, first_row, row_count, 1)
    proj_grad = jnp.dot(hidden_cols.T, stacked, preferred_element_type=jnp.float32)
    out_grad = jnp.dot(cot_cols.T, attended, preferred_element_type=jnp.float32)
    return jnp.concatenate([proj_grad, out_grad], axis=1)


def generic_device(
    layer_inputs,
    loss_adjoint_matrix,
    attention_projection_matrix,
    merge_projection_transposed,
    packed_sequence_labels,
    dropout_factors,
    straggler_filter,
):
    duplicate_workers = lax.axis_size("rep")
    member = lax.axis_index("rep")
    kept_worker = jnp.sum(jnp.arange(duplicate_workers, dtype=jnp.int32) * straggler_filter[:, 0])
    row_count = layer_inputs.shape[1] // duplicate_workers
    first_row = member * row_count
    qkv_full, out_full = (
        lax.all_gather(attention_projection_matrix, ("rep", "grp"), axis=0, tiled=True),
        lax.all_gather(merge_projection_transposed, ("rep", "grp"), axis=0, tiled=True),
    )
    projected_wide = jnp.dot(layer_inputs, qkv_full, preferred_element_type=jnp.float32)
    attn_wide = jnp.dot(loss_adjoint_matrix, out_full, preferred_element_type=jnp.float32)
    chosen_noise = from_root(dropout_factors[0], "rep", kept_worker)
    stacked, attended = token_grads(
        projected_wide, attn_wide, packed_sequence_labels[0], chosen_noise
    )
    gradient = weight_rows(
        layer_inputs, loss_adjoint_matrix, stacked, attended, first_row, row_count
    )
    return lax.psum_scatter(gradient, "grp", scatter_dimension=0, tiled=True)


def dot(a, b, dims):
    return lax.dot_general(a, b, (dims, ((), ())), preferred_element_type=jnp.float32)


VMEM = pl.BlockSpec(memory_space=pltpu.VMEM)
SMEM = pl.BlockSpec(memory_space=pltpu.SMEM)


def cost(flops, count):
    return pl.CostEstimate(flops=flops, bytes_accessed=count, transcendentals=0)


def flip_kernel(order_ref, x_ref, keep_ref, send_ref, flipped):
    half = keep_ref.shape[0]
    blocks = order_ref.shape[0]
    rows = 2 * half // blocks
    width = x_ref.shape[1]
    for first in range(0, width, 256):
        flipped[pl.ds(first, 256), :] = x_ref[:, pl.ds(first, 256)].T
    for block in range(blocks):
        first = pl.multiple_of(order_ref[block] * rows, 16)
        target = keep_ref if block < blocks // 2 else send_ref
        place = (block % (blocks // 2)) * rows
        target[pl.ds(place, rows), :] = flipped[pl.ds(first, rows), :]


def flip(order, x):
    tokens, width = x.shape
    out = jax.ShapeDtypeStruct((width // 2, tokens), x.dtype)
    return pl.pallas_call(
        flip_kernel,
        out_shape=(out, out),
        in_specs=[SMEM, VMEM],
        out_specs=(VMEM, VMEM),
        scratch_shapes=[pltpu.VMEM((width, tokens), x.dtype)],
        cost_estimate=cost(0, 4 * x.size),
        name="flip",
    )(order, x)


def stack_kernel(*refs):
    sources, out_ref, sems = refs[:-2], refs[-2], refs[-1]
    copies = []
    first = 0
    for n, source in enumerate(sources):
        rows = source.shape[0]
        copies.append(pltpu.make_async_copy(source, out_ref.at[pl.ds(first, rows), :], sems.at[n]))
        first += rows
    for copy in copies:
        copy.start()
    for copy in copies:
        copy.wait()


def stack(*pieces):
    shape = (sum(p.shape[0] for p in pieces), pieces[0].shape[1])
    return pl.pallas_call(
        stack_kernel,
        out_shape=jax.ShapeDtypeStruct(shape, pieces[0].dtype),
        in_specs=[pl.BlockSpec(memory_space=pl.ANY)] * len(pieces),
        out_specs=VMEM,
        scratch_shapes=[pltpu.SemaphoreType.DMA((len(pieces),))],
        cost_estimate=cost(0, 4 * shape[0] * shape[1]),
        name="stack",
    )(*pieces)


def one_on_other(a, b):
    zero = jnp.zeros((), a.dtype)
    above = lax.pad(a, zero, ((0, b.shape[0], 0), (0, 0, 0)))
    return above + lax.pad(b, zero, ((a.shape[0], 0, 0), (0, 0, 0)))


def forward_kernel(
    heads, member_ref, own_ref, other_ref, pair_ref, row_ref, column_ref, noise_ref,
    att_ref, probs_ref, parts_ref,
):
    tokens = own_ref.shape[0]
    size = pair_ref.shape[1]
    scale = 1.0 / math.sqrt(size)
    low = jnp.bfloat16

    def part(first):
        return (own_ref[:, pl.ds(first, size)] + other_ref[:, pl.ds(first, size)]).astype(low)

    first_member = member_ref[0] == 0
    mine = part(heads * size).astype(jnp.float32)
    pair = pair_ref[...].astype(jnp.float32)
    keys = jnp.where(first_member, mine, pair).astype(low)
    vals = jnp.where(first_member, pair, mine).astype(low)
    parts_ref[heads] = keys
    parts_ref[heads + 1] = vals
    query_at = lax.broadcasted_iota(jnp.int32, (tokens, tokens), 0)
    key_at = lax.broadcasted_iota(jnp.int32, (tokens, tokens), 1)
    allowed = (column_ref[...] == row_ref[...]) & (key_at <= query_at)
    for head in range(heads):
        query = part(head * size)
        parts_ref[head] = query
        scores = dot(query, keys, ((1,), (1,))) * scale
        scores = jnp.where(allowed, scores, -jnp.inf)
        expon = jnp.exp(scores - jnp.max(scores, axis=1, keepdims=True))
        probs = expon / jnp.sum(expon, axis=1, keepdims=True)
        probs_ref[head] = probs
        dropped = (probs * (1.0 + noise_ref[head].astype(jnp.float32))).astype(low)
        att_ref[:, pl.ds(head * size, size)] = dot(dropped, vals, ((1,), (0,))).astype(low)


def forward(member, own, other, pair, labels, noise):
    tokens, size = pair.shape
    heads = noise.shape[0]
    return pl.pallas_call(
        functools.partial(forward_kernel, heads),
        out_shape=(
            jax.ShapeDtypeStruct((tokens, heads * size), jnp.bfloat16),
            jax.ShapeDtypeStruct(noise.shape, jnp.float32),
            jax.ShapeDtypeStruct((heads + 2, tokens, size), jnp.bfloat16),
        ),
        in_specs=[SMEM] + [VMEM] * 6,
        out_specs=(VMEM,) * 3,
        cost_estimate=cost(4 * noise.size * size, 8 * own.size + 6 * noise.size),
        name="forward",
    )(member, own, other, pair, labels, labels.reshape(tokens, 1), noise)


def backward_kernel(
    heads, member_ref, own_ref, other_ref, probs_ref, parts_ref, noise_ref, query_ref, keep_ref, send_ref
):
    tokens, size = keep_ref.shape
    scale = 1.0 / math.sqrt(size)
    low = jnp.bfloat16
    first_member = member_ref[0] == 0
    keys, vals = parts_ref[heads], parts_ref[heads + 1]
    key_grad = jnp.zeros((tokens, size), jnp.float32)
    val_grad = jnp.zeros((tokens, size), jnp.float32)
    for head in range(heads):
        here = pl.ds(head * size, size)
        query, grad = parts_ref[head], (own_ref[:, here] + other_ref[:, here]).astype(low)
        probs = probs_ref[head]
        factor = 1.0 + noise_ref[head].astype(jnp.float32)
        dropped = (probs * factor).astype(low)
        val_grad += dot(dropped, grad, ((0,), (0,)))
        prob_grad = dot(grad, vals, ((1,), (1,))) * factor
        inner = jnp.sum(probs * prob_grad, axis=1, keepdims=True)
        score_grad = (probs * (prob_grad - inner) * scale).astype(low)
        query_ref[:, here] = dot(score_grad, keys, ((1,), (0,))).astype(low)
        key_grad += dot(score_grad, query, ((0,), (0,)))
    keep_ref[...] = jnp.where(first_member, key_grad, val_grad)
    send_ref[...] = jnp.where(first_member, val_grad, key_grad)


def backward(member, own, other, probs, parts, noise):
    heads, tokens, _ = noise.shape
    size = parts.shape[2]
    narrow = jax.ShapeDtypeStruct((tokens, size), jnp.float32)
    return pl.pallas_call(
        functools.partial(backward_kernel, heads),
        out_shape=(jax.ShapeDtypeStruct((tokens, heads * size), jnp.bfloat16), narrow, narrow),
        in_specs=[SMEM] + [VMEM] * 5,
        out_specs=(VMEM,) * 3,
        cost_estimate=cost(8 * noise.size * size, 6 * noise.size),
        name="backward",
    )(member, own, other, probs, parts, noise)


def place_kernel(member_ref, *refs):
    sources, out_ref = refs[:-1], refs[-1]

    def put(order):
        first = 0
        for pair in range(0, len(sources), 2):
            for n in order:
                source = sources[pair + n]
                out_ref[:, pl.ds(first, source.shape[1])] = source[pl.ds(0, out_ref.shape[0]), :].astype(
                    out_ref.dtype
                )
                first += source.shape[1]

    @pl.when(member_ref[0] == 0)
    def _():
        put((0, 1))

    @pl.when(member_ref[0] != 0)
    def _():
        put((1, 0))


def place_columns(member, *pieces):
    shape = (pieces[1].shape[0], sum(p.shape[1] for p in pieces))
    return pl.pallas_call(
        place_kernel,
        out_shape=jax.ShapeDtypeStruct(shape, pieces[0].dtype),
        in_specs=[SMEM] + [VMEM] * len(pieces),
        out_specs=VMEM,
        cost_estimate=cost(0, 8 * shape[0] * shape[1]),
        name="place",
    )(member, *pieces)


def paired_device(
    layer_inputs,
    loss_adjoint_matrix,
    attention_projection_matrix,
    merge_projection_transposed,
    packed_sequence_labels,
    dropout_factors,
    straggler_filter,
):
    grp = lax.axis_size("grp")
    member = lax.axis_index("rep")
    me = member * grp + lax.axis_index("grp")
    first = member == 0
    core, side, near, far = 1, 2, 4, 8

    def across(a, bit):
        return lax.ppermute(a, "grp", [(g, g ^ bit) for g in range(grp)])

    def across_rep(a):
        return lax.ppermute(a, "rep", [(0, 1), (1, 0)])

    heads = dropout_factors.shape[2]
    share = heads // 2
    width = merge_projection_transposed.shape[1]
    size = width // heads
    part = share * size

    def columns(a, first, count, m):
        return lax.dynamic_slice_in_dim(a, first + m * count, count, 1)

    def qkv_columns(m):
        queries = columns(attention_projection_matrix, 0, part, m)
        return jnp.concatenate(
            [queries, columns(attention_projection_matrix, width, size, m)], axis=1
        )

    def merge_columns(m):
        return columns(merge_projection_transposed, 0, part, m)

    def exchanged(pick):
        return one_on_other(pick(member), across_rep(pick(1 - member)))

    qkv = exchanged(qkv_columns)
    merge = exchanged(merge_columns)

    qkv_near, qkv_far = across(qkv, near), across(qkv, far)
    qkv_both = across(qkv_far, near)
    qkv_side = [
        across(qkv, side), across(qkv_far, side), across(qkv_near, side), across(qkv_both, side)
    ]
    merge_far = across(merge, far)
    merge_line = one_on_other(merge, merge_far)
    merge_pieces = [merge_line, across(merge_line, side), across(merge_line, near)]
    merge_pieces.append(across(merge_pieces[2], side))

    def order(bits):
        found = [0]
        for bit in (core, *bits, grp):
            found = [at | b for at in found for b in (0, bit)]
        return jnp.array(found, jnp.int32) ^ me

    stages = ((side, near, far), (near, side, far))
    x_keep, x_send = flip(order(stages[0]), layer_inputs)
    y_keep, y_send = flip(order(stages[1]), loss_adjoint_matrix)
    x_other, y_other = across(x_send, core), across(y_send, core)

    kept_worker = jnp.sum(jnp.arange(2, dtype=jnp.int32) * straggler_filter[:, 0])
    noise = across_rep(dropout_factors[0])
    noise = jnp.where(kept_worker == member, dropout_factors[0], noise)
    noise = jnp.where(first, noise[:, :share], noise[:, share:])
    noise_used = jnp.transpose(noise, (1, 0, 2))

    def project(rows, weights):
        return dot(rows, weights, ((0,), (0,)))

    qkv_parts = stack(qkv, qkv_far, qkv_near, qkv_both, *qkv_side)
    merge_pieces = stack(*merge_pieces)
    qkv_in = across(project(x_other, qkv_parts), core)
    qkv_own = project(x_keep, qkv_parts)
    merge_in = across(project(y_other, merge_pieces), core)
    merge_own = project(y_keep, merge_pieces)

    pair = (qkv_own[:, part:] + qkv_in[:, part:]).astype(jnp.bfloat16)
    pair = across_rep(pair)
    member = member.reshape(1)
    att, probs, pieces = forward(member, qkv_own, qkv_in, pair, packed_sequence_labels, noise_used)
    query_grad, pair_keep, pair_send = backward(
        member, merge_own, merge_in, probs, pieces, noise_used
    )
    pair_grad = (pair_keep + across_rep(pair_send)).astype(jnp.bfloat16)

    def reduced(keep, other, bits, grad, theirs):
        cut = keep.shape[0] // 2

        def half(rows):
            return dot(keep[rows], grad, ((1,), (0,))), other[rows]

        leaves, rows = half(slice(cut, None))
        leaves = (leaves + dot(rows, theirs, ((1,), (0,)))).astype(jnp.bfloat16)
        total, rows = half(slice(None, cut))
        for n, bit in enumerate(bits):
            arrived = across(leaves, bit)
            if n == 0:
                total = total + dot(rows, theirs, ((1,), (0,)))
            total = total + arrived.astype(jnp.float32)
            cut = total.shape[0] // 2
            whole = total
            leaves, total = total[cut:].astype(jnp.bfloat16), total[:cut]
        return whole, across_rep(leaves)

    merge = reduced(y_keep, y_other, stages[1], att, across(att, core))
    query = reduced(x_keep, x_other, stages[0], query_grad, across(query_grad, core))
    pair = reduced(x_keep, x_other, stages[0], pair_grad, across(pair_grad, core))
    return place_columns(member, *query, *pair, *merge)


def paired(mesh, shapes):
    rep, grp = mesh.shape["rep"], mesh.shape["grp"]
    depth, heads, tokens = shapes[0][1], shapes[5][2], shapes[5][3]
    size = shapes[3][1] // heads
    even = depth % (rep * grp * 16) == 0 and depth % 256 == 0
    return rep == 2 and grp == 16 and even and heads % 2 == 0 and size % 128 == 0 and tokens % 128 == 0


def solution(mesh):
    placed = (
        P("grp", None),
        P("grp", None),
        P(("rep", "grp"), None),
        P(("rep", "grp"), None),
        P("grp", None),
        P("rep", "grp", None, None),
        P(None, "grp"),
    )

    def on_devices(body):
        return jax.shard_map(
            body, mesh=mesh, in_specs=placed, out_specs=P(("rep", "grp"), None), check_vma=False
        )

    def step(*args):
        if not paired(mesh, [a.shape for a in args]):
            return on_devices(generic_device)(*args)
        return on_devices(paired_device)(*args)

    return step
```

```python
import functools
import math

import jax
import jax.numpy as jnp
from jax import lax
from jax.experimental import pallas as pl
from jax.experimental.pallas import tpu as pltpu
from jax.sharding import PartitionSpec as P


def from_root(block, axis, holder):
    block = jnp.where(lax.axis_index(axis) == holder, block, jnp.zeros_like(block))
    return lax.psum(block, axis)


def token_grads(projected_wide, attn_wide, doc_row, noise_rows):
    seq_len = projected_wide.shape[0]
    head_size = (projected_wide.shape[1] - attn_wide.shape[1]) // 2
    heads = attn_wide.shape[1] // head_size
    score_scale = 1.0 / jnp.sqrt(jnp.float32(head_size))
    projected = projected_wide.astype(jnp.bfloat16)
    queries = projected[:, : heads * head_size]
    key_rows = projected[:, heads * head_size : (heads + 1) * head_size]
    val_rows = projected[:, (heads + 1) * head_size :]
    query_heads = queries.reshape(seq_len, heads, head_size).astype(jnp.float32)
    keys_wide = key_rows.astype(jnp.float32)
    vals_wide = val_rows.astype(jnp.float32)
    position = jnp.arange(seq_len, dtype=jnp.int32)
    allowed = (doc_row[:, None] == doc_row[None, :]) & (position[None, :] <= position[:, None])
    scores = jnp.einsum("ihd,jd->hij", query_heads, keys_wide) * score_scale
    scores = jnp.where(allowed[None], scores, -jnp.inf)
    highest = jnp.max(scores, axis=2, keepdims=True)
    expon = jnp.exp(scores - highest)
    attn_probs = expon / jnp.sum(expon, axis=2, keepdims=True)
    factor = 1.0 + jnp.transpose(noise_rows.astype(jnp.float32), (1, 0, 2))
    dropped = (attn_probs * factor).astype(jnp.bfloat16)
    dropped_wide = dropped.astype(jnp.float32)
    attended = (
        jnp.einsum("hij,jd->ihd", dropped_wide, vals_wide)
        .astype(jnp.bfloat16)
        .reshape(seq_len, heads * head_size)
    )
    attn_grad = attn_wide.astype(jnp.bfloat16)
    grad_heads = attn_grad.reshape(seq_len, heads, head_size).astype(jnp.float32)
    val_grad = jnp.einsum("hij,ihd->jd", dropped_wide, grad_heads).astype(jnp.bfloat16)
    prob_grad = jnp.einsum("ihd,jd->hij", grad_heads, vals_wide) * factor
    inner = jnp.sum(attn_probs * prob_grad, axis=2, keepdims=True)
    score_grad = (attn_probs * (prob_grad - inner) * score_scale).astype(jnp.bfloat16)
    score_wide = score_grad.astype(jnp.float32)
    query_grad = (
        jnp.einsum("hij,jd->ihd", score_wide, keys_wide)
        .astype(jnp.bfloat16)
        .reshape(seq_len, heads * head_size)
    )
    key_grad = jnp.einsum("hij,ihd->jd", score_wide, query_heads).astype(jnp.bfloat16)
    stacked = jnp.concatenate([query_grad, key_grad, val_grad], axis=1)
    return (stacked, attended)


def weight_rows(hidden_rows, cot_rows, stacked, attended, first_row, row_count):
    hidden_cols = lax.dynamic_slice_in_dim(hidden_rows, first_row, row_count, 1)
    cot_cols = lax.dynamic_slice_in_dim(cot_rows, first_row, row_count, 1)
    proj_grad = jnp.dot(hidden_cols.T, stacked, preferred_element_type=jnp.float32)
    out_grad = jnp.dot(cot_cols.T, attended, preferred_element_type=jnp.float32)
    return jnp.concatenate([proj_grad, out_grad], axis=1)


def generic_device(
    layer_inputs,
    loss_adjoint_matrix,
    attention_projection_matrix,
    merge_projection_transposed,
    packed_sequence_labels,
    dropout_factors,
    straggler_filter,
):
    duplicate_workers = lax.axis_size("rep")
    member = lax.axis_index("rep")
    kept_worker = jnp.sum(jnp.arange(duplicate_workers, dtype=jnp.int32) * straggler_filter[:, 0])
    row_count = layer_inputs.shape[1] // duplicate_workers
    first_row = member * row_count
    qkv_full, out_full = (
        lax.all_gather(attention_projection_matrix, ("rep", "grp"), axis=0, tiled=True),
        lax.all_gather(merge_projection_transposed, ("rep", "grp"), axis=0, tiled=True),
    )
    projected_wide = jnp.dot(layer_inputs, qkv_full, preferred_element_type=jnp.float32)
    attn_wide = jnp.dot(loss_adjoint_matrix, out_full, preferred_element_type=jnp.float32)
    chosen_noise = from_root(dropout_factors[0], "rep", kept_worker)
    stacked, attended = token_grads(
        projected_wide, attn_wide, packed_sequence_labels[0], chosen_noise
    )
    gradient = weight_rows(
        layer_inputs, loss_adjoint_matrix, stacked, attended, first_row, row_count
    )
    return lax.psum_scatter(gradient, "grp", scatter_dimension=0, tiled=True)


def dot(a, b, dims):
    return lax.dot_general(a, b, (dims, ((), ())), preferred_element_type=jnp.float32)


VMEM = pl.BlockSpec(memory_space=pltpu.VMEM)
SMEM = pl.BlockSpec(memory_space=pltpu.SMEM)


def cost(flops, count):
    return pl.CostEstimate(flops=flops, bytes_accessed=count, transcendentals=0)


def flip_kernel(order_ref, x_ref, keep_ref, send_ref, flipped):
    half = keep_ref.shape[0]
    blocks = order_ref.shape[0]
    rows = 2 * half // blocks
    width = x_ref.shape[1]
    for first in range(0, width, 256):
        flipped[pl.ds(first, 256), :] = x_ref[:, pl.ds(first, 256)].T
    for block in range(blocks):
        first = pl.multiple_of(order_ref[block] * rows, 16)
        target = keep_ref if block < blocks // 2 else send_ref
        place = (block % (blocks // 2)) * rows
        target[pl.ds(place, rows), :] = flipped[pl.ds(first, rows), :]


def flip(order, x):
    tokens, width = x.shape
    out = jax.ShapeDtypeStruct((width // 2, tokens), x.dtype)
    return pl.pallas_call(
        flip_kernel,
        out_shape=(out, out),
        in_specs=[SMEM, VMEM],
        out_specs=(VMEM, VMEM),
        scratch_shapes=[pltpu.VMEM((width, tokens), x.dtype)],
        cost_estimate=cost(0, 4 * x.size),
        name="flip",
    )(order, x)


def stack_kernel(*refs):
    sources, out_ref, sems = refs[:-2], refs[-2], refs[-1]
    copies = []
    first = 0
    for n, source in enumerate(sources):
        rows = source.shape[0]
        copies.append(pltpu.make_async_copy(source, out_ref.at[pl.ds(first, rows), :], sems.at[n]))
        first += rows
    for copy in copies:
        copy.start()
    for copy in copies:
        copy.wait()


def stack(*pieces):
    shape = (sum(p.shape[0] for p in pieces), pieces[0].shape[1])
    return pl.pallas_call(
        stack_kernel,
        out_shape=jax.ShapeDtypeStruct(shape, pieces[0].dtype),
        in_specs=[pl.BlockSpec(memory_space=pl.ANY)] * len(pieces),
        out_specs=VMEM,
        scratch_shapes=[pltpu.SemaphoreType.DMA((len(pieces),))],
        cost_estimate=cost(0, 4 * shape[0] * shape[1]),
        name="stack",
    )(*pieces)


def one_on_other(a, b):
    zero = jnp.zeros((), a.dtype)
    above = lax.pad(a, zero, ((0, b.shape[0], 0), (0, 0, 0)))
    return above + lax.pad(b, zero, ((a.shape[0], 0, 0), (0, 0, 0)))


def forward_kernel(
    heads, member_ref, own_ref, other_ref, pair_ref, row_ref, column_ref, noise_ref,
    att_ref, probs_ref, parts_ref,
):
    tokens = own_ref.shape[0]
    size = pair_ref.shape[1]
    scale = 1.0 / math.sqrt(size)
    low = jnp.bfloat16

    def part(first):
        return (own_ref[:, pl.ds(first, size)] + other_ref[:, pl.ds(first, size)]).astype(low)

    first_member = member_ref[0] == 0
    mine = part(heads * size).astype(jnp.float32)
    pair = pair_ref[...].astype(jnp.float32)
    keys = jnp.where(first_member, mine, pair).astype(low)
    vals = jnp.where(first_member, pair, mine).astype(low)
    parts_ref[heads] = keys
    parts_ref[heads + 1] = vals
    query_at = lax.broadcasted_iota(jnp.int32, (tokens, tokens), 0)
    key_at = lax.broadcasted_iota(jnp.int32, (tokens, tokens), 1)
    allowed = (column_ref[...] == row_ref[...]) & (key_at <= query_at)
    for head in range(heads):
        query = part(head * size)
        parts_ref[head] = query
        scores = dot(query, keys, ((1,), (1,))) * scale
        scores = jnp.where(allowed, scores, -jnp.inf)
        expon = jnp.exp(scores - jnp.max(scores, axis=1, keepdims=True))
        probs = expon / jnp.sum(expon, axis=1, keepdims=True)
        probs_ref[head] = probs
        dropped = (probs * (1.0 + noise_ref[head].astype(jnp.float32))).astype(low)
        att_ref[:, pl.ds(head * size, size)] = dot(dropped, vals, ((1,), (0,))).astype(low)


def forward(member, own, other, pair, labels, noise):
    tokens, size = pair.shape
    heads = noise.shape[0]
    return pl.pallas_call(
        functools.partial(forward_kernel, heads),
        out_shape=(
            jax.ShapeDtypeStruct((tokens, heads * size), jnp.bfloat16),
            jax.ShapeDtypeStruct(noise.shape, jnp.float32),
            jax.ShapeDtypeStruct((heads + 2, tokens, size), jnp.bfloat16),
        ),
        in_specs=[SMEM] + [VMEM] * 6,
        out_specs=(VMEM,) * 3,
        cost_estimate=cost(4 * noise.size * size, 8 * own.size + 6 * noise.size),
        name="forward",
    )(member, own, other, pair, labels, labels.reshape(tokens, 1), noise)


def backward_kernel(
    heads, member_ref, own_ref, other_ref, probs_ref, parts_ref, noise_ref, query_ref, keep_ref, send_ref
):
    tokens, size = keep_ref.shape
    scale = 1.0 / math.sqrt(size)
    low = jnp.bfloat16
    first_member = member_ref[0] == 0
    keys, vals = parts_ref[heads], parts_ref[heads + 1]
    key_grad = jnp.zeros((tokens, size), jnp.float32)
    val_grad = jnp.zeros((tokens, size), jnp.float32)
    for head in range(heads):
        here = pl.ds(head * size, size)
        query, grad = parts_ref[head], (own_ref[:, here] + other_ref[:, here]).astype(low)
        probs = probs_ref[head]
        factor = 1.0 + noise_ref[head].astype(jnp.float32)
        dropped = (probs * factor).astype(low)
        val_grad += dot(dropped, grad, ((0,), (0,)))
        prob_grad = dot(grad, vals, ((1,), (1,))) * factor
        inner = jnp.sum(probs * prob_grad, axis=1, keepdims=True)
        score_grad = (probs * (prob_grad - inner) * scale).astype(low)
        query_ref[:, here] = dot(score_grad, keys, ((1,), (0,))).astype(low)
        key_grad += dot(score_grad, query, ((0,), (0,)))
    keep_ref[...] = jnp.where(first_member, key_grad, val_grad)
    send_ref[...] = jnp.where(first_member, val_grad, key_grad)


def backward(member, own, other, probs, parts, noise):
    heads, tokens, _ = noise.shape
    size = parts.shape[2]
    narrow = jax.ShapeDtypeStruct((tokens, size), jnp.float32)
    return pl.pallas_call(
        functools.partial(backward_kernel, heads),
        out_shape=(jax.ShapeDtypeStruct((tokens, heads * size), jnp.bfloat16), narrow, narrow),
        in_specs=[SMEM] + [VMEM] * 5,
        out_specs=(VMEM,) * 3,
        cost_estimate=cost(8 * noise.size * size, 6 * noise.size),
        name="backward",
    )(member, own, other, probs, parts, noise)


def place_kernel(member_ref, *refs):
    sources, out_ref = refs[:-1], refs[-1]

    def put(order):
        first = 0
        for pair in range(0, len(sources), 2):
            for n in order:
                source = sources[pair + n]
                out_ref[:, pl.ds(first, source.shape[1])] = source[pl.ds(0, out_ref.shape[0]), :].astype(
                    out_ref.dtype
                )
                first += source.shape[1]

    @pl.when(member_ref[0] == 0)
    def _():
        put((0, 1))

    @pl.when(member_ref[0] != 0)
    def _():
        put((1, 0))


def place_columns(member, *pieces):
    shape = (pieces[1].shape[0], sum(p.shape[1] for p in pieces))
    return pl.pallas_call(
        place_kernel,
        out_shape=jax.ShapeDtypeStruct(shape, pieces[0].dtype),
        in_specs=[SMEM] + [VMEM] * len(pieces),
        out_specs=VMEM,
        cost_estimate=cost(0, 8 * shape[0] * shape[1]),
        name="place",
    )(member, *pieces)


def paired_device(
    layer_inputs,
    loss_adjoint_matrix,
    attention_projection_matrix,
    merge_projection_transposed,
    packed_sequence_labels,
    dropout_factors,
    straggler_filter,
):
    grp = lax.axis_size("grp")
    member = lax.axis_index("rep")
    me = member * grp + lax.axis_index("grp")
    first = member == 0
    core, side, near, far = 1, 2, 4, 8

    def across(a, bit):
        return lax.ppermute(a, "grp", [(g, g ^ bit) for g in range(grp)])

    def across_rep(a):
        return lax.ppermute(a, "rep", [(0, 1), (1, 0)])

    heads = dropout_factors.shape[2]
    share = heads // 2
    width = merge_projection_transposed.shape[1]
    size = width // heads
    part = share * size

    def columns(a, first, count, m):
        return lax.dynamic_slice_in_dim(a, first + m * count, count, 1)

    def qkv_columns(m):
        queries = columns(attention_projection_matrix, 0, part, m)
        return jnp.concatenate(
            [queries, columns(attention_projection_matrix, width, size, m)], axis=1
        )

    def merge_columns(m):
        return columns(merge_projection_transposed, 0, part, m)

    def exchanged(pick):
        return one_on_other(pick(member), across_rep(pick(1 - member)))

    qkv = exchanged(qkv_columns)
    merge = exchanged(merge_columns)

    qkv_near, qkv_far = across(qkv, near), across(qkv, far)
    qkv_both = across(qkv_far, near)
    qkv_side = [across(qkv, side), across(qkv_far, side), across(qkv_near, side), across(qkv_both, side)]
    merge_far = across(merge, far)
    merge_line = one_on_other(merge, merge_far)
    merge_near = across(merge_line, near)
    merge_pieces = [merge_line, merge_near, across(merge_line, side), across(merge_near, side)]

    def order(bits):
        found = [0]
        for bit in (core, *bits, grp):
            found = [at | b for at in found for b in (0, bit)]
        return jnp.array(found, jnp.int32) ^ me

    stages = ((near, side, far), (side, near, far))
    x_keep, x_send = flip(order(stages[0]), layer_inputs)
    y_keep, y_send = flip(order(stages[1]), loss_adjoint_matrix)
    x_other, y_other = across(x_send, core), across(y_send, core)

    kept_worker = jnp.sum(jnp.arange(2, dtype=jnp.int32) * straggler_filter[:, 0])
    noise = across_rep(dropout_factors[0])
    noise = jnp.where(kept_worker == member, dropout_factors[0], noise)
    noise = jnp.where(first, noise[:, :share], noise[:, share:])
    noise_used = jnp.transpose(noise, (1, 0, 2))

    def project(rows, weights):
        return dot(rows, weights, ((0,), (0,)))

    qkv_parts = stack(qkv, qkv_far, *qkv_side[:2], qkv_near, qkv_both, *qkv_side[2:])
    merge_pieces = stack(*merge_pieces)
    qkv_in = across(project(x_other, qkv_parts), core)
    qkv_own = project(x_keep, qkv_parts)
    merge_in = across(project(y_other, merge_pieces), core)
    merge_own = project(y_keep, merge_pieces)

    pair = (qkv_own[:, part:] + qkv_in[:, part:]).astype(jnp.bfloat16)
    pair = across_rep(pair)
    member = member.reshape(1)
    att, probs, pieces = forward(member, qkv_own, qkv_in, pair, packed_sequence_labels, noise_used)
    query_grad, pair_keep, pair_send = backward(
        member, merge_own, merge_in, probs, pieces, noise_used
    )
    pair_grad = (pair_keep + across_rep(pair_send)).astype(jnp.bfloat16)

    def first_two_exchanged(rows):
        halves = rows.reshape(2, 2, rows.shape[0] // 4, rows.shape[1])
        return jnp.swapaxes(halves, 0, 1).reshape(rows.shape)

    def reduced(keep, other, bits, grad, theirs):
        cut = keep.shape[0] // 2

        def half(rows):
            return dot(keep[rows], grad, ((1,), (0,))), other[rows]

        leaves, rows = half(slice(cut, None))
        leaves = (leaves + dot(rows, theirs, ((1,), (0,)))).astype(jnp.bfloat16)
        total, rows = half(slice(None, cut))
        for n, bit in enumerate(bits):
            arrived = across(leaves, bit)
            if n == 0:
                total = total + dot(rows, theirs, ((1,), (0,)))
            total = total + arrived.astype(jnp.float32)
            cut = total.shape[0] // 2
            whole = total
            leaves, total = total[cut:].astype(jnp.bfloat16), total[:cut]
        return whole, across_rep(leaves)

    merge = reduced(y_keep, y_other, stages[1], att, across(att, core))
    query = reduced(x_keep, x_other, stages[0], query_grad, across(query_grad, core))
    x_keep, x_other = first_two_exchanged(x_keep), first_two_exchanged(x_other)
    pair = reduced(x_keep, x_other, stages[1], pair_grad, across(pair_grad, core))
    return place_columns(member, *query, *pair, *merge)


def paired(mesh, shapes):
    rep, grp = mesh.shape["rep"], mesh.shape["grp"]
    depth, heads, tokens = shapes[0][1], shapes[5][2], shapes[5][3]
    size = shapes[3][1] // heads
    even = depth % (rep * grp * 16) == 0 and depth % 256 == 0
    return rep == 2 and grp == 16 and even and heads % 2 == 0 and size % 128 == 0 and tokens % 128 == 0


def solution(mesh):
    placed = (
        P("grp", None),
        P("grp", None),
        P(("rep", "grp"), None),
        P(("rep", "grp"), None),
        P("grp", None),
        P("rep", "grp", None, None),
        P(None, "grp"),
    )

    def on_devices(body):
        return jax.shard_map(
            body, mesh=mesh, in_specs=placed, out_specs=P(("rep", "grp"), None), check_vma=False
        )

    def step(*args):
        if not paired(mesh, [a.shape for a in args]):
            return on_devices(generic_device)(*args)
        return on_devices(paired_device)(*args)

    return step
```

```python
import functools
import math

import jax
import jax.numpy as jnp
from jax import lax
from jax.experimental import pallas as pl
from jax.experimental.pallas import tpu as pltpu
from jax.sharding import PartitionSpec as P


def from_root(block, axis, holder):
    block = jnp.where(lax.axis_index(axis) == holder, block, jnp.zeros_like(block))
    return lax.psum(block, axis)


def token_grads(projected_wide, attn_wide, doc_row, noise_rows):
    seq_len = projected_wide.shape[0]
    head_size = (projected_wide.shape[1] - attn_wide.shape[1]) // 2
    heads = attn_wide.shape[1] // head_size
    score_scale = 1.0 / jnp.sqrt(jnp.float32(head_size))
    projected = projected_wide.astype(jnp.bfloat16)
    queries = projected[:, : heads * head_size]
    key_rows = projected[:, heads * head_size : (heads + 1) * head_size]
    val_rows = projected[:, (heads + 1) * head_size :]
    query_heads = queries.reshape(seq_len, heads, head_size).astype(jnp.float32)
    keys_wide = key_rows.astype(jnp.float32)
    vals_wide = val_rows.astype(jnp.float32)
    position = jnp.arange(seq_len, dtype=jnp.int32)
    allowed = (doc_row[:, None] == doc_row[None, :]) & (position[None, :] <= position[:, None])
    scores = jnp.einsum("ihd,jd->hij", query_heads, keys_wide) * score_scale
    scores = jnp.where(allowed[None], scores, -jnp.inf)
    highest = jnp.max(scores, axis=2, keepdims=True)
    expon = jnp.exp(scores - highest)
    attn_probs = expon / jnp.sum(expon, axis=2, keepdims=True)
    factor = 1.0 + jnp.transpose(noise_rows.astype(jnp.float32), (1, 0, 2))
    dropped = (attn_probs * factor).astype(jnp.bfloat16)
    dropped_wide = dropped.astype(jnp.float32)
    attended = (
        jnp.einsum("hij,jd->ihd", dropped_wide, vals_wide)
        .astype(jnp.bfloat16)
        .reshape(seq_len, heads * head_size)
    )
    attn_grad = attn_wide.astype(jnp.bfloat16)
    grad_heads = attn_grad.reshape(seq_len, heads, head_size).astype(jnp.float32)
    val_grad = jnp.einsum("hij,ihd->jd", dropped_wide, grad_heads).astype(jnp.bfloat16)
    prob_grad = jnp.einsum("ihd,jd->hij", grad_heads, vals_wide) * factor
    inner = jnp.sum(attn_probs * prob_grad, axis=2, keepdims=True)
    score_grad = (attn_probs * (prob_grad - inner) * score_scale).astype(jnp.bfloat16)
    score_wide = score_grad.astype(jnp.float32)
    query_grad = (
        jnp.einsum("hij,jd->ihd", score_wide, keys_wide)
        .astype(jnp.bfloat16)
        .reshape(seq_len, heads * head_size)
    )
    key_grad = jnp.einsum("hij,ihd->jd", score_wide, query_heads).astype(jnp.bfloat16)
    stacked = jnp.concatenate([query_grad, key_grad, val_grad], axis=1)
    return (stacked, attended)


def weight_rows(hidden_rows, cot_rows, stacked, attended, first_row, row_count):
    hidden_cols = lax.dynamic_slice_in_dim(hidden_rows, first_row, row_count, 1)
    cot_cols = lax.dynamic_slice_in_dim(cot_rows, first_row, row_count, 1)
    proj_grad = jnp.dot(hidden_cols.T, stacked, preferred_element_type=jnp.float32)
    out_grad = jnp.dot(cot_cols.T, attended, preferred_element_type=jnp.float32)
    return jnp.concatenate([proj_grad, out_grad], axis=1)


def generic_device(
    layer_inputs,
    loss_adjoint_matrix,
    attention_projection_matrix,
    merge_projection_transposed,
    packed_sequence_labels,
    dropout_factors,
    straggler_filter,
):
    duplicate_workers = lax.axis_size("rep")
    member = lax.axis_index("rep")
    kept_worker = jnp.sum(jnp.arange(duplicate_workers, dtype=jnp.int32) * straggler_filter[:, 0])
    row_count = layer_inputs.shape[1] // duplicate_workers
    first_row = member * row_count
    qkv_full, out_full = (
        lax.all_gather(attention_projection_matrix, ("rep", "grp"), axis=0, tiled=True),
        lax.all_gather(merge_projection_transposed, ("rep", "grp"), axis=0, tiled=True),
    )
    projected_wide = jnp.dot(layer_inputs, qkv_full, preferred_element_type=jnp.float32)
    attn_wide = jnp.dot(loss_adjoint_matrix, out_full, preferred_element_type=jnp.float32)
    chosen_noise = from_root(dropout_factors[0], "rep", kept_worker)
    stacked, attended = token_grads(
        projected_wide, attn_wide, packed_sequence_labels[0], chosen_noise
    )
    gradient = weight_rows(
        layer_inputs, loss_adjoint_matrix, stacked, attended, first_row, row_count
    )
    return lax.psum_scatter(gradient, "grp", scatter_dimension=0, tiled=True)


def dot(a, b, dims):
    return lax.dot_general(a, b, (dims, ((), ())), preferred_element_type=jnp.float32)


VMEM = pl.BlockSpec(memory_space=pltpu.VMEM)
SMEM = pl.BlockSpec(memory_space=pltpu.SMEM)


def room(mebibytes):
    return pltpu.CompilerParams(vmem_limit_bytes=mebibytes << 20)


def cost(flops, count):
    return pl.CostEstimate(flops=flops, bytes_accessed=count, transcendentals=0)


def flip_kernel(order_ref, x_ref, keep_ref, send_ref, flipped):
    half = keep_ref.shape[0]
    blocks = order_ref.shape[0]
    rows = 2 * half // blocks
    width = x_ref.shape[1]
    for first in range(0, width, 256):
        flipped[pl.ds(first, 256), :] = x_ref[:, pl.ds(first, 256)].T
    for block in range(blocks):
        first = pl.multiple_of(order_ref[block] * rows, 16)
        target = keep_ref if block < blocks // 2 else send_ref
        place = (block % (blocks // 2)) * rows
        target[pl.ds(place, rows), :] = flipped[pl.ds(first, rows), :]


def flip(order, x):
    tokens, width = x.shape
    out = jax.ShapeDtypeStruct((width // 2, tokens), x.dtype)
    return pl.pallas_call(
        flip_kernel,
        out_shape=(out, out),
        in_specs=[SMEM, VMEM],
        out_specs=(VMEM, VMEM),
        scratch_shapes=[pltpu.VMEM((width, tokens), x.dtype)],
        cost_estimate=cost(0, 4 * x.size),
        compiler_params=room(10),
        name="flip",
    )(order, x)


def stack_kernel(*refs):
    sources, out_ref, sems = refs[:-2], refs[-2], refs[-1]
    copies = []
    first = 0
    for n, source in enumerate(sources):
        rows = source.shape[0]
        copies.append(pltpu.make_async_copy(source, out_ref.at[pl.ds(first, rows), :], sems.at[n]))
        first += rows
    for copy in copies:
        copy.start()
    for copy in copies:
        copy.wait()


def stack(*pieces):
    shape = (sum(p.shape[0] for p in pieces), pieces[0].shape[1])
    return pl.pallas_call(
        stack_kernel,
        out_shape=jax.ShapeDtypeStruct(shape, pieces[0].dtype),
        in_specs=[pl.BlockSpec(memory_space=pl.ANY)] * len(pieces),
        out_specs=VMEM,
        scratch_shapes=[pltpu.SemaphoreType.DMA((len(pieces),))],
        cost_estimate=cost(0, 4 * shape[0] * shape[1]),
        compiler_params=room(4),
        name="stack",
    )(*pieces)


def one_on_other(a, b):
    zero = jnp.zeros((), a.dtype)
    above = lax.pad(a, zero, ((0, b.shape[0], 0), (0, 0, 0)))
    return above + lax.pad(b, zero, ((a.shape[0], 0, 0), (0, 0, 0)))


def forward_kernel(
    heads, member_ref, own_ref, other_ref, pair_ref, row_ref, column_ref, noise_ref,
    att_ref, probs_ref, parts_ref,
):
    tokens = own_ref.shape[0]
    size = pair_ref.shape[1]
    scale = 1.0 / math.sqrt(size)
    low = jnp.bfloat16

    def part(first):
        return (own_ref[:, pl.ds(first, size)] + other_ref[:, pl.ds(first, size)]).astype(low)

    first_member = member_ref[0] == 0
    mine = part(heads * size).astype(jnp.float32)
    pair = pair_ref[...].astype(jnp.float32)
    keys = jnp.where(first_member, mine, pair).astype(low)
    vals = jnp.where(first_member, pair, mine).astype(low)
    parts_ref[heads] = keys
    parts_ref[heads + 1] = vals
    query_at = lax.broadcasted_iota(jnp.int32, (tokens, tokens), 0)
    key_at = lax.broadcasted_iota(jnp.int32, (tokens, tokens), 1)
    allowed = (column_ref[...] == row_ref[...]) & (key_at <= query_at)
    for head in range(heads):
        query = part(head * size)
        parts_ref[head] = query
        scores = dot(query, keys, ((1,), (1,))) * scale
        scores = jnp.where(allowed, scores, -jnp.inf)
        expon = jnp.exp(scores - jnp.max(scores, axis=1, keepdims=True))
        probs = expon / jnp.sum(expon, axis=1, keepdims=True)
        probs_ref[head] = probs
        dropped = (probs * (1.0 + noise_ref[head].astype(jnp.float32))).astype(low)
        att_ref[:, pl.ds(head * size, size)] = dot(dropped, vals, ((1,), (0,))).astype(low)


def forward(member, own, other, pair, labels, noise):
    tokens, size = pair.shape
    heads = noise.shape[0]
    return pl.pallas_call(
        functools.partial(forward_kernel, heads),
        out_shape=(
            jax.ShapeDtypeStruct((tokens, heads * size), jnp.bfloat16),
            jax.ShapeDtypeStruct(noise.shape, jnp.float32),
            jax.ShapeDtypeStruct((heads + 2, tokens, size), jnp.bfloat16),
        ),
        in_specs=[SMEM] + [VMEM] * 6,
        out_specs=(VMEM,) * 3,
        cost_estimate=cost(4 * noise.size * size, 8 * own.size + 6 * noise.size),
        compiler_params=room(10),
        name="forward",
    )(member, own, other, pair, labels, labels.reshape(tokens, 1), noise)


def backward_kernel(
    heads, member_ref, own_ref, other_ref, probs_ref, parts_ref, noise_ref, query_ref, keep_ref, send_ref
):
    tokens, size = keep_ref.shape
    scale = 1.0 / math.sqrt(size)
    low = jnp.bfloat16
    first_member = member_ref[0] == 0
    keys, vals = parts_ref[heads], parts_ref[heads + 1]
    key_grad = jnp.zeros((tokens, size), jnp.float32)
    val_grad = jnp.zeros((tokens, size), jnp.float32)
    for head in range(heads):
        here = pl.ds(head * size, size)
        query, grad = parts_ref[head], (own_ref[:, here] + other_ref[:, here]).astype(low)
        probs = probs_ref[head]
        factor = 1.0 + noise_ref[head].astype(jnp.float32)
        dropped = (probs * factor).astype(low)
        val_grad += dot(dropped, grad, ((0,), (0,)))
        prob_grad = dot(grad, vals, ((1,), (1,))) * factor
        inner = jnp.sum(probs * prob_grad, axis=1, keepdims=True)
        score_grad = (probs * (prob_grad - inner) * scale).astype(low)
        query_ref[:, here] = dot(score_grad, keys, ((1,), (0,))).astype(low)
        key_grad += dot(score_grad, query, ((0,), (0,)))
    keep_ref[...] = jnp.where(first_member, key_grad, val_grad)
    send_ref[...] = jnp.where(first_member, val_grad, key_grad)


def backward(member, own, other, probs, parts, noise):
    heads, tokens, _ = noise.shape
    size = parts.shape[2]
    narrow = jax.ShapeDtypeStruct((tokens, size), jnp.float32)
    return pl.pallas_call(
        functools.partial(backward_kernel, heads),
        out_shape=(jax.ShapeDtypeStruct((tokens, heads * size), jnp.bfloat16), narrow, narrow),
        in_specs=[SMEM] + [VMEM] * 5,
        out_specs=(VMEM,) * 3,
        cost_estimate=cost(8 * noise.size * size, 6 * noise.size),
        compiler_params=room(10),
        name="backward",
    )(member, own, other, probs, parts, noise)


def place_kernel(member_ref, *refs):
    sources, out_ref = refs[:-1], refs[-1]

    def put(order):
        first = 0
        for pair in range(0, len(sources), 2):
            for n in order:
                source = sources[pair + n]
                out_ref[:, pl.ds(first, source.shape[1])] = source[pl.ds(0, out_ref.shape[0]), :].astype(
                    out_ref.dtype
                )
                first += source.shape[1]

    @pl.when(member_ref[0] == 0)
    def _():
        put((0, 1))

    @pl.when(member_ref[0] != 0)
    def _():
        put((1, 0))


def place_columns(member, *pieces):
    shape = (pieces[1].shape[0], sum(p.shape[1] for p in pieces))
    return pl.pallas_call(
        place_kernel,
        out_shape=jax.ShapeDtypeStruct(shape, pieces[0].dtype),
        in_specs=[SMEM] + [VMEM] * len(pieces),
        out_specs=VMEM,
        cost_estimate=cost(0, 8 * shape[0] * shape[1]),
        compiler_params=room(4),
        name="place",
    )(member, *pieces)


def paired_device(
    layer_inputs,
    loss_adjoint_matrix,
    attention_projection_matrix,
    merge_projection_transposed,
    packed_sequence_labels,
    dropout_factors,
    straggler_filter,
):
    grp = lax.axis_size("grp")
    member = lax.axis_index("rep")
    me = member * grp + lax.axis_index("grp")
    first = member == 0
    core, side, near, far = 1, 2, 4, 8

    def across(a, bit):
        return lax.ppermute(a, "grp", [(g, g ^ bit) for g in range(grp)])

    def across_rep(a):
        return lax.ppermute(a, "rep", [(0, 1), (1, 0)])

    heads = dropout_factors.shape[2]
    share = heads // 2
    width = merge_projection_transposed.shape[1]
    size = width // heads
    part = share * size

    def columns(a, first, count, m):
        return lax.dynamic_slice_in_dim(a, first + m * count, count, 1)

    def qkv_columns(m):
        queries = columns(attention_projection_matrix, 0, part, m)
        return jnp.concatenate(
            [queries, columns(attention_projection_matrix, width, size, m)], axis=1
        )

    def merge_columns(m):
        return columns(merge_projection_transposed, 0, part, m)

    def exchanged(pick):
        return one_on_other(pick(member), across_rep(pick(1 - member)))

    qkv = exchanged(qkv_columns)
    merge = exchanged(merge_columns)

    qkv_near, qkv_far = across(qkv, near), across(qkv, far)
    qkv_both = across(qkv_far, near)
    qkv_side = [
        across(qkv, side), across(qkv_far, side), across(qkv_near, side), across(qkv_both, side)
    ]
    merge_far = across(merge, far)
    merge_line = one_on_other(merge, merge_far)
    merge_near = across(merge_line, near)
    merge_pieces = [merge_line, merge_near, across(merge_line, side), across(merge_near, side)]

    def order(bits):
        found = [0]
        for bit in (core, *bits, grp):
            found = [at | b for at in found for b in (0, bit)]
        return jnp.array(found, jnp.int32) ^ me

    stages = ((near, side, far), (side, near, far))
    x_keep, x_send = flip(order(stages[0]), layer_inputs)
    y_keep, y_send = flip(order(stages[1]), loss_adjoint_matrix)
    x_other, y_other = across(x_send, core), across(y_send, core)

    kept_worker = jnp.sum(jnp.arange(2, dtype=jnp.int32) * straggler_filter[:, 0])
    noise = across_rep(dropout_factors[0])
    noise = jnp.where(kept_worker == member, dropout_factors[0], noise)
    noise = jnp.where(first, noise[:, :share], noise[:, share:])
    noise_used = jnp.transpose(noise, (1, 0, 2))

    def project(rows, weights):
        return dot(rows, weights, ((0,), (0,)))

    qkv_parts = stack(qkv, qkv_far, *qkv_side[:2], qkv_near, qkv_both, *qkv_side[2:])
    merge_pieces = stack(*merge_pieces)
    qkv_in = across(project(x_other, qkv_parts), core)
    qkv_own = project(x_keep, qkv_parts)
    merge_in = across(project(y_other, merge_pieces), core)
    merge_own = project(y_keep, merge_pieces)

    pair = (qkv_own[:, part:] + qkv_in[:, part:]).astype(jnp.bfloat16)
    pair = across_rep(pair)
    member = member.reshape(1)
    att, probs, pieces = forward(member, qkv_own, qkv_in, pair, packed_sequence_labels, noise_used)
    query_grad, pair_keep, pair_send = backward(
        member, merge_own, merge_in, probs, pieces, noise_used
    )
    pair_grad = (pair_keep + across_rep(pair_send)).astype(jnp.bfloat16)

    def first_two_exchanged(rows):
        halves = rows.reshape(2, 2, rows.shape[0] // 4, rows.shape[1])
        return jnp.swapaxes(halves, 0, 1).reshape(rows.shape)

    def reduced(keep, other, bits, grad, theirs):
        cut = keep.shape[0] // 2

        def half(rows):
            return dot(keep[rows], grad, ((1,), (0,))), other[rows]

        leaves, rows = half(slice(cut, None))
        leaves = (leaves + dot(rows, theirs, ((1,), (0,)))).astype(jnp.bfloat16)
        total, rows = half(slice(None, cut))
        for n, bit in enumerate(bits):
            arrived = across(leaves, bit)
            if n == 0:
                total = total + dot(rows, theirs, ((1,), (0,)))
            total = total + arrived.astype(jnp.float32)
            cut = total.shape[0] // 2
            whole = total
            leaves, total = total[cut:].astype(jnp.bfloat16), total[:cut]
        return whole, across_rep(leaves)

    merge = reduced(y_keep, y_other, stages[1], att, across(att, core))
    query = reduced(x_keep, x_other, stages[0], query_grad, across(query_grad, core))
    x_keep, x_other = first_two_exchanged(x_keep), first_two_exchanged(x_other)
    pair = reduced(x_keep, x_other, stages[1], pair_grad, across(pair_grad, core))
    return place_columns(member, *query, *pair, *merge)


def paired(mesh, shapes):
    rep, grp = mesh.shape["rep"], mesh.shape["grp"]
    depth, heads, tokens = shapes[0][1], shapes[5][2], shapes[5][3]
    size = shapes[3][1] // heads
    even = depth % (rep * grp * 16) == 0 and depth % 256 == 0
    return rep == 2 and grp == 16 and even and heads % 2 == 0 and size % 128 == 0 and tokens % 128 == 0


def solution(mesh):
    placed = (
        P("grp", None),
        P("grp", None),
        P(("rep", "grp"), None),
        P(("rep", "grp"), None),
        P("grp", None),
        P("rep", "grp", None, None),
        P(None, "grp"),
    )

    def on_devices(body):
        return jax.shard_map(
            body, mesh=mesh, in_specs=placed, out_specs=P(("rep", "grp"), None), check_vma=False
        )

    def step(*args):
        if not paired(mesh, [a.shape for a in args]):
            return on_devices(generic_device)(*args)
        return on_devices(paired_device)(*args)

    return step
```

```python
import functools
import math

import jax
import jax.numpy as jnp
from jax import lax
from jax.experimental import pallas as pl
from jax.experimental.layout import Layout, with_layout_constraint
from jax.experimental.pallas import tpu as pltpu
from jax.sharding import PartitionSpec as P


def from_root(block, axis, holder):
    block = jnp.where(lax.axis_index(axis) == holder, block, jnp.zeros_like(block))
    return lax.psum(block, axis)


def token_grads(projected_wide, attn_wide, doc_row, noise_rows):
    seq_len = projected_wide.shape[0]
    head_size = (projected_wide.shape[1] - attn_wide.shape[1]) // 2
    heads = attn_wide.shape[1] // head_size
    score_scale = 1.0 / jnp.sqrt(jnp.float32(head_size))
    projected = projected_wide.astype(jnp.bfloat16)
    queries = projected[:, : heads * head_size]
    key_rows = projected[:, heads * head_size : (heads + 1) * head_size]
    val_rows = projected[:, (heads + 1) * head_size :]
    query_heads = queries.reshape(seq_len, heads, head_size).astype(jnp.float32)
    keys_wide = key_rows.astype(jnp.float32)
    vals_wide = val_rows.astype(jnp.float32)
    position = jnp.arange(seq_len, dtype=jnp.int32)
    allowed = (doc_row[:, None] == doc_row[None, :]) & (position[None, :] <= position[:, None])
    scores = jnp.einsum("ihd,jd->hij", query_heads, keys_wide) * score_scale
    scores = jnp.where(allowed[None], scores, -jnp.inf)
    highest = jnp.max(scores, axis=2, keepdims=True)
    expon = jnp.exp(scores - highest)
    attn_probs = expon / jnp.sum(expon, axis=2, keepdims=True)
    factor = 1.0 + jnp.transpose(noise_rows.astype(jnp.float32), (1, 0, 2))
    dropped = (attn_probs * factor).astype(jnp.bfloat16)
    dropped_wide = dropped.astype(jnp.float32)
    attended = (
        jnp.einsum("hij,jd->ihd", dropped_wide, vals_wide)
        .astype(jnp.bfloat16)
        .reshape(seq_len, heads * head_size)
    )
    attn_grad = attn_wide.astype(jnp.bfloat16)
    grad_heads = attn_grad.reshape(seq_len, heads, head_size).astype(jnp.float32)
    val_grad = jnp.einsum("hij,ihd->jd", dropped_wide, grad_heads).astype(jnp.bfloat16)
    prob_grad = jnp.einsum("ihd,jd->hij", grad_heads, vals_wide) * factor
    inner = jnp.sum(attn_probs * prob_grad, axis=2, keepdims=True)
    score_grad = (attn_probs * (prob_grad - inner) * score_scale).astype(jnp.bfloat16)
    score_wide = score_grad.astype(jnp.float32)
    query_grad = (
        jnp.einsum("hij,jd->ihd", score_wide, keys_wide)
        .astype(jnp.bfloat16)
        .reshape(seq_len, heads * head_size)
    )
    key_grad = jnp.einsum("hij,ihd->jd", score_wide, query_heads).astype(jnp.bfloat16)
    stacked = jnp.concatenate([query_grad, key_grad, val_grad], axis=1)
    return (stacked, attended)


def weight_rows(hidden_rows, cot_rows, stacked, attended, first_row, row_count):
    hidden_cols = lax.dynamic_slice_in_dim(hidden_rows, first_row, row_count, 1)
    cot_cols = lax.dynamic_slice_in_dim(cot_rows, first_row, row_count, 1)
    proj_grad = jnp.dot(hidden_cols.T, stacked, preferred_element_type=jnp.float32)
    out_grad = jnp.dot(cot_cols.T, attended, preferred_element_type=jnp.float32)
    return jnp.concatenate([proj_grad, out_grad], axis=1)


def generic_device(
    layer_inputs,
    loss_adjoint_matrix,
    attention_projection_matrix,
    merge_projection_transposed,
    packed_sequence_labels,
    dropout_factors,
    straggler_filter,
):
    duplicate_workers = lax.axis_size("rep")
    member = lax.axis_index("rep")
    kept_worker = jnp.sum(jnp.arange(duplicate_workers, dtype=jnp.int32) * straggler_filter[:, 0])
    row_count = layer_inputs.shape[1] // duplicate_workers
    first_row = member * row_count
    qkv_full, out_full = (
        lax.all_gather(attention_projection_matrix, ("rep", "grp"), axis=0, tiled=True),
        lax.all_gather(merge_projection_transposed, ("rep", "grp"), axis=0, tiled=True),
    )
    projected_wide = jnp.dot(layer_inputs, qkv_full, preferred_element_type=jnp.float32)
    attn_wide = jnp.dot(loss_adjoint_matrix, out_full, preferred_element_type=jnp.float32)
    chosen_noise = from_root(dropout_factors[0], "rep", kept_worker)
    stacked, attended = token_grads(
        projected_wide, attn_wide, packed_sequence_labels[0], chosen_noise
    )
    gradient = weight_rows(
        layer_inputs, loss_adjoint_matrix, stacked, attended, first_row, row_count
    )
    return lax.psum_scatter(gradient, "grp", scatter_dimension=0, tiled=True)


def dot(a, b, dims):
    return lax.dot_general(a, b, (dims, ((), ())), preferred_element_type=jnp.float32)


VMEM = pl.BlockSpec(memory_space=pltpu.VMEM)
SMEM = pl.BlockSpec(memory_space=pltpu.SMEM)


def room(mebibytes):
    return pltpu.CompilerParams(vmem_limit_bytes=mebibytes << 20)


def cost(flops, count):
    return pl.CostEstimate(flops=flops, bytes_accessed=count, transcendentals=0)


def flip_kernel(order_ref, x_ref, keep_ref, send_ref, flipped):
    half = keep_ref.shape[0]
    blocks = order_ref.shape[0]
    rows = 2 * half // blocks
    width = x_ref.shape[1]
    for first in range(0, width, 256):
        flipped[pl.ds(first, 256), :] = x_ref[:, pl.ds(first, 256)].T
    for block in range(blocks):
        first = pl.multiple_of(order_ref[block] * rows, 16)
        target = keep_ref if block < blocks // 2 else send_ref
        place = (block % (blocks // 2)) * rows
        target[pl.ds(place, rows), :] = flipped[pl.ds(first, rows), :]


def flip(order, x):
    tokens, width = x.shape
    out = jax.ShapeDtypeStruct((width // 2, tokens), x.dtype)
    return pl.pallas_call(
        flip_kernel,
        out_shape=(out, out),
        in_specs=[SMEM, VMEM],
        out_specs=(VMEM, VMEM),
        scratch_shapes=[pltpu.VMEM((width, tokens), x.dtype)],
        cost_estimate=cost(0, 4 * x.size),
        compiler_params=room(10),
        name="flip",
    )(order, x)


def stack_kernel(runs, *refs):
    sources, out_ref, sems = refs[:-2], refs[-2], refs[-1]
    copies = []
    place = 0
    for n, (source, first, rows) in enumerate(runs):
        copies.append(
            pltpu.make_async_copy(
                sources[source].at[pl.ds(first, rows), :],
                out_ref.at[pl.ds(place, rows), :],
                sems.at[n],
            )
        )
        place += rows
    for copy in copies:
        copy.start()
    for copy in copies:
        copy.wait()


def stack(pieces, runs=None):
    runs = runs or [(n, 0, p.shape[0]) for n, p in enumerate(pieces)]
    shape = (sum(rows for _, _, rows in runs), pieces[0].shape[1])
    return pl.pallas_call(
        functools.partial(stack_kernel, runs),
        out_shape=jax.ShapeDtypeStruct(shape, pieces[0].dtype),
        in_specs=[pl.BlockSpec(memory_space=pl.ANY)] * len(pieces),
        out_specs=VMEM,
        scratch_shapes=[pltpu.SemaphoreType.DMA((len(runs),))],
        cost_estimate=cost(0, 4 * shape[0] * shape[1]),
        compiler_params=room(4),
        name="stack",
    )(*pieces)


def one_on_other(a, b):
    zero = jnp.zeros((), a.dtype)
    above = lax.pad(a, zero, ((0, b.shape[0], 0), (0, 0, 0)))
    return above + lax.pad(b, zero, ((a.shape[0], 0, 0), (0, 0, 0)))


def forward_kernel(
    heads, member_ref, own_ref, other_ref, pair_ref, row_ref, column_ref, noise_ref,
    att_ref, probs_ref, parts_ref,
):
    tokens = own_ref.shape[0]
    size = pair_ref.shape[1]
    scale = 1.0 / math.sqrt(size)
    low = jnp.bfloat16

    def part(first):
        return (own_ref[:, pl.ds(first, size)] + other_ref[:, pl.ds(first, size)]).astype(low)

    first_member = member_ref[0] == 0
    mine = part(heads * size).astype(jnp.float32)
    pair = pair_ref[...].astype(jnp.float32)
    keys = jnp.where(first_member, mine, pair).astype(low)
    vals = jnp.where(first_member, pair, mine).astype(low)
    parts_ref[heads] = keys
    parts_ref[heads + 1] = vals
    query_at = lax.broadcasted_iota(jnp.int32, (tokens, tokens), 0)
    key_at = lax.broadcasted_iota(jnp.int32, (tokens, tokens), 1)
    allowed = (column_ref[...] == row_ref[...]) & (key_at <= query_at)
    for head in range(heads):
        query = part(head * size)
        parts_ref[head] = query
        scores = dot(query, keys, ((1,), (1,))) * scale
        scores = jnp.where(allowed, scores, -jnp.inf)
        expon = jnp.exp(scores - jnp.max(scores, axis=1, keepdims=True))
        probs = expon / jnp.sum(expon, axis=1, keepdims=True)
        probs_ref[head] = probs
        dropped = (probs * (1.0 + noise_ref[head].astype(jnp.float32))).astype(low)
        att_ref[:, pl.ds(head * size, size)] = dot(dropped, vals, ((1,), (0,))).astype(low)


def forward(member, own, other, pair, labels, noise):
    tokens, size = pair.shape
    heads = noise.shape[0]
    return pl.pallas_call(
        functools.partial(forward_kernel, heads),
        out_shape=(
            jax.ShapeDtypeStruct((tokens, heads * size), jnp.bfloat16),
            jax.ShapeDtypeStruct(noise.shape, jnp.float32),
            jax.ShapeDtypeStruct((heads + 2, tokens, size), jnp.bfloat16),
        ),
        in_specs=[SMEM] + [VMEM] * 6,
        out_specs=(VMEM,) * 3,
        cost_estimate=cost(4 * noise.size * size, 8 * own.size + 6 * noise.size),
        compiler_params=room(10),
        name="forward",
    )(member, own, other, pair, labels, labels.reshape(tokens, 1), noise)


def backward_kernel(
    heads, member_ref, own_ref, other_ref, probs_ref, parts_ref, noise_ref, query_ref, keep_ref, send_ref
):
    tokens, size = keep_ref.shape
    scale = 1.0 / math.sqrt(size)
    low = jnp.bfloat16
    first_member = member_ref[0] == 0
    keys, vals = parts_ref[heads], parts_ref[heads + 1]
    key_grad = jnp.zeros((tokens, size), jnp.float32)
    val_grad = jnp.zeros((tokens, size), jnp.float32)
    for head in range(heads):
        here = pl.ds(head * size, size)
        query, grad = parts_ref[head], (own_ref[:, here] + other_ref[:, here]).astype(low)
        probs = probs_ref[head]
        factor = 1.0 + noise_ref[head].astype(jnp.float32)
        dropped = (probs * factor).astype(low)
        val_grad += dot(dropped, grad, ((0,), (0,)))
        prob_grad = dot(grad, vals, ((1,), (1,))) * factor
        inner = jnp.sum(probs * prob_grad, axis=1, keepdims=True)
        score_grad = (probs * (prob_grad - inner) * scale).astype(low)
        query_ref[:, here] = dot(score_grad, keys, ((1,), (0,))).astype(low)
        key_grad += dot(score_grad, query, ((0,), (0,)))
    keep_ref[...] = jnp.where(first_member, key_grad, val_grad)
    send_ref[...] = jnp.where(first_member, val_grad, key_grad)


def backward(member, own, other, probs, parts, noise):
    heads, tokens, _ = noise.shape
    size = parts.shape[2]
    narrow = jax.ShapeDtypeStruct((tokens, size), jnp.float32)
    return pl.pallas_call(
        functools.partial(backward_kernel, heads),
        out_shape=(jax.ShapeDtypeStruct((tokens, heads * size), jnp.bfloat16), narrow, narrow),
        in_specs=[SMEM] + [VMEM] * 5,
        out_specs=(VMEM,) * 3,
        cost_estimate=cost(8 * noise.size * size, 6 * noise.size),
        compiler_params=room(10),
        name="backward",
    )(member, own, other, probs, parts, noise)


def place_kernel(member_ref, *refs):
    sources, out_ref = refs[:-1], refs[-1]

    def put(order):
        first = 0
        for pair in range(0, len(sources), 2):
            for n in order:
                source = sources[pair + n]
                out_ref[:, pl.ds(first, source.shape[1])] = source[pl.ds(0, out_ref.shape[0]), :].astype(
                    out_ref.dtype
                )
                first += source.shape[1]

    @pl.when(member_ref[0] == 0)
    def _():
        put((0, 1))

    @pl.when(member_ref[0] != 0)
    def _():
        put((1, 0))


def place_columns(member, *pieces):
    shape = (pieces[1].shape[0], sum(p.shape[1] for p in pieces))
    return pl.pallas_call(
        place_kernel,
        out_shape=jax.ShapeDtypeStruct(shape, pieces[0].dtype),
        in_specs=[SMEM] + [VMEM] * len(pieces),
        out_specs=VMEM,
        cost_estimate=cost(0, 8 * shape[0] * shape[1]),
        compiler_params=room(4),
        name="place",
    )(member, *pieces)


def paired_device(
    layer_inputs,
    loss_adjoint_matrix,
    attention_projection_matrix,
    merge_projection_transposed,
    packed_sequence_labels,
    dropout_factors,
    straggler_filter,
):
    grp = lax.axis_size("grp")
    member = lax.axis_index("rep")
    me = member * grp + lax.axis_index("grp")
    first = member == 0
    core, side, near, far = 1, 2, 4, 8

    def across(a, bit):
        return lax.ppermute(a, "grp", [(g, g ^ bit) for g in range(grp)])

    def across_rep(a):
        return lax.ppermute(a, "rep", [(0, 1), (1, 0)])

    heads = dropout_factors.shape[2]
    share = heads // 2
    width = merge_projection_transposed.shape[1]
    size = width // heads
    part = share * size

    def columns(a, first, count, m):
        return lax.dynamic_slice_in_dim(a, first + m * count, count, 1)

    def qkv_columns(m):
        queries = columns(attention_projection_matrix, 0, part, m)
        return jnp.concatenate(
            [queries, columns(attention_projection_matrix, width, size, m)], axis=1
        )

    def merge_columns(m):
        return columns(merge_projection_transposed, 0, part, m)

    def exchanged(pick):
        return one_on_other(pick(member), across_rep(pick(1 - member)))

    qkv = exchanged(qkv_columns)
    merge = exchanged(merge_columns)

    qkv_near, qkv_far = across(qkv, near), across(qkv, far)
    qkv_both = across(qkv_far, near)
    qkv_side = [
        across(qkv, side), across(qkv_far, side), across(qkv_near, side), across(qkv_both, side)
    ]
    merge_far = across(merge, far)
    merge_line = one_on_other(merge, merge_far)
    merge_near = across(merge_line, near)
    merge_pieces = [merge_line, merge_near, across(merge_line, side), across(merge_near, side)]

    def order(bits):
        found = [0]
        for bit in (core, *bits, grp):
            found = [at | b for at in found for b in (0, bit)]
        return jnp.array(found, jnp.int32) ^ me

    stages = ((near, side, far), (side, far, near))
    x_keep, x_send = flip(order(stages[0]), layer_inputs)
    y_keep, y_send = flip(order(stages[1]), loss_adjoint_matrix)
    x_other, y_other = across(x_send, core), across(y_send, core)

    def as_it_lies(a):
        return with_layout_constraint(a, Layout(major_to_minor=tuple(range(a.ndim))))

    noise = as_it_lies(across_rep(dropout_factors))

    def project(rows, weights):
        return dot(rows, weights, ((0,), (0,)))

    pieces = [qkv, qkv_far, *qkv_side[:2], qkv_near, qkv_both, qkv_side[2]]
    early = stack(pieces)
    cut = early.shape[0]
    away = project(x_other[:cut], early)
    qkv_in = across(away + project(x_other[cut:], qkv_side[3]), core)
    own = project(x_keep[:cut], early)
    qkv_own = own + project(x_keep[cut:], qkv_side[3])
    rows = merge.shape[0]
    merge_rows = stack(
        merge_pieces,
        [(s + n, f, rows) for s in (0, 2) for f in (0, rows) for n in (0, 1)],
    )
    merge_in = across(project(y_other, merge_rows), core)
    merge_own = project(y_keep, merge_rows)

    pair = (qkv_own[:, part:] + qkv_in[:, part:]).astype(jnp.bfloat16)
    pair, noise, labels, straggler_filter = lax.optimization_barrier(
        (pair, noise, packed_sequence_labels, straggler_filter)
    )
    pair = across_rep(pair)
    kept_worker = jnp.sum(jnp.arange(2, dtype=jnp.int32) * straggler_filter[:, 0])
    noise = jnp.where(kept_worker == member, dropout_factors, noise)[0]
    noise = jnp.where(first, noise[:, :share], noise[:, share:])
    noise_used = jnp.transpose(noise, (1, 0, 2))
    member = member.reshape(1)
    att, probs, pieces = forward(member, qkv_own, qkv_in, pair, labels, noise_used)
    query_grad, pair_keep, pair_send = backward(
        member, merge_own, merge_in, probs, pieces, noise_used
    )
    pair_grad = (pair_keep + across_rep(pair_send)).astype(jnp.bfloat16)

    def first_two_exchanged(rows):
        halves = rows.reshape(2, 2, rows.shape[0] // 4, rows.shape[1])
        return jnp.swapaxes(halves, 0, 1).reshape(rows.shape)

    def reduced(keep, other, bits, grad, theirs):
        cut = keep.shape[0] // 2

        def half(rows):
            return dot(keep[rows], grad, ((1,), (0,))), other[rows]

        leaves, rows = half(slice(cut, None))
        leaves = (leaves + dot(rows, theirs, ((1,), (0,)))).astype(jnp.bfloat16)
        total, rows = half(slice(None, cut))
        for n, bit in enumerate(bits):
            arrived = across(leaves, bit)
            if n == 0:
                total = total + dot(rows, theirs, ((1,), (0,)))
            total = total + arrived.astype(jnp.float32)
            cut = total.shape[0] // 2
            whole = total
            leaves, total = total[cut:].astype(jnp.bfloat16), total[:cut]
        return whole, across_rep(leaves)

    merge = reduced(y_keep, y_other, stages[1], att, across(att, core))
    query = reduced(x_keep, x_other, stages[0], query_grad, across(query_grad, core))
    x_keep, x_other = first_two_exchanged(x_keep), first_two_exchanged(x_other)
    pair = reduced(x_keep, x_other, (side, near, far), pair_grad, across(pair_grad, core))
    return place_columns(member, *query, *pair, *merge)


def paired(mesh, shapes):
    rep, grp = mesh.shape["rep"], mesh.shape["grp"]
    depth, heads, tokens = shapes[0][1], shapes[5][2], shapes[5][3]
    size = shapes[3][1] // heads
    even = depth % (rep * grp * 16) == 0 and depth % 256 == 0
    return rep == 2 and grp == 16 and even and heads % 2 == 0 and size % 128 == 0 and tokens % 128 == 0


def solution(mesh):
    placed = (
        P("grp", None),
        P("grp", None),
        P(("rep", "grp"), None),
        P(("rep", "grp"), None),
        P("grp", None),
        P("rep", "grp", None, None),
        P(None, "grp"),
    )

    def on_devices(body):
        return jax.shard_map(
            body, mesh=mesh, in_specs=placed, out_specs=P(("rep", "grp"), None), check_vma=False
        )

    def step(*args):
        if not paired(mesh, [a.shape for a in args]):
            return on_devices(generic_device)(*args)
        return on_devices(paired_device)(*args)

    return step
```

```python
import functools
import math

import jax
import jax.numpy as jnp
from jax import lax
from jax.experimental import pallas as pl
from jax.experimental.layout import Layout, with_layout_constraint
from jax.experimental.pallas import tpu as pltpu
from jax.sharding import PartitionSpec as P


def from_root(block, axis, holder):
    block = jnp.where(lax.axis_index(axis) == holder, block, jnp.zeros_like(block))
    return lax.psum(block, axis)


def token_grads(projected_wide, attn_wide, doc_row, noise_rows):
    seq_len = projected_wide.shape[0]
    head_size = (projected_wide.shape[1] - attn_wide.shape[1]) // 2
    heads = attn_wide.shape[1] // head_size
    score_scale = 1.0 / jnp.sqrt(jnp.float32(head_size))
    projected = projected_wide.astype(jnp.bfloat16)
    queries = projected[:, : heads * head_size]
    key_rows = projected[:, heads * head_size : (heads + 1) * head_size]
    val_rows = projected[:, (heads + 1) * head_size :]
    query_heads = queries.reshape(seq_len, heads, head_size).astype(jnp.float32)
    keys_wide = key_rows.astype(jnp.float32)
    vals_wide = val_rows.astype(jnp.float32)
    position = jnp.arange(seq_len, dtype=jnp.int32)
    allowed = (doc_row[:, None] == doc_row[None, :]) & (position[None, :] <= position[:, None])
    scores = jnp.einsum("ihd,jd->hij", query_heads, keys_wide) * score_scale
    scores = jnp.where(allowed[None], scores, -jnp.inf)
    highest = jnp.max(scores, axis=2, keepdims=True)
    expon = jnp.exp(scores - highest)
    attn_probs = expon / jnp.sum(expon, axis=2, keepdims=True)
    factor = 1.0 + jnp.transpose(noise_rows.astype(jnp.float32), (1, 0, 2))
    dropped = (attn_probs * factor).astype(jnp.bfloat16)
    dropped_wide = dropped.astype(jnp.float32)
    attended = (
        jnp.einsum("hij,jd->ihd", dropped_wide, vals_wide)
        .astype(jnp.bfloat16)
        .reshape(seq_len, heads * head_size)
    )
    attn_grad = attn_wide.astype(jnp.bfloat16)
    grad_heads = attn_grad.reshape(seq_len, heads, head_size).astype(jnp.float32)
    val_grad = jnp.einsum("hij,ihd->jd", dropped_wide, grad_heads).astype(jnp.bfloat16)
    prob_grad = jnp.einsum("ihd,jd->hij", grad_heads, vals_wide) * factor
    inner = jnp.sum(attn_probs * prob_grad, axis=2, keepdims=True)
    score_grad = (attn_probs * (prob_grad - inner) * score_scale).astype(jnp.bfloat16)
    score_wide = score_grad.astype(jnp.float32)
    query_grad = (
        jnp.einsum("hij,jd->ihd", score_wide, keys_wide)
        .astype(jnp.bfloat16)
        .reshape(seq_len, heads * head_size)
    )
    key_grad = jnp.einsum("hij,ihd->jd", score_wide, query_heads).astype(jnp.bfloat16)
    stacked = jnp.concatenate([query_grad, key_grad, val_grad], axis=1)
    return (stacked, attended)


def weight_rows(hidden_rows, cot_rows, stacked, attended, first_row, row_count):
    hidden_cols = lax.dynamic_slice_in_dim(hidden_rows, first_row, row_count, 1)
    cot_cols = lax.dynamic_slice_in_dim(cot_rows, first_row, row_count, 1)
    proj_grad = jnp.dot(hidden_cols.T, stacked, preferred_element_type=jnp.float32)
    out_grad = jnp.dot(cot_cols.T, attended, preferred_element_type=jnp.float32)
    return jnp.concatenate([proj_grad, out_grad], axis=1)


def generic_device(
    layer_inputs,
    loss_adjoint_matrix,
    attention_projection_matrix,
    merge_projection_transposed,
    packed_sequence_labels,
    dropout_factors,
    straggler_filter,
):
    duplicate_workers = lax.axis_size("rep")
    member = lax.axis_index("rep")
    kept_worker = jnp.sum(jnp.arange(duplicate_workers, dtype=jnp.int32) * straggler_filter[:, 0])
    row_count = layer_inputs.shape[1] // duplicate_workers
    first_row = member * row_count
    qkv_full, out_full = (
        lax.all_gather(attention_projection_matrix, ("rep", "grp"), axis=0, tiled=True),
        lax.all_gather(merge_projection_transposed, ("rep", "grp"), axis=0, tiled=True),
    )
    projected_wide = jnp.dot(layer_inputs, qkv_full, preferred_element_type=jnp.float32)
    attn_wide = jnp.dot(loss_adjoint_matrix, out_full, preferred_element_type=jnp.float32)
    chosen_noise = from_root(dropout_factors[0], "rep", kept_worker)
    stacked, attended = token_grads(
        projected_wide, attn_wide, packed_sequence_labels[0], chosen_noise
    )
    gradient = weight_rows(
        layer_inputs, loss_adjoint_matrix, stacked, attended, first_row, row_count
    )
    return lax.psum_scatter(gradient, "grp", scatter_dimension=0, tiled=True)


def dot(a, b, dims):
    return lax.dot_general(a, b, (dims, ((), ())), preferred_element_type=jnp.float32)


VMEM = pl.BlockSpec(memory_space=pltpu.VMEM)
SMEM = pl.BlockSpec(memory_space=pltpu.SMEM)


def room(mebibytes):
    return pltpu.CompilerParams(vmem_limit_bytes=mebibytes << 20)


def cost(flops, count):
    return pl.CostEstimate(flops=flops, bytes_accessed=count, transcendentals=0)


def flip_kernel(order_ref, x_ref, keep_ref, send_ref, flipped):
    half = keep_ref.shape[0]
    blocks = order_ref.shape[0]
    rows = 2 * half // blocks
    width = x_ref.shape[1]
    for first in range(0, width, 256):
        flipped[pl.ds(first, 256), :] = x_ref[:, pl.ds(first, 256)].T
    for block in range(blocks):
        first = pl.multiple_of(order_ref[block] * rows, 16)
        target = keep_ref if block < blocks // 2 else send_ref
        place = (block % (blocks // 2)) * rows
        target[pl.ds(place, rows), :] = flipped[pl.ds(first, rows), :]


def flip(order, x):
    tokens, width = x.shape
    out = jax.ShapeDtypeStruct((width // 2, tokens), x.dtype)
    return pl.pallas_call(
        flip_kernel,
        out_shape=(out, out),
        in_specs=[SMEM, VMEM],
        out_specs=(VMEM, VMEM),
        scratch_shapes=[pltpu.VMEM((width, tokens), x.dtype)],
        cost_estimate=cost(0, 4 * x.size),
        compiler_params=room(10),
        name="flip",
    )(order, x)


def stack_kernel(*refs):
    sources, out_ref, sems = refs[:-2], refs[-2], refs[-1]
    copies = []
    first = 0
    for n, source in enumerate(sources):
        rows = source.shape[0]
        copies.append(pltpu.make_async_copy(source, out_ref.at[pl.ds(first, rows), :], sems.at[n]))
        first += rows
    for copy in copies:
        copy.start()
    for copy in copies:
        copy.wait()


def stack(pieces):
    shape = (sum(p.shape[0] for p in pieces), pieces[0].shape[1])
    return pl.pallas_call(
        stack_kernel,
        out_shape=jax.ShapeDtypeStruct(shape, pieces[0].dtype),
        in_specs=[pl.BlockSpec(memory_space=pl.ANY)] * len(pieces),
        out_specs=VMEM,
        scratch_shapes=[pltpu.SemaphoreType.DMA((len(pieces),))],
        cost_estimate=cost(0, 4 * shape[0] * shape[1]),
        compiler_params=room(4),
        name="stack",
    )(*pieces)


def one_on_other(a, b):
    zero = jnp.zeros((), a.dtype)
    above = lax.pad(a, zero, ((0, b.shape[0], 0), (0, 0, 0)))
    return above + lax.pad(b, zero, ((a.shape[0], 0, 0), (0, 0, 0)))


def forward_kernel(
    heads, member_ref, own_ref, other_ref, pair_ref, row_ref, column_ref, noise_ref,
    att_ref, probs_ref, parts_ref,
):
    tokens = own_ref.shape[0]
    size = pair_ref.shape[1]
    scale = 1.0 / math.sqrt(size)
    low = jnp.bfloat16

    def part(first):
        return (own_ref[:, pl.ds(first, size)] + other_ref[:, pl.ds(first, size)]).astype(low)

    first_member = member_ref[0] == 0
    mine = part(heads * size).astype(jnp.float32)
    pair = pair_ref[...].astype(jnp.float32)
    keys = jnp.where(first_member, mine, pair).astype(low)
    vals = jnp.where(first_member, pair, mine).astype(low)
    parts_ref[heads] = keys
    parts_ref[heads + 1] = vals
    query_at = lax.broadcasted_iota(jnp.int32, (tokens, tokens), 0)
    key_at = lax.broadcasted_iota(jnp.int32, (tokens, tokens), 1)
    allowed = (column_ref[...] == row_ref[...]) & (key_at <= query_at)
    for head in range(heads):
        query = part(head * size)
        parts_ref[head] = query
        scores = dot(query, keys, ((1,), (1,))) * scale
        scores = jnp.where(allowed, scores, -jnp.inf)
        expon = jnp.exp(scores - jnp.max(scores, axis=1, keepdims=True))
        probs = expon / jnp.sum(expon, axis=1, keepdims=True)
        probs_ref[head] = probs
        dropped = (probs * (1.0 + noise_ref[head].astype(jnp.float32))).astype(low)
        att_ref[:, pl.ds(head * size, size)] = dot(dropped, vals, ((1,), (0,))).astype(low)


def forward(member, own, other, pair, labels, noise):
    tokens, size = pair.shape
    heads = noise.shape[0]
    return pl.pallas_call(
        functools.partial(forward_kernel, heads),
        out_shape=(
            jax.ShapeDtypeStruct((tokens, heads * size), jnp.bfloat16),
            jax.ShapeDtypeStruct(noise.shape, jnp.float32),
            jax.ShapeDtypeStruct((heads + 2, tokens, size), jnp.bfloat16),
        ),
        in_specs=[SMEM] + [VMEM] * 6,
        out_specs=(VMEM,) * 3,
        cost_estimate=cost(4 * noise.size * size, 8 * own.size + 6 * noise.size),
        compiler_params=room(10),
        name="forward",
    )(member, own, other, pair, labels, labels.reshape(tokens, 1), noise)


def backward_kernel(
    heads, member_ref, own_ref, other_ref, probs_ref, parts_ref, noise_ref, query_ref, keep_ref, send_ref
):
    tokens, size = keep_ref.shape
    scale = 1.0 / math.sqrt(size)
    low = jnp.bfloat16
    first_member = member_ref[0] == 0
    keys, vals = parts_ref[heads], parts_ref[heads + 1]
    key_grad = jnp.zeros((tokens, size), jnp.float32)
    val_grad = jnp.zeros((tokens, size), jnp.float32)
    for head in range(heads):
        here = pl.ds(head * size, size)
        query, grad = parts_ref[head], (own_ref[:, here] + other_ref[:, here]).astype(low)
        probs = probs_ref[head]
        factor = 1.0 + noise_ref[head].astype(jnp.float32)
        dropped = (probs * factor).astype(low)
        val_grad += dot(dropped, grad, ((0,), (0,)))
        prob_grad = dot(grad, vals, ((1,), (1,))) * factor
        inner = jnp.sum(probs * prob_grad, axis=1, keepdims=True)
        score_grad = (probs * (prob_grad - inner) * scale).astype(low)
        query_ref[:, here] = dot(score_grad, keys, ((1,), (0,))).astype(low)
        key_grad += dot(score_grad, query, ((0,), (0,)))
    keep_ref[...] = jnp.where(first_member, key_grad, val_grad)
    send_ref[...] = jnp.where(first_member, val_grad, key_grad)


def backward(member, own, other, probs, parts, noise):
    heads, tokens, _ = noise.shape
    size = parts.shape[2]
    narrow = jax.ShapeDtypeStruct((tokens, size), jnp.float32)
    return pl.pallas_call(
        functools.partial(backward_kernel, heads),
        out_shape=(jax.ShapeDtypeStruct((tokens, heads * size), jnp.bfloat16), narrow, narrow),
        in_specs=[SMEM] + [VMEM] * 5,
        out_specs=(VMEM,) * 3,
        cost_estimate=cost(8 * noise.size * size, 6 * noise.size),
        compiler_params=room(10),
        name="backward",
    )(member, own, other, probs, parts, noise)


def place_kernel(groups, member_ref, *refs):
    sources, out_ref = refs[:-1], refs[-1]

    def put(order):
        first = 0
        for group in groups:
            for n in order:
                for pair in group:
                    source = sources[2 * pair + n]
                    out_ref[:, pl.ds(first, source.shape[1])] = source[
                        pl.ds(0, out_ref.shape[0]), :
                    ].astype(out_ref.dtype)
                    first += source.shape[1]

    @pl.when(member_ref[0] == 0)
    def _():
        put((0, 1))

    @pl.when(member_ref[0] != 0)
    def _():
        put((1, 0))


def place_columns(member, *groups):
    pairs = [pair for group in groups for pair in group]
    pieces = [piece for pair in pairs for piece in pair]
    numbers = iter(range(len(pairs)))
    numbered = [[next(numbers) for _ in group] for group in groups]
    shape = (pieces[1].shape[0], sum(p.shape[1] for p in pieces))
    return pl.pallas_call(
        functools.partial(place_kernel, numbered),
        out_shape=jax.ShapeDtypeStruct(shape, pieces[0].dtype),
        in_specs=[SMEM] + [VMEM] * len(pieces),
        out_specs=VMEM,
        cost_estimate=cost(0, 8 * shape[0] * shape[1]),
        compiler_params=room(4),
        name="place",
    )(member, *pieces)


def paired_device(
    layer_inputs,
    loss_adjoint_matrix,
    attention_projection_matrix,
    merge_projection_transposed,
    packed_sequence_labels,
    dropout_factors,
    straggler_filter,
):
    grp = lax.axis_size("grp")
    member = lax.axis_index("rep")
    me = member * grp + lax.axis_index("grp")
    first = member == 0
    core, side, near, far = 1, 2, 4, 8

    def across(a, bit):
        return lax.ppermute(a, "grp", [(g, g ^ bit) for g in range(grp)])

    def across_rep(a):
        return lax.ppermute(a, "rep", [(0, 1), (1, 0)])

    heads = dropout_factors.shape[2]
    share = heads // 2
    width = merge_projection_transposed.shape[1]
    size = width // heads
    part = share * size

    def columns(a, first, count, m):
        return lax.dynamic_slice_in_dim(a, first + m * count, count, 1)

    def qkv_columns(m):
        queries = columns(attention_projection_matrix, 0, part, m)
        return jnp.concatenate(
            [queries, columns(attention_projection_matrix, width, size, m)], axis=1
        )

    def merge_columns(m):
        return columns(merge_projection_transposed, 0, part, m)

    def exchanged(pick):
        return one_on_other(pick(member), across_rep(pick(1 - member)))

    qkv = exchanged(qkv_columns)
    merge = exchanged(merge_columns)

    qkv_near, qkv_far = across(qkv, near), across(qkv, far)
    qkv_both = across(qkv_far, near)
    qkv_side = [
        across(qkv, side), across(qkv_far, side), across(qkv_near, side), across(qkv_both, side)
    ]
    merge_far = across(merge, far)
    merge_line = one_on_other(merge, merge_far)
    merge_near = across(merge_line, near)
    merge_pieces = [merge_line, merge_near, across(merge_line, side), across(merge_near, side)]

    def order(bits):
        found = [0]
        for bit in (core, *bits, grp):
            found = [at | b for at in found for b in (0, bit)]
        return jnp.array(found, jnp.int32) ^ me

    stages = ((near, side, far), (side, near, far))
    x_keep, x_send = flip(order(stages[0]), layer_inputs)
    y_keep, y_send = flip(order(stages[1]), loss_adjoint_matrix)
    x_other, y_other = across(x_send, core), across(y_send, core)

    def as_it_lies(a):
        return with_layout_constraint(a, Layout(major_to_minor=tuple(range(a.ndim))))

    noise = as_it_lies(across_rep(dropout_factors))

    def project(rows, weights):
        return dot(rows, weights, ((0,), (0,)))

    pieces = [qkv, qkv_far, *qkv_side[:2], qkv_near, qkv_both, qkv_side[2]]
    early = stack(pieces)
    cut = early.shape[0]
    away = project(x_other[:cut], early)
    qkv_in = across(away + project(x_other[cut:], qkv_side[3]), core)
    own = project(x_keep[:cut], early)
    qkv_own = own + project(x_keep[cut:], qkv_side[3])
    merge_rows = stack(merge_pieces)
    merge_in = across(project(y_other, merge_rows), core)
    merge_own = project(y_keep, merge_rows)

    pair = (qkv_own[:, part:] + qkv_in[:, part:]).astype(jnp.bfloat16)
    pair, noise, labels, straggler_filter = lax.optimization_barrier(
        (pair, noise, packed_sequence_labels, straggler_filter)
    )
    pair = across_rep(pair)
    kept_worker = jnp.sum(jnp.arange(2, dtype=jnp.int32) * straggler_filter[:, 0])
    noise = jnp.where(kept_worker == member, dropout_factors, noise)[0]
    noise = jnp.where(first, noise[:, :share], noise[:, share:])
    noise_used = jnp.transpose(noise, (1, 0, 2))
    member = member.reshape(1)
    att, probs, pieces = forward(member, qkv_own, qkv_in, pair, labels, noise_used)
    query_grad, pair_keep, pair_send = backward(
        member, merge_own, merge_in, probs, pieces, noise_used
    )
    pair_grad = (pair_keep + across_rep(pair_send)).astype(jnp.bfloat16)

    def first_two_exchanged(rows):
        halves = rows.reshape(2, 2, rows.shape[0] // 4, rows.shape[1])
        return jnp.swapaxes(halves, 0, 1).reshape(rows.shape)

    def reduced(keep, other, bits, grad, theirs):
        cut = keep.shape[0] // 2

        def half(rows):
            return dot(keep[rows], grad, ((1,), (0,))), other[rows]

        leaves, rows = half(slice(cut, None))
        leaves = (leaves + dot(rows, theirs, ((1,), (0,)))).astype(jnp.bfloat16)
        total, rows = half(slice(None, cut))
        for n, bit in enumerate(bits):
            arrived = across(leaves, bit)
            if n == 0:
                total = total + dot(rows, theirs, ((1,), (0,)))
            total = total + arrived.astype(jnp.float32)
            cut = total.shape[0] // 2
            whole = total
            leaves, total = total[cut:].astype(jnp.bfloat16), total[:cut]
        return whole, across_rep(leaves)

    merge = reduced(y_keep, y_other, stages[1], att, across(att, core))
    theirs = across(query_grad, core)
    query = []
    for n in range(2):
        here = slice(n * part // 2, (n + 1) * part // 2)
        query.append(reduced(x_keep, x_other, stages[0], query_grad[:, here], theirs[:, here]))
    x_keep, x_other = first_two_exchanged(x_keep), first_two_exchanged(x_other)
    pair = reduced(x_keep, x_other, (side, near, far), pair_grad, across(pair_grad, core))
    return place_columns(member, query, [pair], [merge])


def paired(mesh, shapes):
    rep, grp = mesh.shape["rep"], mesh.shape["grp"]
    depth, heads, tokens = shapes[0][1], shapes[5][2], shapes[5][3]
    size = shapes[3][1] // heads
    even = depth % (rep * grp * 16) == 0 and depth % 256 == 0
    return rep == 2 and grp == 16 and even and heads % 2 == 0 and size % 128 == 0 and tokens % 128 == 0


def solution(mesh):
    placed = (
        P("grp", None),
        P("grp", None),
        P(("rep", "grp"), None),
        P(("rep", "grp"), None),
        P("grp", None),
        P("rep", "grp", None, None),
        P(None, "grp"),
    )

    def on_devices(body):
        return jax.shard_map(
            body, mesh=mesh, in_specs=placed, out_specs=P(("rep", "grp"), None), check_vma=False
        )

    def step(*args):
        if not paired(mesh, [a.shape for a in args]):
            return on_devices(generic_device)(*args)
        return on_devices(paired_device)(*args)

    return step
```

```python
import functools
import math

import jax
import jax.numpy as jnp
from jax import lax
from jax.experimental import pallas as pl
from jax.experimental.layout import Layout, with_layout_constraint
from jax.experimental.pallas import tpu as pltpu
from jax.sharding import PartitionSpec as P


def from_root(block, axis, holder):
    block = jnp.where(lax.axis_index(axis) == holder, block, jnp.zeros_like(block))
    return lax.psum(block, axis)


def token_grads(projected_wide, attn_wide, doc_row, noise_rows):
    seq_len = projected_wide.shape[0]
    head_size = (projected_wide.shape[1] - attn_wide.shape[1]) // 2
    heads = attn_wide.shape[1] // head_size
    score_scale = 1.0 / jnp.sqrt(jnp.float32(head_size))
    projected = projected_wide.astype(jnp.bfloat16)
    queries = projected[:, : heads * head_size]
    key_rows = projected[:, heads * head_size : (heads + 1) * head_size]
    val_rows = projected[:, (heads + 1) * head_size :]
    query_heads = queries.reshape(seq_len, heads, head_size).astype(jnp.float32)
    keys_wide = key_rows.astype(jnp.float32)
    vals_wide = val_rows.astype(jnp.float32)
    position = jnp.arange(seq_len, dtype=jnp.int32)
    allowed = (doc_row[:, None] == doc_row[None, :]) & (position[None, :] <= position[:, None])
    scores = jnp.einsum("ihd,jd->hij", query_heads, keys_wide) * score_scale
    scores = jnp.where(allowed[None], scores, -jnp.inf)
    highest = jnp.max(scores, axis=2, keepdims=True)
    expon = jnp.exp(scores - highest)
    attn_probs = expon / jnp.sum(expon, axis=2, keepdims=True)
    factor = 1.0 + jnp.transpose(noise_rows.astype(jnp.float32), (1, 0, 2))
    dropped = (attn_probs * factor).astype(jnp.bfloat16)
    dropped_wide = dropped.astype(jnp.float32)
    attended = (
        jnp.einsum("hij,jd->ihd", dropped_wide, vals_wide)
        .astype(jnp.bfloat16)
        .reshape(seq_len, heads * head_size)
    )
    attn_grad = attn_wide.astype(jnp.bfloat16)
    grad_heads = attn_grad.reshape(seq_len, heads, head_size).astype(jnp.float32)
    val_grad = jnp.einsum("hij,ihd->jd", dropped_wide, grad_heads).astype(jnp.bfloat16)
    prob_grad = jnp.einsum("ihd,jd->hij", grad_heads, vals_wide) * factor
    inner = jnp.sum(attn_probs * prob_grad, axis=2, keepdims=True)
    score_grad = (attn_probs * (prob_grad - inner) * score_scale).astype(jnp.bfloat16)
    score_wide = score_grad.astype(jnp.float32)
    query_grad = (
        jnp.einsum("hij,jd->ihd", score_wide, keys_wide)
        .astype(jnp.bfloat16)
        .reshape(seq_len, heads * head_size)
    )
    key_grad = jnp.einsum("hij,ihd->jd", score_wide, query_heads).astype(jnp.bfloat16)
    stacked = jnp.concatenate([query_grad, key_grad, val_grad], axis=1)
    return (stacked, attended)


def weight_rows(hidden_rows, cot_rows, stacked, attended, first_row, row_count):
    hidden_cols = lax.dynamic_slice_in_dim(hidden_rows, first_row, row_count, 1)
    cot_cols = lax.dynamic_slice_in_dim(cot_rows, first_row, row_count, 1)
    proj_grad = jnp.dot(hidden_cols.T, stacked, preferred_element_type=jnp.float32)
    out_grad = jnp.dot(cot_cols.T, attended, preferred_element_type=jnp.float32)
    return jnp.concatenate([proj_grad, out_grad], axis=1)


def generic_device(
    layer_inputs,
    loss_adjoint_matrix,
    attention_projection_matrix,
    merge_projection_transposed,
    packed_sequence_labels,
    dropout_factors,
    straggler_filter,
):
    duplicate_workers = lax.axis_size("rep")
    member = lax.axis_index("rep")
    kept_worker = jnp.sum(jnp.arange(duplicate_workers, dtype=jnp.int32) * straggler_filter[:, 0])
    row_count = layer_inputs.shape[1] // duplicate_workers
    first_row = member * row_count
    qkv_full, out_full = (
        lax.all_gather(attention_projection_matrix, ("rep", "grp"), axis=0, tiled=True),
        lax.all_gather(merge_projection_transposed, ("rep", "grp"), axis=0, tiled=True),
    )
    projected_wide = jnp.dot(layer_inputs, qkv_full, preferred_element_type=jnp.float32)
    attn_wide = jnp.dot(loss_adjoint_matrix, out_full, preferred_element_type=jnp.float32)
    chosen_noise = from_root(dropout_factors[0], "rep", kept_worker)
    stacked, attended = token_grads(
        projected_wide, attn_wide, packed_sequence_labels[0], chosen_noise
    )
    gradient = weight_rows(
        layer_inputs, loss_adjoint_matrix, stacked, attended, first_row, row_count
    )
    return lax.psum_scatter(gradient, "grp", scatter_dimension=0, tiled=True)


def dot(a, b, dims):
    return lax.dot_general(a, b, (dims, ((), ())), preferred_element_type=jnp.float32)


VMEM = pl.BlockSpec(memory_space=pltpu.VMEM)
SMEM = pl.BlockSpec(memory_space=pltpu.SMEM)


def room(mebibytes):
    return pltpu.CompilerParams(vmem_limit_bytes=mebibytes << 20)


def cost(flops, count):
    return pl.CostEstimate(flops=flops, bytes_accessed=count, transcendentals=0)


def flip_kernel(order_ref, x_ref, keep_ref, send_ref, flipped):
    half = keep_ref.shape[0]
    blocks = order_ref.shape[0]
    rows = 2 * half // blocks
    width = x_ref.shape[1]
    for first in range(0, width, 256):
        flipped[pl.ds(first, 256), :] = x_ref[:, pl.ds(first, 256)].T
    for block in range(blocks):
        first = pl.multiple_of(order_ref[block] * rows, 16)
        target = keep_ref if block < blocks // 2 else send_ref
        place = (block % (blocks // 2)) * rows
        target[pl.ds(place, rows), :] = flipped[pl.ds(first, rows), :]


def flip(order, x):
    tokens, width = x.shape
    out = jax.ShapeDtypeStruct((width // 2, tokens), x.dtype)
    return pl.pallas_call(
        flip_kernel,
        out_shape=(out, out),
        in_specs=[SMEM, VMEM],
        out_specs=(VMEM, VMEM),
        scratch_shapes=[pltpu.VMEM((width, tokens), x.dtype)],
        cost_estimate=cost(0, 4 * x.size),
        compiler_params=room(10),
        name="flip",
    )(order, x)


def stack_kernel(*refs):
    sources, out_ref, sems = refs[:-2], refs[-2], refs[-1]
    copies = []
    first = 0
    for n, source in enumerate(sources):
        rows = source.shape[0]
        copies.append(pltpu.make_async_copy(source, out_ref.at[pl.ds(first, rows), :], sems.at[n]))
        first += rows
    for copy in copies:
        copy.start()
    for copy in copies:
        copy.wait()


def stack(pieces):
    shape = (sum(p.shape[0] for p in pieces), pieces[0].shape[1])
    return pl.pallas_call(
        stack_kernel,
        out_shape=jax.ShapeDtypeStruct(shape, pieces[0].dtype),
        in_specs=[pl.BlockSpec(memory_space=pl.ANY)] * len(pieces),
        out_specs=VMEM,
        scratch_shapes=[pltpu.SemaphoreType.DMA((len(pieces),))],
        cost_estimate=cost(0, 4 * shape[0] * shape[1]),
        compiler_params=room(4),
        name="stack",
    )(*pieces)


def one_on_other(a, b):
    zero = jnp.zeros((), a.dtype)
    above = lax.pad(a, zero, ((0, b.shape[0], 0), (0, 0, 0)))
    return above + lax.pad(b, zero, ((a.shape[0], 0, 0), (0, 0, 0)))


def forward_kernel(
    heads, member_ref, own_ref, other_ref, pair_ref, row_ref, column_ref, noise_ref,
    att_ref, probs_ref, parts_ref,
):
    tokens = own_ref.shape[0]
    size = pair_ref.shape[1]
    scale = 1.0 / math.sqrt(size)
    low = jnp.bfloat16

    def part(first):
        return (own_ref[:, pl.ds(first, size)] + other_ref[:, pl.ds(first, size)]).astype(low)

    first_member = member_ref[0] == 0
    mine = part(heads * size).astype(jnp.float32)
    pair = pair_ref[...].astype(jnp.float32)
    keys = jnp.where(first_member, mine, pair).astype(low)
    vals = jnp.where(first_member, pair, mine).astype(low)
    parts_ref[heads] = keys
    parts_ref[heads + 1] = vals
    query_at = lax.broadcasted_iota(jnp.int32, (tokens, tokens), 0)
    key_at = lax.broadcasted_iota(jnp.int32, (tokens, tokens), 1)
    allowed = (column_ref[...] == row_ref[...]) & (key_at <= query_at)
    for head in range(heads):
        query = part(head * size)
        parts_ref[head] = query
        scores = dot(query, keys, ((1,), (1,))) * scale
        scores = jnp.where(allowed, scores, -jnp.inf)
        expon = jnp.exp(scores - jnp.max(scores, axis=1, keepdims=True))
        probs = expon / jnp.sum(expon, axis=1, keepdims=True)
        probs_ref[head] = probs
        dropped = (probs * (1.0 + noise_ref[head].astype(jnp.float32))).astype(low)
        att_ref[:, pl.ds(head * size, size)] = dot(dropped, vals, ((1,), (0,))).astype(low)


def forward(member, own, other, pair, labels, noise):
    tokens, size = pair.shape
    heads = noise.shape[0]
    return pl.pallas_call(
        functools.partial(forward_kernel, heads),
        out_shape=(
            jax.ShapeDtypeStruct((tokens, heads * size), jnp.bfloat16),
            jax.ShapeDtypeStruct(noise.shape, jnp.float32),
            jax.ShapeDtypeStruct((heads + 2, tokens, size), jnp.bfloat16),
        ),
        in_specs=[SMEM] + [VMEM] * 6,
        out_specs=(VMEM,) * 3,
        cost_estimate=cost(4 * noise.size * size, 8 * own.size + 6 * noise.size),
        compiler_params=room(10),
        name="forward",
    )(member, own, other, pair, labels, labels.reshape(tokens, 1), noise)


def backward_kernel(
    heads, member_ref, own_ref, other_ref, probs_ref, parts_ref, noise_ref, query_ref, keep_ref, send_ref
):
    tokens, size = keep_ref.shape
    scale = 1.0 / math.sqrt(size)
    low = jnp.bfloat16
    first_member = member_ref[0] == 0
    keys, vals = parts_ref[heads], parts_ref[heads + 1]
    key_grad = jnp.zeros((tokens, size), jnp.float32)
    val_grad = jnp.zeros((tokens, size), jnp.float32)
    for head in range(heads):
        here = pl.ds(head * size, size)
        query, grad = parts_ref[head], (own_ref[:, here] + other_ref[:, here]).astype(low)
        probs = probs_ref[head]
        factor = 1.0 + noise_ref[head].astype(jnp.float32)
        dropped = (probs * factor).astype(low)
        val_grad += dot(dropped, grad, ((0,), (0,)))
        prob_grad = dot(grad, vals, ((1,), (1,))) * factor
        inner = jnp.sum(probs * prob_grad, axis=1, keepdims=True)
        score_grad = (probs * (prob_grad - inner) * scale).astype(low)
        query_ref[:, here] = dot(score_grad, keys, ((1,), (0,))).astype(low)
        key_grad += dot(score_grad, query, ((0,), (0,)))
    keep_ref[...] = jnp.where(first_member, key_grad, val_grad)
    send_ref[...] = jnp.where(first_member, val_grad, key_grad)


def backward(member, own, other, probs, parts, noise):
    heads, tokens, _ = noise.shape
    size = parts.shape[2]
    narrow = jax.ShapeDtypeStruct((tokens, size), jnp.float32)
    return pl.pallas_call(
        functools.partial(backward_kernel, heads),
        out_shape=(jax.ShapeDtypeStruct((tokens, heads * size), jnp.bfloat16), narrow, narrow),
        in_specs=[SMEM] + [VMEM] * 5,
        out_specs=(VMEM,) * 3,
        cost_estimate=cost(8 * noise.size * size, 6 * noise.size),
        compiler_params=room(10),
        name="backward",
    )(member, own, other, probs, parts, noise)


def place_kernel(member_ref, *refs):
    sources, out_ref = refs[:-1], refs[-1]

    def put(order):
        first = 0
        for pair in range(0, len(sources), 2):
            for n in order:
                source = sources[pair + n]
                out_ref[:, pl.ds(first, source.shape[1])] = source[pl.ds(0, out_ref.shape[0]), :].astype(
                    out_ref.dtype
                )
                first += source.shape[1]

    @pl.when(member_ref[0] == 0)
    def _():
        put((0, 1))

    @pl.when(member_ref[0] != 0)
    def _():
        put((1, 0))


def place_columns(member, *pieces):
    shape = (pieces[1].shape[0], sum(p.shape[1] for p in pieces))
    return pl.pallas_call(
        place_kernel,
        out_shape=jax.ShapeDtypeStruct(shape, pieces[0].dtype),
        in_specs=[SMEM] + [VMEM] * len(pieces),
        out_specs=VMEM,
        cost_estimate=cost(0, 8 * shape[0] * shape[1]),
        compiler_params=room(4),
        name="place",
    )(member, *pieces)


def paired_device(
    layer_inputs,
    loss_adjoint_matrix,
    attention_projection_matrix,
    merge_projection_transposed,
    packed_sequence_labels,
    dropout_factors,
    straggler_filter,
):
    grp = lax.axis_size("grp")
    member = lax.axis_index("rep")
    me = member * grp + lax.axis_index("grp")
    first = member == 0
    core, side, near, far = 1, 2, 4, 8

    def across(a, bit):
        return lax.ppermute(a, "grp", [(g, g ^ bit) for g in range(grp)])

    def across_rep(a):
        return lax.ppermute(a, "rep", [(0, 1), (1, 0)])

    heads = dropout_factors.shape[2]
    share = heads // 2
    width = merge_projection_transposed.shape[1]
    size = width // heads
    part = share * size

    def columns(a, first, count, m):
        return lax.dynamic_slice_in_dim(a, first + m * count, count, 1)

    def qkv_columns(m):
        queries = columns(attention_projection_matrix, 0, part, m)
        return jnp.concatenate(
            [queries, columns(attention_projection_matrix, width, size, m)], axis=1
        )

    def merge_columns(m):
        return columns(merge_projection_transposed, 0, part, m)

    def exchanged(pick):
        return one_on_other(pick(member), across_rep(pick(1 - member)))

    qkv = exchanged(qkv_columns)
    merge = exchanged(merge_columns)

    qkv_near, qkv_far = across(qkv, near), across(qkv, far)
    qkv_both = across(qkv_far, near)
    qkv_side = [
        across(qkv, side), across(qkv_far, side), across(qkv_near, side), across(qkv_both, side)
    ]
    merge_far = across(merge, far)
    merge_line = one_on_other(merge, merge_far)
    merge_near = across(merge_line, near)
    merge_pieces = [merge_line, merge_near, across(merge_line, side), across(merge_near, side)]

    def order(bits):
        found = [0]
        for bit in (core, *bits, grp):
            found = [at | b for at in found for b in (0, bit)]
        return jnp.array(found, jnp.int32) ^ me

    stages = ((near, side, far), (side, near, far))
    x_keep, x_send = flip(order(stages[0]), layer_inputs)
    y_keep, y_send = flip(order(stages[1]), loss_adjoint_matrix)
    x_other, y_other = across(x_send, core), across(y_send, core)

    def as_it_lies(a):
        return with_layout_constraint(a, Layout(major_to_minor=tuple(range(a.ndim))))

    noise = as_it_lies(across_rep(dropout_factors))

    def project(rows, weights):
        return dot(rows, weights, ((0,), (0,)))

    pieces = [qkv, qkv_far, *qkv_side[:2], qkv_near, qkv_both, qkv_side[2]]
    early = stack(pieces)
    cut = early.shape[0]
    away = project(x_other[:cut], early)
    qkv_in = across(away + project(x_other[cut:], qkv_side[3]), core)
    own = project(x_keep[:cut], early)
    qkv_own = own + project(x_keep[cut:], qkv_side[3])
    merge_rows = stack(merge_pieces)
    merge_in = across(project(y_other, merge_rows), core)
    merge_own = project(y_keep, merge_rows)

    pair = (qkv_own[:, part:] + qkv_in[:, part:]).astype(jnp.bfloat16)
    pair, noise, labels, straggler_filter = lax.optimization_barrier(
        (pair, noise, packed_sequence_labels, straggler_filter)
    )
    pair = across_rep(pair)
    kept_worker = jnp.sum(jnp.arange(2, dtype=jnp.int32) * straggler_filter[:, 0])
    noise = jnp.where(kept_worker == member, dropout_factors, noise)[0]
    noise = jnp.where(first, noise[:, :share], noise[:, share:])
    noise_used = jnp.transpose(noise, (1, 0, 2))
    member = member.reshape(1)
    att, probs, pieces = forward(member, qkv_own, qkv_in, pair, labels, noise_used)
    query_grad, pair_keep, pair_send = backward(
        member, merge_own, merge_in, probs, pieces, noise_used
    )
    pair_grad = (pair_keep + across_rep(pair_send)).astype(jnp.bfloat16)

    def first_two_exchanged(rows):
        halves = rows.reshape(2, 2, rows.shape[0] // 4, rows.shape[1])
        return jnp.swapaxes(halves, 0, 1).reshape(rows.shape)

    def reduced(keep, other, bits, grad, theirs):
        cut = keep.shape[0] // 2

        def half(rows):
            return dot(keep[rows], grad, ((1,), (0,))), other[rows]

        leaves, rows = half(slice(cut, None))
        leaves = (leaves + dot(rows, theirs, ((1,), (0,)))).astype(jnp.bfloat16)
        total, rows = half(slice(None, cut))
        for n, bit in enumerate(bits):
            arrived = across(leaves, bit)
            if n == 0:
                total = total + dot(rows, theirs, ((1,), (0,)))
            total = total + arrived.astype(jnp.float32)
            cut = total.shape[0] // 2
            whole = total
            leaves, total = total[cut:].astype(jnp.bfloat16), total[:cut]
        return whole, across_rep(leaves)

    merge = reduced(y_keep, y_other, stages[1], att, across(att, core))
    query = reduced(x_keep, x_other, stages[0], query_grad, across(query_grad, core))
    x_keep, x_other = first_two_exchanged(x_keep), first_two_exchanged(x_other)
    pair = reduced(x_keep, x_other, (side, near, far), pair_grad, across(pair_grad, core))
    return place_columns(member, *query, *pair, *merge)


def paired(mesh, shapes):
    rep, grp = mesh.shape["rep"], mesh.shape["grp"]
    depth, heads, tokens = shapes[0][1], shapes[5][2], shapes[5][3]
    size = shapes[3][1] // heads
    even = depth % (rep * grp * 16) == 0 and depth % 256 == 0
    return rep == 2 and grp == 16 and even and heads % 2 == 0 and size % 128 == 0 and tokens % 128 == 0


def solution(mesh):
    placed = (
        P("grp", None),
        P("grp", None),
        P(("rep", "grp"), None),
        P(("rep", "grp"), None),
        P("grp", None),
        P("rep", "grp", None, None),
        P(None, "grp"),
    )

    def on_devices(body):
        return jax.shard_map(
            body, mesh=mesh, in_specs=placed, out_specs=P(("rep", "grp"), None), check_vma=False
        )

    def step(*args):
        if not paired(mesh, [a.shape for a in args]):
            return on_devices(generic_device)(*args)
        return on_devices(paired_device)(*args)

    return step
```

```python
import functools
import math

import jax
import jax.numpy as jnp
from jax import lax
from jax.experimental import pallas as pl
from jax.experimental.layout import Layout, with_layout_constraint
from jax.experimental.pallas import tpu as pltpu
from jax.sharding import PartitionSpec as P


def from_root(block, axis, holder):
    block = jnp.where(lax.axis_index(axis) == holder, block, jnp.zeros_like(block))
    return lax.psum(block, axis)


def token_grads(projected_wide, attn_wide, doc_row, noise_rows):
    seq_len = projected_wide.shape[0]
    head_size = (projected_wide.shape[1] - attn_wide.shape[1]) // 2
    heads = attn_wide.shape[1] // head_size
    score_scale = 1.0 / jnp.sqrt(jnp.float32(head_size))
    projected = projected_wide.astype(jnp.bfloat16)
    queries = projected[:, : heads * head_size]
    key_rows = projected[:, heads * head_size : (heads + 1) * head_size]
    val_rows = projected[:, (heads + 1) * head_size :]
    query_heads = queries.reshape(seq_len, heads, head_size).astype(jnp.float32)
    keys_wide = key_rows.astype(jnp.float32)
    vals_wide = val_rows.astype(jnp.float32)
    position = jnp.arange(seq_len, dtype=jnp.int32)
    allowed = (doc_row[:, None] == doc_row[None, :]) & (position[None, :] <= position[:, None])
    scores = jnp.einsum("ihd,jd->hij", query_heads, keys_wide) * score_scale
    scores = jnp.where(allowed[None], scores, -jnp.inf)
    highest = jnp.max(scores, axis=2, keepdims=True)
    expon = jnp.exp(scores - highest)
    attn_probs = expon / jnp.sum(expon, axis=2, keepdims=True)
    factor = 1.0 + jnp.transpose(noise_rows.astype(jnp.float32), (1, 0, 2))
    dropped = (attn_probs * factor).astype(jnp.bfloat16)
    dropped_wide = dropped.astype(jnp.float32)
    attended = (
        jnp.einsum("hij,jd->ihd", dropped_wide, vals_wide)
        .astype(jnp.bfloat16)
        .reshape(seq_len, heads * head_size)
    )
    attn_grad = attn_wide.astype(jnp.bfloat16)
    grad_heads = attn_grad.reshape(seq_len, heads, head_size).astype(jnp.float32)
    val_grad = jnp.einsum("hij,ihd->jd", dropped_wide, grad_heads).astype(jnp.bfloat16)
    prob_grad = jnp.einsum("ihd,jd->hij", grad_heads, vals_wide) * factor
    inner = jnp.sum(attn_probs * prob_grad, axis=2, keepdims=True)
    score_grad = (attn_probs * (prob_grad - inner) * score_scale).astype(jnp.bfloat16)
    score_wide = score_grad.astype(jnp.float32)
    query_grad = (
        jnp.einsum("hij,jd->ihd", score_wide, keys_wide)
        .astype(jnp.bfloat16)
        .reshape(seq_len, heads * head_size)
    )
    key_grad = jnp.einsum("hij,ihd->jd", score_wide, query_heads).astype(jnp.bfloat16)
    stacked = jnp.concatenate([query_grad, key_grad, val_grad], axis=1)
    return (stacked, attended)


def weight_rows(hidden_rows, cot_rows, stacked, attended, first_row, row_count):
    hidden_cols = lax.dynamic_slice_in_dim(hidden_rows, first_row, row_count, 1)
    cot_cols = lax.dynamic_slice_in_dim(cot_rows, first_row, row_count, 1)
    proj_grad = jnp.dot(hidden_cols.T, stacked, preferred_element_type=jnp.float32)
    out_grad = jnp.dot(cot_cols.T, attended, preferred_element_type=jnp.float32)
    return jnp.concatenate([proj_grad, out_grad], axis=1)


def generic_device(
    layer_inputs,
    loss_adjoint_matrix,
    attention_projection_matrix,
    merge_projection_transposed,
    packed_sequence_labels,
    dropout_factors,
    straggler_filter,
):
    duplicate_workers = lax.axis_size("rep")
    member = lax.axis_index("rep")
    kept_worker = jnp.sum(jnp.arange(duplicate_workers, dtype=jnp.int32) * straggler_filter[:, 0])
    row_count = layer_inputs.shape[1] // duplicate_workers
    first_row = member * row_count
    qkv_full, out_full = (
        lax.all_gather(attention_projection_matrix, ("rep", "grp"), axis=0, tiled=True),
        lax.all_gather(merge_projection_transposed, ("rep", "grp"), axis=0, tiled=True),
    )
    projected_wide = jnp.dot(layer_inputs, qkv_full, preferred_element_type=jnp.float32)
    attn_wide = jnp.dot(loss_adjoint_matrix, out_full, preferred_element_type=jnp.float32)
    chosen_noise = from_root(dropout_factors[0], "rep", kept_worker)
    stacked, attended = token_grads(
        projected_wide, attn_wide, packed_sequence_labels[0], chosen_noise
    )
    gradient = weight_rows(
        layer_inputs, loss_adjoint_matrix, stacked, attended, first_row, row_count
    )
    return lax.psum_scatter(gradient, "grp", scatter_dimension=0, tiled=True)


def dot(a, b, dims):
    return lax.dot_general(a, b, (dims, ((), ())), preferred_element_type=jnp.float32)


VMEM = pl.BlockSpec(memory_space=pltpu.VMEM)
SMEM = pl.BlockSpec(memory_space=pltpu.SMEM)


def room(mebibytes):
    return pltpu.CompilerParams(vmem_limit_bytes=mebibytes << 20)


def cost(flops, count):
    return pl.CostEstimate(flops=flops, bytes_accessed=count, transcendentals=0)


def flip_kernel(order_ref, x_ref, keep_ref, send_ref, flipped):
    half = keep_ref.shape[0]
    blocks = order_ref.shape[0]
    rows = 2 * half // blocks
    width = x_ref.shape[1]
    for first in range(0, width, 256):
        flipped[pl.ds(first, 256), :] = x_ref[:, pl.ds(first, 256)].T
    for block in range(blocks):
        first = pl.multiple_of(order_ref[block] * rows, 16)
        target = keep_ref if block < blocks // 2 else send_ref
        place = (block % (blocks // 2)) * rows
        target[pl.ds(place, rows), :] = flipped[pl.ds(first, rows), :]


def flip(order, x):
    tokens, width = x.shape
    out = jax.ShapeDtypeStruct((width // 2, tokens), x.dtype)
    return pl.pallas_call(
        flip_kernel,
        out_shape=(out, out),
        in_specs=[SMEM, VMEM],
        out_specs=(VMEM, VMEM),
        scratch_shapes=[pltpu.VMEM((width, tokens), x.dtype)],
        cost_estimate=cost(0, 4 * x.size),
        compiler_params=room(10),
        name="flip",
    )(order, x)


def stack_kernel(*refs):
    sources, out_ref, sems = refs[:-2], refs[-2], refs[-1]
    copies = []
    first = 0
    for n, source in enumerate(sources):
        rows = source.shape[0]
        copies.append(pltpu.make_async_copy(source, out_ref.at[pl.ds(first, rows), :], sems.at[n]))
        first += rows
    for copy in copies:
        copy.start()
    for copy in copies:
        copy.wait()


def stack(pieces):
    shape = (sum(p.shape[0] for p in pieces), pieces[0].shape[1])
    return pl.pallas_call(
        stack_kernel,
        out_shape=jax.ShapeDtypeStruct(shape, pieces[0].dtype),
        in_specs=[pl.BlockSpec(memory_space=pl.ANY)] * len(pieces),
        out_specs=VMEM,
        scratch_shapes=[pltpu.SemaphoreType.DMA((len(pieces),))],
        cost_estimate=cost(0, 4 * shape[0] * shape[1]),
        compiler_params=room(4),
        name="stack",
    )(*pieces)


def one_on_other(a, b):
    zero = jnp.zeros((), a.dtype)
    above = lax.pad(a, zero, ((0, b.shape[0], 0), (0, 0, 0)))
    return above + lax.pad(b, zero, ((a.shape[0], 0, 0), (0, 0, 0)))


def forward_kernel(
    heads, member_ref, own_ref, other_ref, pair_ref, row_ref, column_ref, noise_ref,
    att_ref, probs_ref, parts_ref,
):
    tokens = own_ref.shape[0]
    size = pair_ref.shape[1]
    scale = 1.0 / math.sqrt(size)
    low = jnp.bfloat16

    def part(first):
        return (own_ref[:, pl.ds(first, size)] + other_ref[:, pl.ds(first, size)]).astype(low)

    first_member = member_ref[0] == 0
    mine = part(heads * size).astype(jnp.float32)
    pair = pair_ref[...].astype(jnp.float32)
    keys = jnp.where(first_member, mine, pair).astype(low)
    vals = jnp.where(first_member, pair, mine).astype(low)
    parts_ref[heads] = keys
    parts_ref[heads + 1] = vals
    query_at = lax.broadcasted_iota(jnp.int32, (tokens, tokens), 0)
    key_at = lax.broadcasted_iota(jnp.int32, (tokens, tokens), 1)
    allowed = (column_ref[...] == row_ref[...]) & (key_at <= query_at)
    for head in range(heads):
        query = part(head * size)
        parts_ref[head] = query
        scores = dot(query, keys, ((1,), (1,))) * scale
        scores = jnp.where(allowed, scores, -jnp.inf)
        expon = jnp.exp(scores - jnp.max(scores, axis=1, keepdims=True))
        probs = expon / jnp.sum(expon, axis=1, keepdims=True)
        probs_ref[head] = probs
        dropped = (probs * (1.0 + noise_ref[head].astype(jnp.float32))).astype(low)
        att_ref[:, pl.ds(head * size, size)] = dot(dropped, vals, ((1,), (0,))).astype(low)


def forward(member, own, other, pair, labels, noise):
    tokens, size = pair.shape
    heads = noise.shape[0]
    return pl.pallas_call(
        functools.partial(forward_kernel, heads),
        out_shape=(
            jax.ShapeDtypeStruct((tokens, heads * size), jnp.bfloat16),
            jax.ShapeDtypeStruct(noise.shape, jnp.float32),
            jax.ShapeDtypeStruct((heads + 2, tokens, size), jnp.bfloat16),
        ),
        in_specs=[SMEM] + [VMEM] * 6,
        out_specs=(VMEM,) * 3,
        cost_estimate=cost(4 * noise.size * size, 8 * own.size + 6 * noise.size),
        compiler_params=room(10),
        name="forward",
    )(member, own, other, pair, labels, labels.reshape(tokens, 1), noise)


def backward_kernel(
    heads, member_ref, own_ref, other_ref, probs_ref, parts_ref, noise_ref, query_ref, keep_ref, send_ref
):
    tokens, size = keep_ref.shape
    scale = 1.0 / math.sqrt(size)
    low = jnp.bfloat16
    first_member = member_ref[0] == 0
    keys, vals = parts_ref[heads], parts_ref[heads + 1]
    key_grad = jnp.zeros((tokens, size), jnp.float32)
    val_grad = jnp.zeros((tokens, size), jnp.float32)
    for head in range(heads):
        here = pl.ds(head * size, size)
        query, grad = parts_ref[head], (own_ref[:, here] + other_ref[:, here]).astype(low)
        probs = probs_ref[head]
        factor = 1.0 + noise_ref[head].astype(jnp.float32)
        dropped = (probs * factor).astype(low)
        val_grad += dot(dropped, grad, ((0,), (0,)))
        prob_grad = dot(grad, vals, ((1,), (1,))) * factor
        inner = jnp.sum(probs * prob_grad, axis=1, keepdims=True)
        score_grad = (probs * (prob_grad - inner) * scale).astype(low)
        query_ref[:, here] = dot(score_grad, keys, ((1,), (0,))).astype(low)
        key_grad += dot(score_grad, query, ((0,), (0,)))
    keep_ref[...] = jnp.where(first_member, key_grad, val_grad)
    send_ref[...] = jnp.where(first_member, val_grad, key_grad)


def backward(member, own, other, probs, parts, noise):
    heads, tokens, _ = noise.shape
    size = parts.shape[2]
    narrow = jax.ShapeDtypeStruct((tokens, size), jnp.float32)
    return pl.pallas_call(
        functools.partial(backward_kernel, heads),
        out_shape=(jax.ShapeDtypeStruct((tokens, heads * size), jnp.bfloat16), narrow, narrow),
        in_specs=[SMEM] + [VMEM] * 5,
        out_specs=(VMEM,) * 3,
        cost_estimate=cost(8 * noise.size * size, 6 * noise.size),
        compiler_params=room(10),
        name="backward",
    )(member, own, other, probs, parts, noise)


def gather_kernel(runs, *refs):
    sources, out_ref = refs[:-1], refs[-1]
    place = 0
    for source, (first, rows) in zip(sources, runs):
        out_ref[pl.ds(place, rows), :] = source[pl.ds(first, rows), :].astype(out_ref.dtype)
        place += rows


def gather_rows(*runs):
    arrays = [array for array, _, _ in runs]
    shape = (sum(rows for _, _, rows in runs), arrays[0].shape[1])
    return pl.pallas_call(
        functools.partial(gather_kernel, [(first, rows) for _, first, rows in runs]),
        out_shape=jax.ShapeDtypeStruct(shape, jnp.bfloat16),
        in_specs=[VMEM] * len(arrays),
        out_specs=VMEM,
        cost_estimate=cost(0, 4 * shape[0] * shape[1]),
        compiler_params=room(4),
        name="gather",
    )(*arrays)


def place_kernel(terms, member_ref, *refs):
    sources, out_ref = list(refs[:-1]), refs[-1]
    rows = out_ref.shape[0]
    columns = [[(sources.pop(0), first) for first in firsts] for firsts in terms]

    def put(order):
        place = 0
        for pair in range(0, len(columns), 2):
            for n in order:
                values = sum(
                    source[pl.ds(first, rows), :].astype(out_ref.dtype)
                    for source, first in columns[pair + n]
                )
                out_ref[:, pl.ds(place, values.shape[1])] = values
                place += values.shape[1]

    @pl.when(member_ref[0] == 0)
    def _():
        put((0, 1))

    @pl.when(member_ref[0] != 0)
    def _():
        put((1, 0))


def place_columns(member, rows, *pieces):
    terms = [[first for _, first in piece] for piece in pieces]
    arrays = [array for piece in pieces for array, _ in piece]
    shape = (rows, sum(piece[0][0].shape[1] for piece in pieces))
    return pl.pallas_call(
        functools.partial(place_kernel, terms),
        out_shape=jax.ShapeDtypeStruct(shape, jnp.float32),
        in_specs=[SMEM] + [VMEM] * len(arrays),
        out_specs=VMEM,
        cost_estimate=cost(0, 8 * shape[0] * shape[1]),
        compiler_params=room(4),
        name="place",
    )(member, *arrays)


def paired_device(
    layer_inputs,
    loss_adjoint_matrix,
    attention_projection_matrix,
    merge_projection_transposed,
    packed_sequence_labels,
    dropout_factors,
    straggler_filter,
):
    grp = lax.axis_size("grp")
    member = lax.axis_index("rep")
    me = member * grp + lax.axis_index("grp")
    first = member == 0
    core, side, near, far = 1, 2, 4, 8

    def across(a, bit):
        return lax.ppermute(a, "grp", [(g, g ^ bit) for g in range(grp)])

    def across_rep(a):
        return lax.ppermute(a, "rep", [(0, 1), (1, 0)])

    heads = dropout_factors.shape[2]
    share = heads // 2
    width = merge_projection_transposed.shape[1]
    size = width // heads
    part = share * size

    def columns(a, first, count, m):
        return lax.dynamic_slice_in_dim(a, first + m * count, count, 1)

    def qkv_columns(m):
        queries = columns(attention_projection_matrix, 0, part, m)
        return jnp.concatenate(
            [queries, columns(attention_projection_matrix, width, size, m)], axis=1
        )

    def merge_columns(m):
        return columns(merge_projection_transposed, 0, part, m)

    def exchanged(pick):
        return one_on_other(pick(member), across_rep(pick(1 - member)))

    qkv = exchanged(qkv_columns)
    merge = exchanged(merge_columns)

    qkv_near, qkv_far = across(qkv, near), across(qkv, far)
    qkv_both = across(qkv_far, near)
    qkv_side = [
        across(qkv, side), across(qkv_far, side), across(qkv_near, side), across(qkv_both, side)
    ]
    merge_far = across(merge, far)
    merge_line = one_on_other(merge, merge_far)
    merge_near = across(merge_line, near)
    merge_pieces = [merge_line, merge_near, across(merge_line, side), across(merge_near, side)]

    def order(bits):
        found = [0]
        for bit in (core, *bits, grp):
            found = [at | b for at in found for b in (0, bit)]
        return jnp.array(found, jnp.int32) ^ me

    stages = ((near, side, far), (side, near, far))
    x_keep, x_send = flip(order(stages[0]), layer_inputs)
    y_keep, y_send = flip(order(stages[1]), loss_adjoint_matrix)
    x_other, y_other = across(x_send, core), across(y_send, core)

    def as_it_lies(a):
        return with_layout_constraint(a, Layout(major_to_minor=tuple(range(a.ndim))))

    noise = as_it_lies(across_rep(dropout_factors))

    def project(rows, weights):
        return dot(rows, weights, ((0,), (0,)))

    pieces = [qkv, qkv_far, *qkv_side[:2], qkv_near, qkv_both, qkv_side[2]]
    early = stack(pieces)
    cut = early.shape[0]
    away = project(x_other[:cut], early)
    qkv_in = across(away + project(x_other[cut:], qkv_side[3]), core)
    own = project(x_keep[:cut], early)
    qkv_own = own + project(x_keep[cut:], qkv_side[3])
    merge_rows = stack(merge_pieces)
    merge_in = across(project(y_other, merge_rows), core)
    merge_own = project(y_keep, merge_rows)

    pair = (qkv_own[:, part:] + qkv_in[:, part:]).astype(jnp.bfloat16)
    pair, noise, labels, straggler_filter = lax.optimization_barrier(
        (pair, noise, packed_sequence_labels, straggler_filter)
    )
    pair = across_rep(pair)
    kept_worker = jnp.sum(jnp.arange(2, dtype=jnp.int32) * straggler_filter[:, 0])
    noise = jnp.where(kept_worker == member, dropout_factors, noise)[0]
    noise = jnp.where(first, noise[:, :share], noise[:, share:])
    noise_used = jnp.transpose(noise, (1, 0, 2))
    member = member.reshape(1)
    att, probs, pieces = forward(member, qkv_own, qkv_in, pair, labels, noise_used)
    query_grad, pair_keep, pair_send = backward(
        member, merge_own, merge_in, probs, pieces, noise_used
    )
    pair_grad = (pair_keep + across_rep(pair_send)).astype(jnp.bfloat16)

    def first_two_exchanged(rows):
        halves = rows.reshape(2, 2, rows.shape[0] // 4, rows.shape[1])
        return jnp.swapaxes(halves, 0, 1).reshape(rows.shape)

    def reduced(name, keep, other, bits, grad, theirs):
        cut = keep.shape[0] // 2

        def half(rows):
            return dot(keep[rows], grad, ((1,), (0,))), other[rows]

        leaves, rows = half(slice(cut, None))
        leaves = (leaves + dot(rows, theirs, ((1,), (0,)))).astype(jnp.bfloat16)
        total, rows = half(slice(None, cut))
        for n, bit in enumerate(bits):
            arrived = across(leaves, bit)
            if n == 0:
                total = total + dot(rows, theirs, ((1,), (0,)))
            total = total + arrived.astype(jnp.float32)
            whole = total
            if n < len(bits) - 1 or name == "m":
                cut = total.shape[0] // 2
                leaves, total = total[cut:].astype(jnp.bfloat16), total[:cut]
        return whole, leaves

    def swapped_last(name, keep, other, bits, grad, theirs):
        whole, leaves = reduced(name, keep, other, bits, grad, theirs)
        swapped = across_rep(leaves)
        return ((whole, 0),), ((swapped, 0),)

    def swapped_first(name, keep, other, bits, grad, theirs):
        whole, _ = reduced(name, keep, other, bits[:-1], grad, theirs)
        rows, count = whole.shape[0] // 4, whole.shape[1]
        leaves = whole.reshape(2, 2, rows, count)[:, 1].astype(jnp.bfloat16)
        leaves = leaves.reshape(2 * rows, count)
        partner = across_rep(leaves)
        leaves = gather_rows((whole, 2 * rows, rows), (partner, rows, rows))
        arrived = across(leaves, bits[-1])
        return ((whole, 0), (arrived, 0)), ((partner, 0), (arrived, rows))

    merge = swapped_last("m", y_keep, y_other, stages[1], att, across(att, core))
    query = swapped_first("q", x_keep, x_other, stages[0], query_grad, across(query_grad, core))
    x_keep, x_other = first_two_exchanged(x_keep), first_two_exchanged(x_other)
    pair = swapped_first(
        "p", x_keep, x_other, (side, near, far), pair_grad, across(pair_grad, core)
    )
    rows = attention_projection_matrix.shape[0]
    return place_columns(member, rows, *query, *pair, *merge)


def paired(mesh, shapes):
    rep, grp = mesh.shape["rep"], mesh.shape["grp"]
    depth, heads, tokens = shapes[0][1], shapes[5][2], shapes[5][3]
    size = shapes[3][1] // heads
    even = depth % (rep * grp * 16) == 0 and depth % 256 == 0
    return rep == 2 and grp == 16 and even and heads % 2 == 0 and size % 128 == 0 and tokens % 128 == 0


def solution(mesh):
    placed = (
        P("grp", None),
        P("grp", None),
        P(("rep", "grp"), None),
        P(("rep", "grp"), None),
        P("grp", None),
        P("rep", "grp", None, None),
        P(None, "grp"),
    )

    def on_devices(body):
        return jax.shard_map(
            body, mesh=mesh, in_specs=placed, out_specs=P(("rep", "grp"), None), check_vma=False
        )

    def step(*args):
        if not paired(mesh, [a.shape for a in args]):
            return on_devices(generic_device)(*args)
        return on_devices(paired_device)(*args)

    return step
```

```python
import functools
import math

import jax
import jax.numpy as jnp
from jax import lax
from jax.experimental import pallas as pl
from jax.experimental.layout import Layout, with_layout_constraint
from jax.experimental.pallas import tpu as pltpu
from jax.sharding import PartitionSpec as P


def from_root(block, axis, holder):
    block = jnp.where(lax.axis_index(axis) == holder, block, jnp.zeros_like(block))
    return lax.psum(block, axis)


def token_grads(projected_wide, attn_wide, doc_row, noise_rows):
    seq_len = projected_wide.shape[0]
    head_size = (projected_wide.shape[1] - attn_wide.shape[1]) // 2
    heads = attn_wide.shape[1] // head_size
    score_scale = 1.0 / jnp.sqrt(jnp.float32(head_size))
    projected = projected_wide.astype(jnp.bfloat16)
    queries = projected[:, : heads * head_size]
    key_rows = projected[:, heads * head_size : (heads + 1) * head_size]
    val_rows = projected[:, (heads + 1) * head_size :]
    query_heads = queries.reshape(seq_len, heads, head_size).astype(jnp.float32)
    keys_wide = key_rows.astype(jnp.float32)
    vals_wide = val_rows.astype(jnp.float32)
    position = jnp.arange(seq_len, dtype=jnp.int32)
    allowed = (doc_row[:, None] == doc_row[None, :]) & (position[None, :] <= position[:, None])
    scores = jnp.einsum("ihd,jd->hij", query_heads, keys_wide) * score_scale
    scores = jnp.where(allowed[None], scores, -jnp.inf)
    highest = jnp.max(scores, axis=2, keepdims=True)
    expon = jnp.exp(scores - highest)
    attn_probs = expon / jnp.sum(expon, axis=2, keepdims=True)
    factor = 1.0 + jnp.transpose(noise_rows.astype(jnp.float32), (1, 0, 2))
    dropped = (attn_probs * factor).astype(jnp.bfloat16)
    dropped_wide = dropped.astype(jnp.float32)
    attended = (
        jnp.einsum("hij,jd->ihd", dropped_wide, vals_wide)
        .astype(jnp.bfloat16)
        .reshape(seq_len, heads * head_size)
    )
    attn_grad = attn_wide.astype(jnp.bfloat16)
    grad_heads = attn_grad.reshape(seq_len, heads, head_size).astype(jnp.float32)
    val_grad = jnp.einsum("hij,ihd->jd", dropped_wide, grad_heads).astype(jnp.bfloat16)
    prob_grad = jnp.einsum("ihd,jd->hij", grad_heads, vals_wide) * factor
    inner = jnp.sum(attn_probs * prob_grad, axis=2, keepdims=True)
    score_grad = (attn_probs * (prob_grad - inner) * score_scale).astype(jnp.bfloat16)
    score_wide = score_grad.astype(jnp.float32)
    query_grad = (
        jnp.einsum("hij,jd->ihd", score_wide, keys_wide)
        .astype(jnp.bfloat16)
        .reshape(seq_len, heads * head_size)
    )
    key_grad = jnp.einsum("hij,ihd->jd", score_wide, query_heads).astype(jnp.bfloat16)
    stacked = jnp.concatenate([query_grad, key_grad, val_grad], axis=1)
    return (stacked, attended)


def weight_rows(hidden_rows, cot_rows, stacked, attended, first_row, row_count):
    hidden_cols = lax.dynamic_slice_in_dim(hidden_rows, first_row, row_count, 1)
    cot_cols = lax.dynamic_slice_in_dim(cot_rows, first_row, row_count, 1)
    proj_grad = jnp.dot(hidden_cols.T, stacked, preferred_element_type=jnp.float32)
    out_grad = jnp.dot(cot_cols.T, attended, preferred_element_type=jnp.float32)
    return jnp.concatenate([proj_grad, out_grad], axis=1)


def generic_device(
    layer_inputs,
    loss_adjoint_matrix,
    attention_projection_matrix,
    merge_projection_transposed,
    packed_sequence_labels,
    dropout_factors,
    straggler_filter,
):
    duplicate_workers = lax.axis_size("rep")
    member = lax.axis_index("rep")
    kept_worker = jnp.sum(jnp.arange(duplicate_workers, dtype=jnp.int32) * straggler_filter[:, 0])
    row_count = layer_inputs.shape[1] // duplicate_workers
    first_row = member * row_count
    qkv_full, out_full = (
        lax.all_gather(attention_projection_matrix, ("rep", "grp"), axis=0, tiled=True),
        lax.all_gather(merge_projection_transposed, ("rep", "grp"), axis=0, tiled=True),
    )
    projected_wide = jnp.dot(layer_inputs, qkv_full, preferred_element_type=jnp.float32)
    attn_wide = jnp.dot(loss_adjoint_matrix, out_full, preferred_element_type=jnp.float32)
    chosen_noise = from_root(dropout_factors[0], "rep", kept_worker)
    stacked, attended = token_grads(
        projected_wide, attn_wide, packed_sequence_labels[0], chosen_noise
    )
    gradient = weight_rows(
        layer_inputs, loss_adjoint_matrix, stacked, attended, first_row, row_count
    )
    return lax.psum_scatter(gradient, "grp", scatter_dimension=0, tiled=True)


def dot(a, b, dims):
    return lax.dot_general(a, b, (dims, ((), ())), preferred_element_type=jnp.float32)


VMEM = pl.BlockSpec(memory_space=pltpu.VMEM)
SMEM = pl.BlockSpec(memory_space=pltpu.SMEM)


def room(mebibytes):
    return pltpu.CompilerParams(vmem_limit_bytes=mebibytes << 20)


def cost(flops, count):
    return pl.CostEstimate(flops=flops, bytes_accessed=count, transcendentals=0)


def flip_kernel(order_ref, x_ref, keep_ref, send_ref, landed, flipped, sems):
    half = keep_ref.shape[0]
    blocks = order_ref.shape[0]
    rows = 2 * half // blocks
    parts = sems.shape[0]
    width = x_ref.shape[1] // parts
    copies = []
    for part in range(parts):
        here = pl.ds(part * width, width)
        copies.append(pltpu.make_async_copy(x_ref.at[:, here], landed.at[:, here], sems.at[part]))
    for copy in copies:
        copy.start()
    for part, copy in enumerate(copies):
        copy.wait()
        for first in range(part * width, (part + 1) * width, 128):
            flipped[pl.ds(first, 128), :] = landed[:, pl.ds(first, 128)].T
    for block in range(blocks):
        first = pl.multiple_of(order_ref[block] * rows, 16)
        target = keep_ref if block < blocks // 2 else send_ref
        place = (block % (blocks // 2)) * rows
        target[pl.ds(place, rows), :] = flipped[pl.ds(first, rows), :]


def flip(order, x):
    tokens, width = x.shape
    parts = 4 if width % 512 == 0 else 1
    out = jax.ShapeDtypeStruct((width // 2, tokens), x.dtype)
    return pl.pallas_call(
        flip_kernel,
        out_shape=(out, out),
        in_specs=[SMEM, pl.BlockSpec(memory_space=pltpu.HBM)],
        out_specs=(VMEM, VMEM),
        scratch_shapes=[
            pltpu.VMEM((tokens, width), x.dtype),
            pltpu.VMEM((width, tokens), x.dtype),
            pltpu.SemaphoreType.DMA((parts,)),
        ],
        cost_estimate=cost(0, 4 * x.size),
        compiler_params=room(12),
        name="flip",
    )(order, x)


def stack_kernel(pieces, *refs):
    sources, targets, sems = refs[:pieces], refs[pieces:-1], refs[-1]
    carried, targets = targets[: len(targets) // 2], targets[len(targets) // 2 :]
    copies = []
    first = 0
    for source in sources:
        rows = source.shape[0]
        copies.append((source, targets[0].at[pl.ds(first, rows), :]))
        first += rows
    copies += zip(carried, targets[1:])
    copies = [pltpu.make_async_copy(*ends, sems.at[n]) for n, ends in enumerate(copies)]
    for copy in copies:
        copy.start()
    for copy in copies:
        copy.wait()


def stack(pieces, carried=()):
    shape = (sum(p.shape[0] for p in pieces), pieces[0].shape[1])
    out = [jax.ShapeDtypeStruct(shape, pieces[0].dtype)]
    out += [jax.ShapeDtypeStruct(a.shape, a.dtype) for a in carried]
    moved = len(pieces) + len(carried)
    return pl.pallas_call(
        functools.partial(stack_kernel, len(pieces)),
        out_shape=out,
        in_specs=[pl.BlockSpec(memory_space=pl.ANY)] * moved,
        out_specs=[VMEM] * len(out),
        scratch_shapes=[pltpu.SemaphoreType.DMA((moved,))],
        cost_estimate=cost(0, 4 * sum(a.size for a in out)),
        compiler_params=room(6),
        name="stack",
    )(*pieces, *carried)


def one_on_other(a, b):
    zero = jnp.zeros((), a.dtype)
    above = lax.pad(a, zero, ((0, b.shape[0], 0), (0, 0, 0)))
    return above + lax.pad(b, zero, ((a.shape[0], 0, 0), (0, 0, 0)))


def forward_kernel(
    heads, member_ref, own_ref, other_ref, pair_ref, row_ref, column_ref, noise_ref,
    att_ref, probs_ref, parts_ref,
):
    tokens = own_ref.shape[0]
    size = pair_ref.shape[1]
    scale = 1.0 / math.sqrt(size)
    low = jnp.bfloat16

    def part(first):
        return (own_ref[:, pl.ds(first, size)] + other_ref[:, pl.ds(first, size)]).astype(low)

    first_member = member_ref[0] == 0
    mine = part(heads * size).astype(jnp.float32)
    pair = pair_ref[...].astype(jnp.float32)
    keys = jnp.where(first_member, mine, pair).astype(low)
    vals = jnp.where(first_member, pair, mine).astype(low)
    parts_ref[heads] = keys
    parts_ref[heads + 1] = vals
    query_at = lax.broadcasted_iota(jnp.int32, (tokens, tokens), 0)
    key_at = lax.broadcasted_iota(jnp.int32, (tokens, tokens), 1)
    allowed = (column_ref[...] == row_ref[...]) & (key_at <= query_at)
    for head in range(heads):
        query = part(head * size)
        parts_ref[head] = query
        scores = dot(query, keys, ((1,), (1,))) * scale
        scores = jnp.where(allowed, scores, -jnp.inf)
        expon = jnp.exp(scores - jnp.max(scores, axis=1, keepdims=True))
        probs = expon / jnp.sum(expon, axis=1, keepdims=True)
        probs_ref[head] = probs
        dropped = (probs * (1.0 + noise_ref[head].astype(jnp.float32))).astype(low)
        att_ref[:, pl.ds(head * size, size)] = dot(dropped, vals, ((1,), (0,))).astype(low)


def forward(member, own, other, pair, labels, noise):
    tokens, size = pair.shape
    heads = noise.shape[0]
    return pl.pallas_call(
        functools.partial(forward_kernel, heads),
        out_shape=(
            jax.ShapeDtypeStruct((tokens, heads * size), jnp.bfloat16),
            jax.ShapeDtypeStruct(noise.shape, jnp.float32),
            jax.ShapeDtypeStruct((heads + 2, tokens, size), jnp.bfloat16),
        ),
        in_specs=[SMEM] + [VMEM] * 6,
        out_specs=(VMEM,) * 3,
        cost_estimate=cost(4 * noise.size * size, 8 * own.size + 6 * noise.size),
        compiler_params=room(10),
        name="forward",
    )(member, own, other, pair, *labels, noise)


def backward_kernel(
    heads, member_ref, own_ref, other_ref, probs_ref, parts_ref, noise_ref, query_ref, keep_ref, send_ref
):
    tokens, size = keep_ref.shape
    scale = 1.0 / math.sqrt(size)
    low = jnp.bfloat16
    first_member = member_ref[0] == 0
    keys, vals = parts_ref[heads], parts_ref[heads + 1]
    key_grad = jnp.zeros((tokens, size), jnp.float32)
    val_grad = jnp.zeros((tokens, size), jnp.float32)
    for head in range(heads):
        here = pl.ds(head * size, size)
        query, grad = parts_ref[head], (own_ref[:, here] + other_ref[:, here]).astype(low)
        probs = probs_ref[head]
        factor = 1.0 + noise_ref[head].astype(jnp.float32)
        dropped = (probs * factor).astype(low)
        val_grad += dot(dropped, grad, ((0,), (0,)))
        prob_grad = dot(grad, vals, ((1,), (1,))) * factor
        inner = jnp.sum(probs * prob_grad, axis=1, keepdims=True)
        score_grad = (probs * (prob_grad - inner) * scale).astype(low)
        query_ref[:, here] = dot(score_grad, keys, ((1,), (0,))).astype(low)
        key_grad += dot(score_grad, query, ((0,), (0,)))
    keep_ref[...] = jnp.where(first_member, key_grad, val_grad)
    send_ref[...] = jnp.where(first_member, val_grad, key_grad)


def backward(member, own, other, probs, parts, noise):
    heads, tokens, _ = noise.shape
    size = parts.shape[2]
    narrow = jax.ShapeDtypeStruct((tokens, size), jnp.float32)
    return pl.pallas_call(
        functools.partial(backward_kernel, heads),
        out_shape=(jax.ShapeDtypeStruct((tokens, heads * size), jnp.bfloat16), narrow, narrow),
        in_specs=[SMEM] + [VMEM] * 5,
        out_specs=(VMEM,) * 3,
        cost_estimate=cost(8 * noise.size * size, 6 * noise.size),
        compiler_params=room(10),
        name="backward",
    )(member, own, other, probs, parts, noise)


def gather_kernel(runs, *refs):
    sources, out_ref = refs[:-1], refs[-1]
    place = 0
    for source, (first, rows) in zip(sources, runs):
        out_ref[pl.ds(place, rows), :] = source[pl.ds(first, rows), :].astype(out_ref.dtype)
        place += rows


def gather_rows(*runs):
    arrays = [array for array, _, _ in runs]
    shape = (sum(rows for _, _, rows in runs), arrays[0].shape[1])
    return pl.pallas_call(
        functools.partial(gather_kernel, [(first, rows) for _, first, rows in runs]),
        out_shape=jax.ShapeDtypeStruct(shape, jnp.bfloat16),
        in_specs=[VMEM] * len(arrays),
        out_specs=VMEM,
        cost_estimate=cost(0, 4 * shape[0] * shape[1]),
        compiler_params=room(4),
        name="gather",
    )(*arrays)


def place_kernel(terms, member_ref, *refs):
    sources, out_ref = list(refs[:-1]), refs[-1]
    rows = out_ref.shape[0]
    columns = [[(sources.pop(0), first) for first in firsts] for firsts in terms]

    def put(order):
        place = 0
        for pair in range(0, len(columns), 2):
            for n in order:
                values = sum(
                    source[pl.ds(first, rows), :].astype(out_ref.dtype)
                    for source, first in columns[pair + n]
                )
                out_ref[:, pl.ds(place, values.shape[1])] = values
                place += values.shape[1]

    @pl.when(member_ref[0] == 0)
    def _():
        put((0, 1))

    @pl.when(member_ref[0] != 0)
    def _():
        put((1, 0))


def place_columns(member, rows, *pieces):
    terms = [[first for _, first in piece] for piece in pieces]
    arrays = [array for piece in pieces for array, _ in piece]
    shape = (rows, sum(piece[0][0].shape[1] for piece in pieces))
    return pl.pallas_call(
        functools.partial(place_kernel, terms),
        out_shape=jax.ShapeDtypeStruct(shape, jnp.float32),
        in_specs=[SMEM] + [VMEM] * len(arrays),
        out_specs=VMEM,
        cost_estimate=cost(0, 8 * shape[0] * shape[1]),
        compiler_params=room(4),
        name="place",
    )(member, *arrays)


def paired_device(
    layer_inputs,
    loss_adjoint_matrix,
    attention_projection_matrix,
    merge_projection_transposed,
    packed_sequence_labels,
    dropout_factors,
    straggler_filter,
):
    grp = lax.axis_size("grp")
    member = lax.axis_index("rep")
    me = member * grp + lax.axis_index("grp")
    first = member == 0
    core, side, near, far = 1, 2, 4, 8

    def across(a, bit):
        return lax.ppermute(a, "grp", [(g, g ^ bit) for g in range(grp)])

    def across_rep(a):
        return lax.ppermute(a, "rep", [(0, 1), (1, 0)])

    heads, tokens = dropout_factors.shape[2], dropout_factors.shape[3]
    share = heads // 2
    width = merge_projection_transposed.shape[1]
    size = width // heads
    part = share * size

    def columns(a, first, count, m):
        return lax.dynamic_slice_in_dim(a, first + m * count, count, 1)

    def qkv_columns(m):
        queries = columns(attention_projection_matrix, 0, part, m)
        return jnp.concatenate(
            [queries, columns(attention_projection_matrix, width, size, m)], axis=1
        )

    def merge_columns(m):
        return columns(merge_projection_transposed, 0, part, m)

    def exchanged(pick):
        return one_on_other(pick(member), across_rep(pick(1 - member)))

    qkv = exchanged(qkv_columns)
    merge = exchanged(merge_columns)

    qkv_near, qkv_far = across(qkv, near), across(qkv, far)
    qkv_both = across(qkv_far, near)
    qkv_side = [
        across(qkv, side), across(qkv_far, side), across(qkv_near, side), across(qkv_both, side)
    ]
    merge_far = across(merge, far)
    merge_line = one_on_other(merge, merge_far)
    merge_near = across(merge_line, near)
    merge_pieces = [merge_line, merge_near, across(merge_line, side), across(merge_near, side)]

    def order(bits):
        found = [0]
        for bit in (core, *bits, grp):
            found = [at | b for at in found for b in (0, bit)]
        return jnp.array(found, jnp.int32) ^ me

    stages = ((near, side, far), (side, near, far))
    x_keep, x_send = flip(order(stages[0]), layer_inputs)
    y_keep, y_send = flip(order(stages[1]), loss_adjoint_matrix)
    x_other, y_other = across(x_send, core), across(y_send, core)

    def as_it_lies(a):
        return with_layout_constraint(a, Layout(major_to_minor=tuple(range(a.ndim))))

    noise = as_it_lies(across_rep(dropout_factors))

    def project(rows, weights):
        return dot(rows, weights, ((0,), (0,)))

    pieces = [qkv, qkv_far, *qkv_side[:2], qkv_near, qkv_both, qkv_side[2]]
    (early,) = stack(pieces)
    cut = early.shape[0]
    away = project(x_other[:cut], early)
    qkv_in = across(away + project(x_other[cut:], qkv_side[3]), core)
    own = project(x_keep[:cut], early)
    qkv_own = own + project(x_keep[cut:], qkv_side[3])
    merge_rows, y_other = stack(merge_pieces, (y_other,))
    merge_in = across(project(y_other, merge_rows), core)
    merge_own = project(y_keep, merge_rows)

    pair = (qkv_own[:, part:] + qkv_in[:, part:]).astype(jnp.bfloat16)
    pair, noise = lax.optimization_barrier((pair, noise))
    pair = across_rep(pair)
    kept_worker = jnp.sum(jnp.arange(2, dtype=jnp.int32) * straggler_filter[:, 0])
    labels = (packed_sequence_labels, packed_sequence_labels.reshape(tokens, 1))
    noise = jnp.where(kept_worker == member, dropout_factors, noise)[0]
    noise = jnp.where(first, noise[:, :share], noise[:, share:])
    noise_used = jnp.transpose(noise, (1, 0, 2))
    member = member.reshape(1)
    att, probs, pieces = forward(member, qkv_own, qkv_in, pair, labels, noise_used)
    query_grad, pair_keep, pair_send = backward(
        member, merge_own, merge_in, probs, pieces, noise_used
    )
    pair_grad = (pair_keep + across_rep(pair_send)).astype(jnp.bfloat16)

    def first_two_exchanged(rows):
        halves = rows.reshape(2, 2, rows.shape[0] // 4, rows.shape[1])
        return jnp.swapaxes(halves, 0, 1).reshape(rows.shape)

    def reduced(name, keep, other, bits, grad, theirs):
        cut = keep.shape[0] // 2

        def half(rows):
            return dot(keep[rows], grad, ((1,), (0,))), other[rows]

        leaves, rows = half(slice(cut, None))
        leaves = (leaves + dot(rows, theirs, ((1,), (0,)))).astype(jnp.bfloat16)
        total, rows = half(slice(None, cut))
        for n, bit in enumerate(bits):
            arrived = across(leaves, bit)
            if n == 0:
                total = total + dot(rows, theirs, ((1,), (0,)))
            total = total + arrived.astype(jnp.float32)
            whole = total
            if n < len(bits) - 1 or name != "q":
                cut = total.shape[0] // 2
                leaves, total = total[cut:].astype(jnp.bfloat16), total[:cut]
        return whole, leaves

    def swapped_last(name, keep, other, bits, grad, theirs):
        whole, leaves = reduced(name, keep, other, bits, grad, theirs)
        swapped = across_rep(leaves)
        return ((whole, 0),), ((swapped, 0),)

    def swapped_first(name, keep, other, bits, grad, theirs):
        whole, _ = reduced(name, keep, other, bits[:-1], grad, theirs)
        rows, count = whole.shape[0] // 4, whole.shape[1]
        leaves = whole.reshape(2, 2, rows, count)[:, 1].astype(jnp.bfloat16)
        leaves = leaves.reshape(2 * rows, count)
        partner = across_rep(leaves)
        leaves = gather_rows((whole, 2 * rows, rows), (partner, rows, rows))
        arrived = across(leaves, bits[-1])
        return ((whole, 0), (arrived, 0)), ((partner, 0), (arrived, rows))

    merge = swapped_last("m", y_keep, y_other, stages[1], att, across(att, core))
    query = swapped_first("q", x_keep, x_other, stages[0], query_grad, across(query_grad, core))
    x_keep, x_other = first_two_exchanged(x_keep), first_two_exchanged(x_other)
    pair = swapped_last("p", x_keep, x_other, (side, near, far), pair_grad, across(pair_grad, core))
    rows = attention_projection_matrix.shape[0]
    return place_columns(member, rows, *query, *pair, *merge)


def paired(mesh, shapes):
    rep, grp = mesh.shape["rep"], mesh.shape["grp"]
    depth, heads, tokens = shapes[0][1], shapes[5][2], shapes[5][3]
    size = shapes[3][1] // heads
    even = depth % (rep * grp * 16) == 0 and depth % 256 == 0
    return rep == 2 and grp == 16 and even and heads % 2 == 0 and size % 128 == 0 and tokens % 128 == 0


def solution(mesh):
    placed = (
        P("grp", None),
        P("grp", None),
        P(("rep", "grp"), None),
        P(("rep", "grp"), None),
        P("grp", None),
        P("rep", "grp", None, None),
        P(None, "grp"),
    )

    def on_devices(body):
        return jax.shard_map(
            body, mesh=mesh, in_specs=placed, out_specs=P(("rep", "grp"), None), check_vma=False
        )

    def step(*args):
        if not paired(mesh, [a.shape for a in args]):
            return on_devices(generic_device)(*args)
        return on_devices(paired_device)(*args)

    return step
```

```python
import functools
import math

import jax
import jax.numpy as jnp
from jax import lax
from jax.experimental import pallas as pl
from jax.experimental.layout import Layout, with_layout_constraint
from jax.experimental.pallas import tpu as pltpu
from jax.sharding import PartitionSpec as P


def from_root(block, axis, holder):
    block = jnp.where(lax.axis_index(axis) == holder, block, jnp.zeros_like(block))
    return lax.psum(block, axis)


def token_grads(projected_wide, attn_wide, doc_row, noise_rows):
    seq_len = projected_wide.shape[0]
    head_size = (projected_wide.shape[1] - attn_wide.shape[1]) // 2
    heads = attn_wide.shape[1] // head_size
    score_scale = 1.0 / jnp.sqrt(jnp.float32(head_size))
    projected = projected_wide.astype(jnp.bfloat16)
    queries = projected[:, : heads * head_size]
    key_rows = projected[:, heads * head_size : (heads + 1) * head_size]
    val_rows = projected[:, (heads + 1) * head_size :]
    query_heads = queries.reshape(seq_len, heads, head_size).astype(jnp.float32)
    keys_wide = key_rows.astype(jnp.float32)
    vals_wide = val_rows.astype(jnp.float32)
    position = jnp.arange(seq_len, dtype=jnp.int32)
    allowed = (doc_row[:, None] == doc_row[None, :]) & (position[None, :] <= position[:, None])
    scores = jnp.einsum("ihd,jd->hij", query_heads, keys_wide) * score_scale
    scores = jnp.where(allowed[None], scores, -jnp.inf)
    highest = jnp.max(scores, axis=2, keepdims=True)
    expon = jnp.exp(scores - highest)
    attn_probs = expon / jnp.sum(expon, axis=2, keepdims=True)
    factor = 1.0 + jnp.transpose(noise_rows.astype(jnp.float32), (1, 0, 2))
    dropped = (attn_probs * factor).astype(jnp.bfloat16)
    dropped_wide = dropped.astype(jnp.float32)
    attended = (
        jnp.einsum("hij,jd->ihd", dropped_wide, vals_wide)
        .astype(jnp.bfloat16)
        .reshape(seq_len, heads * head_size)
    )
    attn_grad = attn_wide.astype(jnp.bfloat16)
    grad_heads = attn_grad.reshape(seq_len, heads, head_size).astype(jnp.float32)
    val_grad = jnp.einsum("hij,ihd->jd", dropped_wide, grad_heads).astype(jnp.bfloat16)
    prob_grad = jnp.einsum("ihd,jd->hij", grad_heads, vals_wide) * factor
    inner = jnp.sum(attn_probs * prob_grad, axis=2, keepdims=True)
    score_grad = (attn_probs * (prob_grad - inner) * score_scale).astype(jnp.bfloat16)
    score_wide = score_grad.astype(jnp.float32)
    query_grad = (
        jnp.einsum("hij,jd->ihd", score_wide, keys_wide)
        .astype(jnp.bfloat16)
        .reshape(seq_len, heads * head_size)
    )
    key_grad = jnp.einsum("hij,ihd->jd", score_wide, query_heads).astype(jnp.bfloat16)
    stacked = jnp.concatenate([query_grad, key_grad, val_grad], axis=1)
    return (stacked, attended)


def weight_rows(hidden_rows, cot_rows, stacked, attended, first_row, row_count):
    hidden_cols = lax.dynamic_slice_in_dim(hidden_rows, first_row, row_count, 1)
    cot_cols = lax.dynamic_slice_in_dim(cot_rows, first_row, row_count, 1)
    proj_grad = jnp.dot(hidden_cols.T, stacked, preferred_element_type=jnp.float32)
    out_grad = jnp.dot(cot_cols.T, attended, preferred_element_type=jnp.float32)
    return jnp.concatenate([proj_grad, out_grad], axis=1)


def generic_device(
    layer_inputs,
    loss_adjoint_matrix,
    attention_projection_matrix,
    merge_projection_transposed,
    packed_sequence_labels,
    dropout_factors,
    straggler_filter,
):
    duplicate_workers = lax.axis_size("rep")
    member = lax.axis_index("rep")
    kept_worker = jnp.sum(jnp.arange(duplicate_workers, dtype=jnp.int32) * straggler_filter[:, 0])
    row_count = layer_inputs.shape[1] // duplicate_workers
    first_row = member * row_count
    qkv_full, out_full = (
        lax.all_gather(attention_projection_matrix, ("rep", "grp"), axis=0, tiled=True),
        lax.all_gather(merge_projection_transposed, ("rep", "grp"), axis=0, tiled=True),
    )
    projected_wide = jnp.dot(layer_inputs, qkv_full, preferred_element_type=jnp.float32)
    attn_wide = jnp.dot(loss_adjoint_matrix, out_full, preferred_element_type=jnp.float32)
    chosen_noise = from_root(dropout_factors[0], "rep", kept_worker)
    stacked, attended = token_grads(
        projected_wide, attn_wide, packed_sequence_labels[0], chosen_noise
    )
    gradient = weight_rows(
        layer_inputs, loss_adjoint_matrix, stacked, attended, first_row, row_count
    )
    return lax.psum_scatter(gradient, "grp", scatter_dimension=0, tiled=True)


def dot(a, b, dims):
    return lax.dot_general(a, b, (dims, ((), ())), preferred_element_type=jnp.float32)


VMEM = pl.BlockSpec(memory_space=pltpu.VMEM)
SMEM = pl.BlockSpec(memory_space=pltpu.SMEM)


def room(mebibytes):
    return pltpu.CompilerParams(vmem_limit_bytes=mebibytes << 20)


def cost(flops, count):
    return pl.CostEstimate(flops=flops, bytes_accessed=count, transcendentals=0)


def flip_kernel(order_ref, x_ref, keep_ref, send_ref, flipped):
    half = keep_ref.shape[0]
    blocks = order_ref.shape[0]
    rows = 2 * half // blocks
    width = x_ref.shape[1]
    for first in range(0, width, 256):
        flipped[pl.ds(first, 256), :] = x_ref[:, pl.ds(first, 256)].T
    for block in range(blocks):
        first = pl.multiple_of(order_ref[block] * rows, 16)
        target = keep_ref if block < blocks // 2 else send_ref
        place = (block % (blocks // 2)) * rows
        target[pl.ds(place, rows), :] = flipped[pl.ds(first, rows), :]


def flip(order, x):
    tokens, width = x.shape
    out = jax.ShapeDtypeStruct((width // 2, tokens), x.dtype)
    return pl.pallas_call(
        flip_kernel,
        out_shape=(out, out),
        in_specs=[SMEM, VMEM],
        out_specs=(VMEM, VMEM),
        scratch_shapes=[pltpu.VMEM((width, tokens), x.dtype)],
        cost_estimate=cost(0, 4 * x.size),
        compiler_params=room(10),
        name="flip",
    )(order, x)


def stack_kernel(pieces, *refs):
    sources, targets, sems = refs[:pieces], refs[pieces:-1], refs[-1]
    carried, targets = targets[: len(targets) // 2], targets[len(targets) // 2 :]
    copies = []
    first = 0
    for source in sources:
        rows = source.shape[0]
        copies.append((source, targets[0].at[pl.ds(first, rows), :]))
        first += rows
    copies += zip(carried, targets[1:])
    copies = [pltpu.make_async_copy(*ends, sems.at[n]) for n, ends in enumerate(copies)]
    for copy in copies:
        copy.start()
    for copy in copies:
        copy.wait()


def stack(pieces, carried=()):
    shape = (sum(p.shape[0] for p in pieces), pieces[0].shape[1])
    out = [jax.ShapeDtypeStruct(shape, pieces[0].dtype)]
    out += [jax.ShapeDtypeStruct(a.shape, a.dtype) for a in carried]
    moved = len(pieces) + len(carried)
    return pl.pallas_call(
        functools.partial(stack_kernel, len(pieces)),
        out_shape=out,
        in_specs=[pl.BlockSpec(memory_space=pl.ANY)] * moved,
        out_specs=[VMEM] * len(out),
        scratch_shapes=[pltpu.SemaphoreType.DMA((moved,))],
        cost_estimate=cost(0, 4 * sum(a.size for a in out)),
        compiler_params=room(6),
        name="stack",
    )(*pieces, *carried)


def one_on_other(a, b):
    zero = jnp.zeros((), a.dtype)
    above = lax.pad(a, zero, ((0, b.shape[0], 0), (0, 0, 0)))
    return above + lax.pad(b, zero, ((a.shape[0], 0, 0), (0, 0, 0)))


def forward_kernel(
    heads, member_ref, own_ref, other_ref, pair_ref, row_ref, column_ref, noise_ref,
    att_ref, probs_ref, parts_ref,
):
    tokens = own_ref.shape[0]
    size = pair_ref.shape[1]
    scale = 1.0 / math.sqrt(size)
    low = jnp.bfloat16

    def part(first):
        return (own_ref[:, pl.ds(first, size)] + other_ref[:, pl.ds(first, size)]).astype(low)

    first_member = member_ref[0] == 0
    mine = part(heads * size).astype(jnp.float32)
    pair = pair_ref[...].astype(jnp.float32)
    keys = jnp.where(first_member, mine, pair).astype(low)
    vals = jnp.where(first_member, pair, mine).astype(low)
    parts_ref[heads] = keys
    parts_ref[heads + 1] = vals
    query_at = lax.broadcasted_iota(jnp.int32, (tokens, tokens), 0)
    key_at = lax.broadcasted_iota(jnp.int32, (tokens, tokens), 1)
    allowed = (column_ref[...] == row_ref[...]) & (key_at <= query_at)
    for head in range(heads):
        query = part(head * size)
        parts_ref[head] = query
        scores = dot(query, keys, ((1,), (1,))) * scale
        scores = jnp.where(allowed, scores, -jnp.inf)
        expon = jnp.exp(scores - jnp.max(scores, axis=1, keepdims=True))
        probs = expon / jnp.sum(expon, axis=1, keepdims=True)
        probs_ref[head] = probs
        dropped = (probs * (1.0 + noise_ref[head].astype(jnp.float32))).astype(low)
        att_ref[:, pl.ds(head * size, size)] = dot(dropped, vals, ((1,), (0,))).astype(low)


def forward(member, own, other, pair, labels, noise):
    tokens, size = pair.shape
    heads = noise.shape[0]
    return pl.pallas_call(
        functools.partial(forward_kernel, heads),
        out_shape=(
            jax.ShapeDtypeStruct((tokens, heads * size), jnp.bfloat16),
            jax.ShapeDtypeStruct(noise.shape, jnp.float32),
            jax.ShapeDtypeStruct((heads + 2, tokens, size), jnp.bfloat16),
        ),
        in_specs=[SMEM] + [VMEM] * 6,
        out_specs=(VMEM,) * 3,
        cost_estimate=cost(4 * noise.size * size, 8 * own.size + 6 * noise.size),
        compiler_params=room(10),
        name="forward",
    )(member, own, other, pair, *labels, noise)


def backward_kernel(
    heads, member_ref, own_ref, other_ref, probs_ref, parts_ref, noise_ref, query_ref, keep_ref, send_ref
):
    tokens, size = keep_ref.shape
    scale = 1.0 / math.sqrt(size)
    low = jnp.bfloat16
    first_member = member_ref[0] == 0
    keys, vals = parts_ref[heads], parts_ref[heads + 1]
    key_grad = jnp.zeros((tokens, size), jnp.float32)
    val_grad = jnp.zeros((tokens, size), jnp.float32)
    for head in range(heads):
        here = pl.ds(head * size, size)
        query, grad = parts_ref[head], (own_ref[:, here] + other_ref[:, here]).astype(low)
        probs = probs_ref[head]
        factor = 1.0 + noise_ref[head].astype(jnp.float32)
        dropped = (probs * factor).astype(low)
        val_grad += dot(dropped, grad, ((0,), (0,)))
        prob_grad = dot(grad, vals, ((1,), (1,))) * factor
        inner = jnp.sum(probs * prob_grad, axis=1, keepdims=True)
        score_grad = (probs * (prob_grad - inner) * scale).astype(low)
        query_ref[:, here] = dot(score_grad, keys, ((1,), (0,))).astype(low)
        key_grad += dot(score_grad, query, ((0,), (0,)))
    keep_ref[...] = jnp.where(first_member, key_grad, val_grad)
    send_ref[...] = jnp.where(first_member, val_grad, key_grad)


def backward(member, own, other, probs, parts, noise):
    heads, tokens, _ = noise.shape
    size = parts.shape[2]
    narrow = jax.ShapeDtypeStruct((tokens, size), jnp.float32)
    return pl.pallas_call(
        functools.partial(backward_kernel, heads),
        out_shape=(jax.ShapeDtypeStruct((tokens, heads * size), jnp.bfloat16), narrow, narrow),
        in_specs=[SMEM] + [VMEM] * 5,
        out_specs=(VMEM,) * 3,
        cost_estimate=cost(8 * noise.size * size, 6 * noise.size),
        compiler_params=room(10),
        name="backward",
    )(member, own, other, probs, parts, noise)


def gather_kernel(runs, *refs):
    sources, out_ref = refs[:-1], refs[-1]
    place = 0
    for source, (first, rows) in zip(sources, runs):
        out_ref[pl.ds(place, rows), :] = source[pl.ds(first, rows), :].astype(out_ref.dtype)
        place += rows


def gather_rows(*runs):
    arrays = [array for array, _, _ in runs]
    shape = (sum(rows for _, _, rows in runs), arrays[0].shape[1])
    return pl.pallas_call(
        functools.partial(gather_kernel, [(first, rows) for _, first, rows in runs]),
        out_shape=jax.ShapeDtypeStruct(shape, jnp.bfloat16),
        in_specs=[VMEM] * len(arrays),
        out_specs=VMEM,
        cost_estimate=cost(0, 4 * shape[0] * shape[1]),
        compiler_params=room(4),
        name="gather",
    )(*arrays)


def place_kernel(terms, member_ref, *refs):
    sources, out_ref = list(refs[:-1]), refs[-1]
    rows = out_ref.shape[0]
    columns = [[(sources.pop(0), first) for first in firsts] for firsts in terms]

    def put(order):
        place = 0
        for pair in range(0, len(columns), 2):
            for n in order:
                values = sum(
                    source[pl.ds(first, rows), :].astype(out_ref.dtype)
                    for source, first in columns[pair + n]
                )
                out_ref[:, pl.ds(place, values.shape[1])] = values
                place += values.shape[1]

    @pl.when(member_ref[0] == 0)
    def _():
        put((0, 1))

    @pl.when(member_ref[0] != 0)
    def _():
        put((1, 0))


def place_columns(member, rows, *pieces):
    terms = [[first for _, first in piece] for piece in pieces]
    arrays = [array for piece in pieces for array, _ in piece]
    shape = (rows, sum(piece[0][0].shape[1] for piece in pieces))
    return pl.pallas_call(
        functools.partial(place_kernel, terms),
        out_shape=jax.ShapeDtypeStruct(shape, jnp.float32),
        in_specs=[SMEM] + [VMEM] * len(arrays),
        out_specs=VMEM,
        cost_estimate=cost(0, 8 * shape[0] * shape[1]),
        compiler_params=room(4),
        name="place",
    )(member, *arrays)


def paired_device(
    layer_inputs,
    loss_adjoint_matrix,
    attention_projection_matrix,
    merge_projection_transposed,
    packed_sequence_labels,
    dropout_factors,
    straggler_filter,
):
    grp = lax.axis_size("grp")
    member = lax.axis_index("rep")
    me = member * grp + lax.axis_index("grp")
    first = member == 0
    core, side, near, far = 1, 2, 4, 8

    def across(a, bit):
        return lax.ppermute(a, "grp", [(g, g ^ bit) for g in range(grp)])

    def across_rep(a):
        return lax.ppermute(a, "rep", [(0, 1), (1, 0)])

    heads, tokens = dropout_factors.shape[2], dropout_factors.shape[3]
    share = heads // 2
    width = merge_projection_transposed.shape[1]
    size = width // heads
    part = share * size

    def columns(a, first, count, m):
        return lax.dynamic_slice_in_dim(a, first + m * count, count, 1)

    def qkv_columns(m):
        queries = columns(attention_projection_matrix, 0, part, m)
        return jnp.concatenate(
            [queries, columns(attention_projection_matrix, width, size, m)], axis=1
        )

    def merge_columns(m):
        return columns(merge_projection_transposed, 0, part, m)

    def exchanged(pick):
        return one_on_other(pick(member), across_rep(pick(1 - member)))

    qkv = exchanged(qkv_columns)
    merge = exchanged(merge_columns)

    qkv_near, qkv_far = across(qkv, near), across(qkv, far)
    qkv_both = across(qkv_far, near)
    qkv_side = [
        across(qkv, side), across(qkv_far, side), across(qkv_near, side), across(qkv_both, side)
    ]
    merge_far = across(merge, far)
    merge_line = one_on_other(merge, merge_far)
    merge_near = across(merge_line, near)
    merge_pieces = [merge_line, merge_near, across(merge_line, side), across(merge_near, side)]

    def order(bits):
        found = [0]
        for bit in (core, *bits, grp):
            found = [at | b for at in found for b in (0, bit)]
        return jnp.array(found, jnp.int32) ^ me

    stages = ((near, side, far), (side, near, far))
    x_keep, x_send = flip(order(stages[0]), layer_inputs)
    y_keep, y_send = flip(order(stages[1]), loss_adjoint_matrix)
    x_other, y_other = across(x_send, core), across(y_send, core)

    def as_it_lies(a):
        return with_layout_constraint(a, Layout(major_to_minor=tuple(range(a.ndim))))

    noise = as_it_lies(across_rep(dropout_factors))

    def project(rows, weights):
        return dot(rows, weights, ((0,), (0,)))

    pieces = [qkv, qkv_far, *qkv_side[:2], qkv_near, qkv_both, qkv_side[2]]
    (early,) = stack(pieces)
    cut = early.shape[0]
    away = project(x_other[:cut], early)
    qkv_in = across(away + project(x_other[cut:], qkv_side[3]), core)
    own = project(x_keep[:cut], early)
    qkv_own = own + project(x_keep[cut:], qkv_side[3])
    merge_rows, y_other = stack(merge_pieces, (y_other,))
    merge_in = across(project(y_other, merge_rows), core)
    merge_own = project(y_keep, merge_rows)

    pair = (qkv_own[:, part:] + qkv_in[:, part:]).astype(jnp.bfloat16)
    pair, noise = lax.optimization_barrier((pair, noise))
    pair = across_rep(pair)
    kept_worker = jnp.sum(jnp.arange(2, dtype=jnp.int32) * straggler_filter[:, 0])
    labels = (packed_sequence_labels, packed_sequence_labels.reshape(tokens, 1))
    noise = jnp.where(kept_worker == member, dropout_factors, noise)[0]
    noise = jnp.where(first, noise[:, :share], noise[:, share:])
    noise_used = jnp.transpose(noise, (1, 0, 2))
    member = member.reshape(1)
    att, probs, pieces = forward(member, qkv_own, qkv_in, pair, labels, noise_used)
    query_grad, pair_keep, pair_send = backward(
        member, merge_own, merge_in, probs, pieces, noise_used
    )
    pair_grad = (pair_keep + across_rep(pair_send)).astype(jnp.bfloat16)

    def first_two_exchanged(rows):
        halves = rows.reshape(2, 2, rows.shape[0] // 4, rows.shape[1])
        return jnp.swapaxes(halves, 0, 1).reshape(rows.shape)

    def reduced(name, keep, other, bits, grad, theirs):
        cut = keep.shape[0] // 2

        def half(rows):
            return dot(keep[rows], grad, ((1,), (0,))), other[rows]

        leaves, rows = half(slice(cut, None))
        leaves = (leaves + dot(rows, theirs, ((1,), (0,)))).astype(jnp.bfloat16)
        total, rows = half(slice(None, cut))
        for n, bit in enumerate(bits):
            arrived = across(leaves, bit)
            if n == 0:
                total = total + dot(rows, theirs, ((1,), (0,)))
            total = total + arrived.astype(jnp.float32)
            whole = total
            if n < len(bits) - 1 or name != "q":
                cut = total.shape[0] // 2
                leaves, total = total[cut:].astype(jnp.bfloat16), total[:cut]
        return whole, leaves

    def swapped_last(name, keep, other, bits, grad, theirs):
        whole, leaves = reduced(name, keep, other, bits, grad, theirs)
        swapped = across_rep(leaves)
        return ((whole, 0),), ((swapped, 0),)

    def swapped_first(name, keep, other, bits, grad, theirs):
        whole, _ = reduced(name, keep, other, bits[:-1], grad, theirs)
        rows, count = whole.shape[0] // 4, whole.shape[1]
        leaves = whole.reshape(2, 2, rows, count)[:, 1].astype(jnp.bfloat16)
        leaves = leaves.reshape(2 * rows, count)
        partner = across_rep(leaves)
        leaves = gather_rows((whole, 2 * rows, rows), (partner, rows, rows))
        arrived = across(leaves, bits[-1])
        return ((whole, 0), (arrived, 0)), ((partner, 0), (arrived, rows))

    merge = swapped_last("m", y_keep, y_other, stages[1], att, across(att, core))
    query = swapped_first("q", x_keep, x_other, stages[0], query_grad, across(query_grad, core))
    x_keep, x_other = first_two_exchanged(x_keep), first_two_exchanged(x_other)
    pair = swapped_last("p", x_keep, x_other, (side, near, far), pair_grad, across(pair_grad, core))
    rows = attention_projection_matrix.shape[0]
    return place_columns(member, rows, *query, *pair, *merge)


def paired(mesh, shapes):
    rep, grp = mesh.shape["rep"], mesh.shape["grp"]
    depth, heads, tokens = shapes[0][1], shapes[5][2], shapes[5][3]
    size = shapes[3][1] // heads
    even = depth % (rep * grp * 16) == 0 and depth % 256 == 0
    return rep == 2 and grp == 16 and even and heads % 2 == 0 and size % 128 == 0 and tokens % 128 == 0


def solution(mesh):
    placed = (
        P("grp", None),
        P("grp", None),
        P(("rep", "grp"), None),
        P(("rep", "grp"), None),
        P("grp", None),
        P("rep", "grp", None, None),
        P(None, "grp"),
    )

    def on_devices(body):
        return jax.shard_map(
            body, mesh=mesh, in_specs=placed, out_specs=P(("rep", "grp"), None), check_vma=False
        )

    def step(*args):
        if not paired(mesh, [a.shape for a in args]):
            return on_devices(generic_device)(*args)
        return on_devices(paired_device)(*args)

    return step
```

```python
import functools
import math

import jax
import jax.numpy as jnp
from jax import lax
from jax.experimental import pallas as pl
from jax.experimental.layout import Layout, with_layout_constraint
from jax.experimental.pallas import tpu as pltpu
from jax.sharding import PartitionSpec as P


def from_root(block, axis, holder):
    block = jnp.where(lax.axis_index(axis) == holder, block, jnp.zeros_like(block))
    return lax.psum(block, axis)


def token_grads(projected_wide, attn_wide, doc_row, noise_rows):
    seq_len = projected_wide.shape[0]
    head_size = (projected_wide.shape[1] - attn_wide.shape[1]) // 2
    heads = attn_wide.shape[1] // head_size
    score_scale = 1.0 / jnp.sqrt(jnp.float32(head_size))
    projected = projected_wide.astype(jnp.bfloat16)
    queries = projected[:, : heads * head_size]
    key_rows = projected[:, heads * head_size : (heads + 1) * head_size]
    val_rows = projected[:, (heads + 1) * head_size :]
    query_heads = queries.reshape(seq_len, heads, head_size).astype(jnp.float32)
    keys_wide = key_rows.astype(jnp.float32)
    vals_wide = val_rows.astype(jnp.float32)
    position = jnp.arange(seq_len, dtype=jnp.int32)
    allowed = (doc_row[:, None] == doc_row[None, :]) & (position[None, :] <= position[:, None])
    scores = jnp.einsum("ihd,jd->hij", query_heads, keys_wide) * score_scale
    scores = jnp.where(allowed[None], scores, -jnp.inf)
    highest = jnp.max(scores, axis=2, keepdims=True)
    expon = jnp.exp(scores - highest)
    attn_probs = expon / jnp.sum(expon, axis=2, keepdims=True)
    factor = 1.0 + jnp.transpose(noise_rows.astype(jnp.float32), (1, 0, 2))
    dropped = (attn_probs * factor).astype(jnp.bfloat16)
    dropped_wide = dropped.astype(jnp.float32)
    attended = (
        jnp.einsum("hij,jd->ihd", dropped_wide, vals_wide)
        .astype(jnp.bfloat16)
        .reshape(seq_len, heads * head_size)
    )
    attn_grad = attn_wide.astype(jnp.bfloat16)
    grad_heads = attn_grad.reshape(seq_len, heads, head_size).astype(jnp.float32)
    val_grad = jnp.einsum("hij,ihd->jd", dropped_wide, grad_heads).astype(jnp.bfloat16)
    prob_grad = jnp.einsum("ihd,jd->hij", grad_heads, vals_wide) * factor
    inner = jnp.sum(attn_probs * prob_grad, axis=2, keepdims=True)
    score_grad = (attn_probs * (prob_grad - inner) * score_scale).astype(jnp.bfloat16)
    score_wide = score_grad.astype(jnp.float32)
    query_grad = (
        jnp.einsum("hij,jd->ihd", score_wide, keys_wide)
        .astype(jnp.bfloat16)
        .reshape(seq_len, heads * head_size)
    )
    key_grad = jnp.einsum("hij,ihd->jd", score_wide, query_heads).astype(jnp.bfloat16)
    stacked = jnp.concatenate([query_grad, key_grad, val_grad], axis=1)
    return (stacked, attended)


def weight_rows(hidden_rows, cot_rows, stacked, attended, first_row, row_count):
    hidden_cols = lax.dynamic_slice_in_dim(hidden_rows, first_row, row_count, 1)
    cot_cols = lax.dynamic_slice_in_dim(cot_rows, first_row, row_count, 1)
    proj_grad = jnp.dot(hidden_cols.T, stacked, preferred_element_type=jnp.float32)
    out_grad = jnp.dot(cot_cols.T, attended, preferred_element_type=jnp.float32)
    return jnp.concatenate([proj_grad, out_grad], axis=1)


def generic_device(
    layer_inputs,
    loss_adjoint_matrix,
    attention_projection_matrix,
    merge_projection_transposed,
    packed_sequence_labels,
    dropout_factors,
    straggler_filter,
):
    duplicate_workers = lax.axis_size("rep")
    member = lax.axis_index("rep")
    kept_worker = jnp.sum(jnp.arange(duplicate_workers, dtype=jnp.int32) * straggler_filter[:, 0])
    row_count = layer_inputs.shape[1] // duplicate_workers
    first_row = member * row_count
    qkv_full, out_full = (
        lax.all_gather(attention_projection_matrix, ("rep", "grp"), axis=0, tiled=True),
        lax.all_gather(merge_projection_transposed, ("rep", "grp"), axis=0, tiled=True),
    )
    projected_wide = jnp.dot(layer_inputs, qkv_full, preferred_element_type=jnp.float32)
    attn_wide = jnp.dot(loss_adjoint_matrix, out_full, preferred_element_type=jnp.float32)
    chosen_noise = from_root(dropout_factors[0], "rep", kept_worker)
    stacked, attended = token_grads(
        projected_wide, attn_wide, packed_sequence_labels[0], chosen_noise
    )
    gradient = weight_rows(
        layer_inputs, loss_adjoint_matrix, stacked, attended, first_row, row_count
    )
    return lax.psum_scatter(gradient, "grp", scatter_dimension=0, tiled=True)


def dot(a, b, dims):
    return lax.dot_general(a, b, (dims, ((), ())), preferred_element_type=jnp.float32)


VMEM = pl.BlockSpec(memory_space=pltpu.VMEM)
SMEM = pl.BlockSpec(memory_space=pltpu.SMEM)


def room(mebibytes):
    return pltpu.CompilerParams(vmem_limit_bytes=mebibytes << 20)


def cost(flops, count):
    return pl.CostEstimate(flops=flops, bytes_accessed=count, transcendentals=0)


def flip_kernel(order_ref, x_ref, keep_ref, send_ref, flipped):
    half = keep_ref.shape[0]
    blocks = order_ref.shape[0]
    rows = 2 * half // blocks
    width = x_ref.shape[1]
    for first in range(0, width, 256):
        flipped[pl.ds(first, 256), :] = x_ref[:, pl.ds(first, 256)].T
    for block in range(blocks):
        first = pl.multiple_of(order_ref[block] * rows, 16)
        target = keep_ref if block < blocks // 2 else send_ref
        place = (block % (blocks // 2)) * rows
        target[pl.ds(place, rows), :] = flipped[pl.ds(first, rows), :]


def flip(order, x):
    tokens, width = x.shape
    out = jax.ShapeDtypeStruct((width // 2, tokens), x.dtype)
    return pl.pallas_call(
        flip_kernel,
        out_shape=(out, out),
        in_specs=[SMEM, VMEM],
        out_specs=(VMEM, VMEM),
        scratch_shapes=[pltpu.VMEM((width, tokens), x.dtype)],
        cost_estimate=cost(0, 4 * x.size),
        compiler_params=room(10),
        name="flip",
    )(order, x)


def stack_kernel(pieces, *refs):
    sources, targets, sems = refs[:pieces], refs[pieces:-1], refs[-1]
    carried, targets = targets[: len(targets) // 2], targets[len(targets) // 2 :]
    copies = []
    first = 0
    for source in sources:
        rows = source.shape[0]
        copies.append((source, targets[0].at[pl.ds(first, rows), :]))
        first += rows
    copies += zip(carried, targets[1:])
    copies = [pltpu.make_async_copy(*ends, sems.at[n]) for n, ends in enumerate(copies)]
    for copy in copies:
        copy.start()
    for copy in copies:
        copy.wait()


def stack(pieces, carried=()):
    shape = (sum(p.shape[0] for p in pieces), pieces[0].shape[1])
    out = [jax.ShapeDtypeStruct(shape, pieces[0].dtype)]
    out += [jax.ShapeDtypeStruct(a.shape, a.dtype) for a in carried]
    moved = len(pieces) + len(carried)
    return pl.pallas_call(
        functools.partial(stack_kernel, len(pieces)),
        out_shape=out,
        in_specs=[pl.BlockSpec(memory_space=pl.ANY)] * moved,
        out_specs=[VMEM] * len(out),
        scratch_shapes=[pltpu.SemaphoreType.DMA((moved,))],
        cost_estimate=cost(0, 4 * sum(a.size for a in out)),
        compiler_params=room(6),
        name="stack",
    )(*pieces, *carried)


def pick_kernel(groups, member_ref, source_ref, mine_ref, theirs_ref):
    def put(target, m):
        place = 0
        for first, count in groups:
            target[:, pl.ds(place, count)] = source_ref[:, pl.ds(first + m * count, count)]
            place += count

    @pl.when(member_ref[0] == 0)
    def _():
        put(theirs_ref, 1)
        put(mine_ref, 0)

    @pl.when(member_ref[0] != 0)
    def _():
        put(theirs_ref, 0)
        put(mine_ref, 1)


def pick_columns(member, a, groups):
    out = jax.ShapeDtypeStruct((a.shape[0], sum(count for _, count in groups)), a.dtype)
    return pl.pallas_call(
        functools.partial(pick_kernel, groups),
        out_shape=(out, out),
        in_specs=[SMEM, VMEM],
        out_specs=(VMEM, VMEM),
        cost_estimate=cost(0, 4 * a.size),
        compiler_params=room(2),
        name="pick",
    )(member, a)


def one_on_other(a, b):
    zero = jnp.zeros((), a.dtype)
    above = lax.pad(a, zero, ((0, b.shape[0], 0), (0, 0, 0)))
    return above + lax.pad(b, zero, ((a.shape[0], 0, 0), (0, 0, 0)))


def forward_kernel(
    heads, member_ref, own_ref, other_ref, pair_ref, row_ref, column_ref, noise_ref,
    att_ref, probs_ref, parts_ref,
):
    tokens = own_ref.shape[0]
    size = pair_ref.shape[1]
    scale = 1.0 / math.sqrt(size)
    low = jnp.bfloat16

    def part(first):
        return (own_ref[:, pl.ds(first, size)] + other_ref[:, pl.ds(first, size)]).astype(low)

    first_member = member_ref[0] == 0
    mine = part(heads * size).astype(jnp.float32)
    pair = pair_ref[...].astype(jnp.float32)
    keys = jnp.where(first_member, mine, pair).astype(low)
    vals = jnp.where(first_member, pair, mine).astype(low)
    parts_ref[heads] = keys
    parts_ref[heads + 1] = vals
    query_at = lax.broadcasted_iota(jnp.int32, (tokens, tokens), 0)
    key_at = lax.broadcasted_iota(jnp.int32, (tokens, tokens), 1)
    allowed = (column_ref[...] == row_ref[...]) & (key_at <= query_at)
    for head in range(heads):
        query = part(head * size)
        parts_ref[head] = query
        scores = dot(query, keys, ((1,), (1,))) * scale
        scores = jnp.where(allowed, scores, -jnp.inf)
        expon = jnp.exp(scores - jnp.max(scores, axis=1, keepdims=True))
        probs = expon / jnp.sum(expon, axis=1, keepdims=True)
        probs_ref[head] = probs
        dropped = (probs * (1.0 + noise_ref[head].astype(jnp.float32))).astype(low)
        att_ref[:, pl.ds(head * size, size)] = dot(dropped, vals, ((1,), (0,))).astype(low)


def forward(member, own, other, pair, labels, noise):
    tokens, size = pair.shape
    heads = noise.shape[0]
    return pl.pallas_call(
        functools.partial(forward_kernel, heads),
        out_shape=(
            jax.ShapeDtypeStruct((tokens, heads * size), jnp.bfloat16),
            jax.ShapeDtypeStruct(noise.shape, jnp.float32),
            jax.ShapeDtypeStruct((heads + 2, tokens, size), jnp.bfloat16),
        ),
        in_specs=[SMEM] + [VMEM] * 6,
        out_specs=(VMEM,) * 3,
        cost_estimate=cost(4 * noise.size * size, 8 * own.size + 6 * noise.size),
        compiler_params=room(10),
        name="forward",
    )(member, own, other, pair, *labels, noise)


def backward_kernel(
    heads, member_ref, own_ref, other_ref, probs_ref, parts_ref, noise_ref, query_ref, keep_ref, send_ref
):
    tokens, size = keep_ref.shape
    scale = 1.0 / math.sqrt(size)
    low = jnp.bfloat16
    first_member = member_ref[0] == 0
    keys, vals = parts_ref[heads], parts_ref[heads + 1]
    key_grad = jnp.zeros((tokens, size), jnp.float32)
    val_grad = jnp.zeros((tokens, size), jnp.float32)
    for head in range(heads):
        here = pl.ds(head * size, size)
        query, grad = parts_ref[head], (own_ref[:, here] + other_ref[:, here]).astype(low)
        probs = probs_ref[head]
        factor = 1.0 + noise_ref[head].astype(jnp.float32)
        dropped = (probs * factor).astype(low)
        val_grad += dot(dropped, grad, ((0,), (0,)))
        prob_grad = dot(grad, vals, ((1,), (1,))) * factor
        inner = jnp.sum(probs * prob_grad, axis=1, keepdims=True)
        score_grad = (probs * (prob_grad - inner) * scale).astype(low)
        query_ref[:, here] = dot(score_grad, keys, ((1,), (0,))).astype(low)
        key_grad += dot(score_grad, query, ((0,), (0,)))
    keep_ref[...] = jnp.where(first_member, key_grad, val_grad)
    send_ref[...] = jnp.where(first_member, val_grad, key_grad)


def backward(member, own, other, probs, parts, noise):
    heads, tokens, _ = noise.shape
    size = parts.shape[2]
    narrow = jax.ShapeDtypeStruct((tokens, size), jnp.float32)
    return pl.pallas_call(
        functools.partial(backward_kernel, heads),
        out_shape=(jax.ShapeDtypeStruct((tokens, heads * size), jnp.bfloat16), narrow, narrow),
        in_specs=[SMEM] + [VMEM] * 5,
        out_specs=(VMEM,) * 3,
        cost_estimate=cost(8 * noise.size * size, 6 * noise.size),
        compiler_params=room(10),
        name="backward",
    )(member, own, other, probs, parts, noise)


def gather_kernel(runs, *refs):
    sources, out_ref = refs[:-1], refs[-1]
    place = 0
    for source, (first, rows) in zip(sources, runs):
        out_ref[pl.ds(place, rows), :] = source[pl.ds(first, rows), :].astype(out_ref.dtype)
        place += rows


def gather_rows(*runs):
    arrays = [array for array, _, _ in runs]
    shape = (sum(rows for _, _, rows in runs), arrays[0].shape[1])
    return pl.pallas_call(
        functools.partial(gather_kernel, [(first, rows) for _, first, rows in runs]),
        out_shape=jax.ShapeDtypeStruct(shape, jnp.bfloat16),
        in_specs=[VMEM] * len(arrays),
        out_specs=VMEM,
        cost_estimate=cost(0, 4 * shape[0] * shape[1]),
        compiler_params=room(4),
        name="gather",
    )(*arrays)


def place_kernel(terms, member_ref, *refs):
    sources, out_ref = list(refs[:-1]), refs[-1]
    rows = out_ref.shape[0]
    columns = [[(sources.pop(0), first) for first in firsts] for firsts in terms]

    def put(order):
        place = 0
        for pair in range(0, len(columns), 2):
            for n in order:
                values = sum(
                    source[pl.ds(first, rows), :].astype(out_ref.dtype)
                    for source, first in columns[pair + n]
                )
                out_ref[:, pl.ds(place, values.shape[1])] = values
                place += values.shape[1]

    @pl.when(member_ref[0] == 0)
    def _():
        put((0, 1))

    @pl.when(member_ref[0] != 0)
    def _():
        put((1, 0))


def place_columns(member, rows, *pieces):
    terms = [[first for _, first in piece] for piece in pieces]
    arrays = [array for piece in pieces for array, _ in piece]
    shape = (rows, sum(piece[0][0].shape[1] for piece in pieces))
    return pl.pallas_call(
        functools.partial(place_kernel, terms),
        out_shape=jax.ShapeDtypeStruct(shape, jnp.float32),
        in_specs=[SMEM] + [VMEM] * len(arrays),
        out_specs=VMEM,
        cost_estimate=cost(0, 8 * shape[0] * shape[1]),
        compiler_params=room(4),
        name="place",
    )(member, *arrays)


def paired_device(
    layer_inputs,
    loss_adjoint_matrix,
    attention_projection_matrix,
    merge_projection_transposed,
    packed_sequence_labels,
    dropout_factors,
    straggler_filter,
):
    grp = lax.axis_size("grp")
    member = lax.axis_index("rep")
    me = member * grp + lax.axis_index("grp")
    first = member == 0
    core, side, near, far = 1, 2, 4, 8

    def across(a, bit):
        return lax.ppermute(a, "grp", [(g, g ^ bit) for g in range(grp)])

    def across_rep(a):
        return lax.ppermute(a, "rep", [(0, 1), (1, 0)])

    heads, tokens = dropout_factors.shape[2], dropout_factors.shape[3]
    share = heads // 2
    width = merge_projection_transposed.shape[1]
    size = width // heads
    part = share * size

    qkv, theirs = pick_columns(
        member.reshape(1), attention_projection_matrix, ((0, part), (width, size))
    )
    qkv = one_on_other(qkv, across_rep(theirs))

    def merge_columns(m):
        return lax.dynamic_slice_in_dim(merge_projection_transposed, m * part, part, 1)

    merge = one_on_other(merge_columns(member), across_rep(merge_columns(1 - member)))

    qkv_near, qkv_far = across(qkv, near), across(qkv, far)
    qkv_both = across(qkv_far, near)
    qkv_side = [
        across(qkv, side), across(qkv_far, side), across(qkv_near, side), across(qkv_both, side)
    ]
    merge_far = across(merge, far)
    merge_line = one_on_other(merge, merge_far)
    merge_near = across(merge_line, near)
    merge_pieces = [merge_line, merge_near, across(merge_line, side), across(merge_near, side)]

    def order(bits):
        found = [0]
        for bit in (core, *bits, grp):
            found = [at | b for at in found for b in (0, bit)]
        return jnp.array(found, jnp.int32) ^ me

    stages = ((near, side, far), (side, near, far))
    x_keep, x_send = flip(order(stages[0]), layer_inputs)
    y_keep, y_send = flip(order(stages[1]), loss_adjoint_matrix)
    x_other, y_other = across(x_send, core), across(y_send, core)

    def as_it_lies(a):
        return with_layout_constraint(a, Layout(major_to_minor=tuple(range(a.ndim))))

    noise = as_it_lies(across_rep(dropout_factors))

    def project(rows, weights):
        return dot(rows, weights, ((0,), (0,)))

    pieces = [qkv, qkv_far, *qkv_side[:2], qkv_near, qkv_both, qkv_side[2]]
    (early,) = stack(pieces)
    cut = early.shape[0]
    away = project(x_other[:cut], early)
    qkv_in = across(away + project(x_other[cut:], qkv_side[3]), core)
    own = project(x_keep[:cut], early)
    qkv_own = own + project(x_keep[cut:], qkv_side[3])
    merge_rows, y_other = stack(merge_pieces, (y_other,))
    merge_in = across(project(y_other, merge_rows), core)
    merge_own = project(y_keep, merge_rows)

    pair = (qkv_own[:, part:] + qkv_in[:, part:]).astype(jnp.bfloat16)
    pair, noise = lax.optimization_barrier((pair, noise))
    pair = across_rep(pair)
    kept_worker = jnp.sum(jnp.arange(2, dtype=jnp.int32) * straggler_filter[:, 0])
    labels = (packed_sequence_labels, packed_sequence_labels.reshape(tokens, 1))
    noise = jnp.where(kept_worker == member, dropout_factors, noise)[0]
    noise = jnp.where(first, noise[:, :share], noise[:, share:])
    noise_used = jnp.transpose(noise, (1, 0, 2))
    member = member.reshape(1)
    att, probs, pieces = forward(member, qkv_own, qkv_in, pair, labels, noise_used)
    query_grad, pair_keep, pair_send = backward(
        member, merge_own, merge_in, probs, pieces, noise_used
    )
    pair_grad = (pair_keep + across_rep(pair_send)).astype(jnp.bfloat16)

    def first_two_exchanged(rows):
        halves = rows.reshape(2, 2, rows.shape[0] // 4, rows.shape[1])
        return jnp.swapaxes(halves, 0, 1).reshape(rows.shape)

    def reduced(name, keep, other, bits, grad, theirs):
        cut = keep.shape[0] // 2

        def half(rows):
            return dot(keep[rows], grad, ((1,), (0,))), other[rows]

        leaves, rows = half(slice(cut, None))
        leaves = (leaves + dot(rows, theirs, ((1,), (0,)))).astype(jnp.bfloat16)
        total, rows = half(slice(None, cut))
        for n, bit in enumerate(bits):
            arrived = across(leaves, bit)
            if n == 0:
                total = total + dot(rows, theirs, ((1,), (0,)))
            total = total + arrived.astype(jnp.float32)
            whole = total
            if n < len(bits) - 1 or name != "q":
                cut = total.shape[0] // 2
                leaves, total = total[cut:].astype(jnp.bfloat16), total[:cut]
        return whole, leaves

    def swapped_last(name, keep, other, bits, grad, theirs):
        whole, leaves = reduced(name, keep, other, bits, grad, theirs)
        swapped = across_rep(leaves)
        return ((whole, 0),), ((swapped, 0),)

    def swapped_first(name, keep, other, bits, grad, theirs):
        whole, _ = reduced(name, keep, other, bits[:-1], grad, theirs)
        rows, count = whole.shape[0] // 4, whole.shape[1]
        leaves = whole.reshape(2, 2, rows, count)[:, 1].astype(jnp.bfloat16)
        leaves = leaves.reshape(2 * rows, count)
        partner = across_rep(leaves)
        leaves = gather_rows((whole, 2 * rows, rows), (partner, rows, rows))
        arrived = across(leaves, bits[-1])
        return ((whole, 0), (arrived, 0)), ((partner, 0), (arrived, rows))

    merge = swapped_last("m", y_keep, y_other, stages[1], att, across(att, core))
    query = swapped_first("q", x_keep, x_other, stages[0], query_grad, across(query_grad, core))
    x_keep, x_other = first_two_exchanged(x_keep), first_two_exchanged(x_other)
    pair = swapped_last("p", x_keep, x_other, (side, near, far), pair_grad, across(pair_grad, core))
    rows = attention_projection_matrix.shape[0]
    return place_columns(member, rows, *query, *pair, *merge)


def paired(mesh, shapes):
    rep, grp = mesh.shape["rep"], mesh.shape["grp"]
    depth, heads, tokens = shapes[0][1], shapes[5][2], shapes[5][3]
    size = shapes[3][1] // heads
    even = depth % (rep * grp * 16) == 0 and depth % 256 == 0
    return rep == 2 and grp == 16 and even and heads % 2 == 0 and size % 128 == 0 and tokens % 128 == 0


def solution(mesh):
    placed = (
        P("grp", None),
        P("grp", None),
        P(("rep", "grp"), None),
        P(("rep", "grp"), None),
        P("grp", None),
        P("rep", "grp", None, None),
        P(None, "grp"),
    )

    def on_devices(body):
        return jax.shard_map(
            body, mesh=mesh, in_specs=placed, out_specs=P(("rep", "grp"), None), check_vma=False
        )

    def step(*args):
        if not paired(mesh, [a.shape for a in args]):
            return on_devices(generic_device)(*args)
        return on_devices(paired_device)(*args)

    return step
```

```python
import functools
import math

import jax
import jax.numpy as jnp
from jax import lax
from jax.experimental import pallas as pl
from jax.experimental.layout import Layout, with_layout_constraint
from jax.experimental.pallas import tpu as pltpu
from jax.sharding import PartitionSpec as P


def from_root(block, axis, holder):
    block = jnp.where(lax.axis_index(axis) == holder, block, jnp.zeros_like(block))
    return lax.psum(block, axis)


def token_grads(projected_wide, attn_wide, doc_row, noise_rows):
    seq_len = projected_wide.shape[0]
    head_size = (projected_wide.shape[1] - attn_wide.shape[1]) // 2
    heads = attn_wide.shape[1] // head_size
    score_scale = 1.0 / jnp.sqrt(jnp.float32(head_size))
    projected = projected_wide.astype(jnp.bfloat16)
    queries = projected[:, : heads * head_size]
    key_rows = projected[:, heads * head_size : (heads + 1) * head_size]
    val_rows = projected[:, (heads + 1) * head_size :]
    query_heads = queries.reshape(seq_len, heads, head_size).astype(jnp.float32)
    keys_wide = key_rows.astype(jnp.float32)
    vals_wide = val_rows.astype(jnp.float32)
    position = jnp.arange(seq_len, dtype=jnp.int32)
    allowed = (doc_row[:, None] == doc_row[None, :]) & (position[None, :] <= position[:, None])
    scores = jnp.einsum("ihd,jd->hij", query_heads, keys_wide) * score_scale
    scores = jnp.where(allowed[None], scores, -jnp.inf)
    highest = jnp.max(scores, axis=2, keepdims=True)
    expon = jnp.exp(scores - highest)
    attn_probs = expon / jnp.sum(expon, axis=2, keepdims=True)
    factor = 1.0 + jnp.transpose(noise_rows.astype(jnp.float32), (1, 0, 2))
    dropped = (attn_probs * factor).astype(jnp.bfloat16)
    dropped_wide = dropped.astype(jnp.float32)
    attended = (
        jnp.einsum("hij,jd->ihd", dropped_wide, vals_wide)
        .astype(jnp.bfloat16)
        .reshape(seq_len, heads * head_size)
    )
    attn_grad = attn_wide.astype(jnp.bfloat16)
    grad_heads = attn_grad.reshape(seq_len, heads, head_size).astype(jnp.float32)
    val_grad = jnp.einsum("hij,ihd->jd", dropped_wide, grad_heads).astype(jnp.bfloat16)
    prob_grad = jnp.einsum("ihd,jd->hij", grad_heads, vals_wide) * factor
    inner = jnp.sum(attn_probs * prob_grad, axis=2, keepdims=True)
    score_grad = (attn_probs * (prob_grad - inner) * score_scale).astype(jnp.bfloat16)
    score_wide = score_grad.astype(jnp.float32)
    query_grad = (
        jnp.einsum("hij,jd->ihd", score_wide, keys_wide)
        .astype(jnp.bfloat16)
        .reshape(seq_len, heads * head_size)
    )
    key_grad = jnp.einsum("hij,ihd->jd", score_wide, query_heads).astype(jnp.bfloat16)
    stacked = jnp.concatenate([query_grad, key_grad, val_grad], axis=1)
    return (stacked, attended)


def weight_rows(hidden_rows, cot_rows, stacked, attended, first_row, row_count):
    hidden_cols = lax.dynamic_slice_in_dim(hidden_rows, first_row, row_count, 1)
    cot_cols = lax.dynamic_slice_in_dim(cot_rows, first_row, row_count, 1)
    proj_grad = jnp.dot(hidden_cols.T, stacked, preferred_element_type=jnp.float32)
    out_grad = jnp.dot(cot_cols.T, attended, preferred_element_type=jnp.float32)
    return jnp.concatenate([proj_grad, out_grad], axis=1)


def generic_device(
    layer_inputs,
    loss_adjoint_matrix,
    attention_projection_matrix,
    merge_projection_transposed,
    packed_sequence_labels,
    dropout_factors,
    straggler_filter,
):
    duplicate_workers = lax.axis_size("rep")
    member = lax.axis_index("rep")
    kept_worker = jnp.sum(jnp.arange(duplicate_workers, dtype=jnp.int32) * straggler_filter[:, 0])
    row_count = layer_inputs.shape[1] // duplicate_workers
    first_row = member * row_count
    qkv_full, out_full = (
        lax.all_gather(attention_projection_matrix, ("rep", "grp"), axis=0, tiled=True),
        lax.all_gather(merge_projection_transposed, ("rep", "grp"), axis=0, tiled=True),
    )
    projected_wide = jnp.dot(layer_inputs, qkv_full, preferred_element_type=jnp.float32)
    attn_wide = jnp.dot(loss_adjoint_matrix, out_full, preferred_element_type=jnp.float32)
    chosen_noise = from_root(dropout_factors[0], "rep", kept_worker)
    stacked, attended = token_grads(
        projected_wide, attn_wide, packed_sequence_labels[0], chosen_noise
    )
    gradient = weight_rows(
        layer_inputs, loss_adjoint_matrix, stacked, attended, first_row, row_count
    )
    return lax.psum_scatter(gradient, "grp", scatter_dimension=0, tiled=True)


def dot(a, b, dims):
    return lax.dot_general(a, b, (dims, ((), ())), preferred_element_type=jnp.float32)


VMEM = pl.BlockSpec(memory_space=pltpu.VMEM)
SMEM = pl.BlockSpec(memory_space=pltpu.SMEM)


def room(mebibytes):
    return pltpu.CompilerParams(vmem_limit_bytes=mebibytes << 20)


def cost(flops, count):
    return pl.CostEstimate(flops=flops, bytes_accessed=count, transcendentals=0)


def flip_kernel(order, me_ref, x_ref, keep_ref, send_ref, flipped):
    half = keep_ref.shape[0]
    blocks = len(order)
    rows = 2 * half // blocks
    width = x_ref.shape[1]
    for first in range(0, width, 256):
        flipped[pl.ds(first, 256), :] = x_ref[:, pl.ds(first, 256)].T
    for block in range(blocks):
        first = pl.multiple_of((me_ref[0] ^ order[block]) * rows, 16)
        target = keep_ref if block < blocks // 2 else send_ref
        place = (block % (blocks // 2)) * rows
        target[pl.ds(place, rows), :] = flipped[pl.ds(first, rows), :]


def flip(order, me, x):
    tokens, width = x.shape
    out = jax.ShapeDtypeStruct((width // 2, tokens), x.dtype)
    return pl.pallas_call(
        functools.partial(flip_kernel, order),
        out_shape=(out, out),
        in_specs=[SMEM, VMEM],
        out_specs=(VMEM, VMEM),
        scratch_shapes=[pltpu.VMEM((width, tokens), x.dtype)],
        cost_estimate=cost(0, 4 * x.size),
        compiler_params=room(10),
        name="flip",
    )(me.reshape(1), x)


def stack_kernel(pieces, *refs):
    sources, targets, sems = refs[:pieces], refs[pieces:-1], refs[-1]
    carried, targets = targets[: len(targets) // 2], targets[len(targets) // 2 :]
    copies = []
    first = 0
    for source in sources:
        rows = source.shape[0]
        copies.append((source, targets[0].at[pl.ds(first, rows), :]))
        first += rows
    copies += zip(carried, targets[1:])
    copies = [pltpu.make_async_copy(*ends, sems.at[n]) for n, ends in enumerate(copies)]
    for copy in copies:
        copy.start()
    for copy in copies:
        copy.wait()


def stack(pieces, carried=()):
    shape = (sum(p.shape[0] for p in pieces), pieces[0].shape[1])
    out = [jax.ShapeDtypeStruct(shape, pieces[0].dtype)]
    out += [jax.ShapeDtypeStruct(a.shape, a.dtype) for a in carried]
    moved = len(pieces) + len(carried)
    return pl.pallas_call(
        functools.partial(stack_kernel, len(pieces)),
        out_shape=out,
        in_specs=[pl.BlockSpec(memory_space=pl.ANY)] * moved,
        out_specs=[VMEM] * len(out),
        scratch_shapes=[pltpu.SemaphoreType.DMA((moved,))],
        cost_estimate=cost(0, 4 * sum(a.size for a in out)),
        compiler_params=room(6),
        name="stack",
    )(*pieces, *carried)


def pick_kernel(groups, member_ref, source_ref, mine_ref, theirs_ref):
    def put(target, m):
        place = 0
        for first, count in groups:
            target[:, pl.ds(place, count)] = source_ref[:, pl.ds(first + m * count, count)]
            place += count

    @pl.when(member_ref[0] == 0)
    def _():
        put(theirs_ref, 1)
        put(mine_ref, 0)

    @pl.when(member_ref[0] != 0)
    def _():
        put(theirs_ref, 0)
        put(mine_ref, 1)


def pick_columns(member, a, groups):
    out = jax.ShapeDtypeStruct((a.shape[0], sum(count for _, count in groups)), a.dtype)
    return pl.pallas_call(
        functools.partial(pick_kernel, groups),
        out_shape=(out, out),
        in_specs=[SMEM, VMEM],
        out_specs=(VMEM, VMEM),
        cost_estimate=cost(0, 4 * a.size),
        compiler_params=room(2),
        name="pick",
    )(member, a)


def one_on_other(a, b):
    zero = jnp.zeros((), a.dtype)
    above = lax.pad(a, zero, ((0, b.shape[0], 0), (0, 0, 0)))
    return above + lax.pad(b, zero, ((a.shape[0], 0, 0), (0, 0, 0)))


def forward_kernel(
    heads, member_ref, own_ref, other_ref, pair_ref, row_ref, noise_ref,
    att_ref, probs_ref, parts_ref,
):
    tokens = own_ref.shape[0]
    size = pair_ref.shape[1]
    scale = 1.0 / math.sqrt(size)
    low = jnp.bfloat16

    def part(first):
        return (own_ref[:, pl.ds(first, size)] + other_ref[:, pl.ds(first, size)]).astype(low)

    first_member = member_ref[0] == 0
    mine = part(heads * size).astype(jnp.float32)
    pair = pair_ref[...].astype(jnp.float32)
    keys = jnp.where(first_member, mine, pair).astype(low)
    vals = jnp.where(first_member, pair, mine).astype(low)
    parts_ref[heads] = keys
    parts_ref[heads + 1] = vals
    query_at = lax.broadcasted_iota(jnp.int32, (tokens, tokens), 0)
    key_at = lax.broadcasted_iota(jnp.int32, (tokens, tokens), 1)
    labels = jnp.broadcast_to(row_ref[...].astype(jnp.float32), (tokens, tokens))
    allowed = (labels.T == labels) & (key_at <= query_at)
    for head in range(heads):
        query = part(head * size)
        parts_ref[head] = query
        scores = dot(query, keys, ((1,), (1,))) * scale
        scores = jnp.where(allowed, scores, -jnp.inf)
        expon = jnp.exp(scores - jnp.max(scores, axis=1, keepdims=True))
        probs = expon / jnp.sum(expon, axis=1, keepdims=True)
        probs_ref[head] = probs
        dropped = (probs * (1.0 + noise_ref[head].astype(jnp.float32))).astype(low)
        att_ref[:, pl.ds(head * size, size)] = dot(dropped, vals, ((1,), (0,))).astype(low)


def forward(member, own, other, pair, labels, noise):
    tokens, size = pair.shape
    heads = noise.shape[0]
    return pl.pallas_call(
        functools.partial(forward_kernel, heads),
        out_shape=(
            jax.ShapeDtypeStruct((tokens, heads * size), jnp.bfloat16),
            jax.ShapeDtypeStruct(noise.shape, jnp.float32),
            jax.ShapeDtypeStruct((heads + 2, tokens, size), jnp.bfloat16),
        ),
        in_specs=[SMEM] + [VMEM] * 5,
        out_specs=(VMEM,) * 3,
        cost_estimate=cost(4 * noise.size * size, 8 * own.size + 6 * noise.size),
        compiler_params=room(10),
        name="forward",
    )(member, own, other, pair, labels, noise)


def backward_kernel(
    heads, member_ref, own_ref, other_ref, probs_ref, parts_ref, noise_ref, query_ref, keep_ref, send_ref
):
    tokens, size = keep_ref.shape
    scale = 1.0 / math.sqrt(size)
    low = jnp.bfloat16
    first_member = member_ref[0] == 0
    keys, vals = parts_ref[heads], parts_ref[heads + 1]
    key_grad = jnp.zeros((tokens, size), jnp.float32)
    val_grad = jnp.zeros((tokens, size), jnp.float32)
    for head in range(heads):
        here = pl.ds(head * size, size)
        query, grad = parts_ref[head], (own_ref[:, here] + other_ref[:, here]).astype(low)
        probs = probs_ref[head]
        factor = 1.0 + noise_ref[head].astype(jnp.float32)
        dropped = (probs * factor).astype(low)
        val_grad += dot(dropped, grad, ((0,), (0,)))
        prob_grad = dot(grad, vals, ((1,), (1,))) * factor
        inner = jnp.sum(probs * prob_grad, axis=1, keepdims=True)
        score_grad = (probs * (prob_grad - inner) * scale).astype(low)
        query_ref[:, here] = dot(score_grad, keys, ((1,), (0,))).astype(low)
        key_grad += dot(score_grad, query, ((0,), (0,)))
    keep_ref[...] = jnp.where(first_member, key_grad, val_grad)
    send_ref[...] = jnp.where(first_member, val_grad, key_grad)


def backward(member, own, other, probs, parts, noise):
    heads, tokens, _ = noise.shape
    size = parts.shape[2]
    narrow = jax.ShapeDtypeStruct((tokens, size), jnp.float32)
    return pl.pallas_call(
        functools.partial(backward_kernel, heads),
        out_shape=(jax.ShapeDtypeStruct((tokens, heads * size), jnp.bfloat16), narrow, narrow),
        in_specs=[SMEM] + [VMEM] * 5,
        out_specs=(VMEM,) * 3,
        cost_estimate=cost(8 * noise.size * size, 6 * noise.size),
        compiler_params=room(10),
        name="backward",
    )(member, own, other, probs, parts, noise)


def gather_kernel(runs, *refs):
    sources, out_ref = refs[:-1], refs[-1]
    place = 0
    for source, (first, rows) in zip(sources, runs):
        out_ref[pl.ds(place, rows), :] = source[pl.ds(first, rows), :].astype(out_ref.dtype)
        place += rows


def gather_rows(*runs):
    arrays = [array for array, _, _ in runs]
    shape = (sum(rows for _, _, rows in runs), arrays[0].shape[1])
    return pl.pallas_call(
        functools.partial(gather_kernel, [(first, rows) for _, first, rows in runs]),
        out_shape=jax.ShapeDtypeStruct(shape, jnp.bfloat16),
        in_specs=[VMEM] * len(arrays),
        out_specs=VMEM,
        cost_estimate=cost(0, 4 * shape[0] * shape[1]),
        compiler_params=room(4),
        name="gather",
    )(*arrays)


def place_kernel(terms, member_ref, *refs):
    sources, out_ref = list(refs[:-1]), refs[-1]
    rows = out_ref.shape[0]
    columns = [[(sources.pop(0), first) for first in firsts] for firsts in terms]

    def put(order):
        place = 0
        for pair in range(0, len(columns), 2):
            for n in order:
                values = sum(
                    source[pl.ds(first, rows), :].astype(out_ref.dtype)
                    for source, first in columns[pair + n]
                )
                out_ref[:, pl.ds(place, values.shape[1])] = values
                place += values.shape[1]

    @pl.when(member_ref[0] == 0)
    def _():
        put((0, 1))

    @pl.when(member_ref[0] != 0)
    def _():
        put((1, 0))


def place_columns(member, rows, *pieces):
    terms = [[first for _, first in piece] for piece in pieces]
    arrays = [array for piece in pieces for array, _ in piece]
    shape = (rows, sum(piece[0][0].shape[1] for piece in pieces))
    return pl.pallas_call(
        functools.partial(place_kernel, terms),
        out_shape=jax.ShapeDtypeStruct(shape, jnp.float32),
        in_specs=[SMEM] + [VMEM] * len(arrays),
        out_specs=VMEM,
        cost_estimate=cost(0, 8 * shape[0] * shape[1]),
        compiler_params=room(4),
        name="place",
    )(member, *arrays)


def paired_device(
    layer_inputs,
    loss_adjoint_matrix,
    attention_projection_matrix,
    merge_projection_transposed,
    packed_sequence_labels,
    dropout_factors,
    straggler_filter,
):
    grp = lax.axis_size("grp")
    member = lax.axis_index("rep")
    me = member * grp + lax.axis_index("grp")
    first = member == 0
    core, side, near, far = 1, 2, 4, 8

    def across(a, bit):
        return lax.ppermute(a, "grp", [(g, g ^ bit) for g in range(grp)])

    def across_rep(a):
        return lax.ppermute(a, "rep", [(0, 1), (1, 0)])

    heads = dropout_factors.shape[2]
    share = heads // 2
    width = merge_projection_transposed.shape[1]
    size = width // heads
    part = share * size

    qkv, theirs = pick_columns(
        member.reshape(1), attention_projection_matrix, ((0, part), (width, size))
    )
    qkv = one_on_other(qkv, across_rep(theirs))

    def merge_columns(m):
        return lax.dynamic_slice_in_dim(merge_projection_transposed, m * part, part, 1)

    merge = one_on_other(merge_columns(member), across_rep(merge_columns(1 - member)))

    qkv_near, qkv_far = across(qkv, near), across(qkv, far)
    qkv_both = across(qkv_far, near)
    qkv_side = [
        across(qkv, side), across(qkv_far, side), across(qkv_near, side), across(qkv_both, side)
    ]
    merge_far = across(merge, far)
    merge_line = one_on_other(merge, merge_far)
    merge_near = across(merge_line, near)
    merge_pieces = [merge_line, merge_near, across(merge_line, side), across(merge_near, side)]

    def order(bits):
        found = [0]
        for bit in (core, *bits, grp):
            found = [at | b for at in found for b in (0, bit)]
        return found

    stages = ((near, side, far), (side, near, far))
    x_keep, x_send = flip(order(stages[0]), me, layer_inputs)
    y_keep, y_send = flip(order(stages[1]), me, loss_adjoint_matrix)
    x_other, y_other = across(x_send, core), across(y_send, core)

    def as_it_lies(a):
        return with_layout_constraint(a, Layout(major_to_minor=tuple(range(a.ndim))))

    noise = as_it_lies(across_rep(dropout_factors))

    def project(rows, weights):
        return dot(rows, weights, ((0,), (0,)))

    pieces = [qkv, qkv_far, *qkv_side[:2], qkv_near, qkv_both, qkv_side[2]]
    (early,) = stack(pieces)
    cut = early.shape[0]
    away = project(x_other[:cut], early)
    qkv_in = across(away + project(x_other[cut:], qkv_side[3]), core)
    own = project(x_keep[:cut], early)
    qkv_own = own + project(x_keep[cut:], qkv_side[3])
    merge_rows, y_other = stack(merge_pieces, (y_other,))
    merge_in = across(project(y_other, merge_rows), core)
    merge_own = project(y_keep, merge_rows)

    pair = (qkv_own[:, part:] + qkv_in[:, part:]).astype(jnp.bfloat16)
    pair, noise = lax.optimization_barrier((pair, noise))
    pair = across_rep(pair)
    kept = lax.dynamic_slice(straggler_filter, (member, 0), (1, 1)).reshape(()) == 1
    noise = jnp.where(kept, dropout_factors, noise)[0]
    noise = jnp.where(first, noise[:, :share], noise[:, share:])
    noise_used = jnp.transpose(noise, (1, 0, 2))
    member = member.reshape(1)
    att, probs, pieces = forward(member, qkv_own, qkv_in, pair, packed_sequence_labels, noise_used)
    query_grad, pair_keep, pair_send = backward(
        member, merge_own, merge_in, probs, pieces, noise_used
    )
    pair_grad = (pair_keep + across_rep(pair_send)).astype(jnp.bfloat16)

    def first_two_exchanged(rows):
        halves = rows.reshape(2, 2, rows.shape[0] // 4, rows.shape[1])
        return jnp.swapaxes(halves, 0, 1).reshape(rows.shape)

    def reduced(name, keep, other, bits, grad, theirs):
        cut = keep.shape[0] // 2

        def half(rows):
            return dot(keep[rows], grad, ((1,), (0,))), other[rows]

        leaves, rows = half(slice(cut, None))
        leaves = (leaves + dot(rows, theirs, ((1,), (0,)))).astype(jnp.bfloat16)
        total, rows = half(slice(None, cut))
        for n, bit in enumerate(bits):
            arrived = across(leaves, bit)
            if n == 0:
                total = total + dot(rows, theirs, ((1,), (0,)))
            total = total + arrived.astype(jnp.float32)
            whole = total
            if n < len(bits) - 1 or name != "q":
                cut = total.shape[0] // 2
                leaves, total = total[cut:].astype(jnp.bfloat16), total[:cut]
        return whole, leaves

    def swapped_last(name, keep, other, bits, grad, theirs):
        whole, leaves = reduced(name, keep, other, bits, grad, theirs)
        swapped = across_rep(leaves)
        return ((whole, 0),), ((swapped, 0),)

    def swapped_first(name, keep, other, bits, grad, theirs):
        whole, _ = reduced(name, keep, other, bits[:-1], grad, theirs)
        rows, count = whole.shape[0] // 4, whole.shape[1]
        leaves = whole.reshape(2, 2, rows, count)[:, 1].astype(jnp.bfloat16)
        leaves = leaves.reshape(2 * rows, count)
        partner = across_rep(leaves)
        leaves = gather_rows((whole, 2 * rows, rows), (partner, rows, rows))
        arrived = across(leaves, bits[-1])
        return ((whole, 0), (arrived, 0)), ((partner, 0), (arrived, rows))

    merge = swapped_last("m", y_keep, y_other, stages[1], att, across(att, core))
    query = swapped_first("q", x_keep, x_other, stages[0], query_grad, across(query_grad, core))
    x_keep, x_other = first_two_exchanged(x_keep), first_two_exchanged(x_other)
    pair = swapped_last("p", x_keep, x_other, (side, near, far), pair_grad, across(pair_grad, core))
    rows = attention_projection_matrix.shape[0]
    return place_columns(member, rows, *query, *pair, *merge)


def paired(mesh, shapes):
    rep, grp = mesh.shape["rep"], mesh.shape["grp"]
    depth, heads, tokens = shapes[0][1], shapes[5][2], shapes[5][3]
    size = shapes[3][1] // heads
    even = depth % (rep * grp * 16) == 0 and depth % 256 == 0
    return rep == 2 and grp == 16 and even and heads % 2 == 0 and size % 128 == 0 and tokens % 128 == 0


def solution(mesh):
    placed = (
        P("grp", None),
        P("grp", None),
        P(("rep", "grp"), None),
        P(("rep", "grp"), None),
        P("grp", None),
        P("rep", "grp", None, None),
        P(None, "grp"),
    )

    def on_devices(body):
        return jax.shard_map(
            body, mesh=mesh, in_specs=placed, out_specs=P(("rep", "grp"), None), check_vma=False
        )

    def step(*args):
        if not paired(mesh, [a.shape for a in args]):
            return on_devices(generic_device)(*args)
        return on_devices(paired_device)(*args)

    return step
```
